256 devices in a mesh: box: 64 (over z, x, y_hi), grp: 4 (over y_lo, core).
Axes of the slice: x: 4, y: 4 (y_hi: 2, y_lo: 2; y = y_hi * 2 + y_lo), z: 8, core: 2. Of those that a mesh axis runs over, the one named last changes fastest.
Arguments:
- old_fields: float32 [3, 4, 256, 32, 1024], P(None, 'grp', 'box'), may hold values from -6 to 6, as said below
- old_count: int32 [4, 64], P('grp'), may hold values from 0 to 4, as said below
- neighbours: int32 [4, 128, 6], P('grp', 'box'), may hold values from -1 to 127, as said below
- parents: int32 [4, 128, 3], P('grp', 'box'), may hold values from 0 to 7, as said below
- coarse_source: float32 [4, 128, 8, 16, 256], P('grp', 'box'), may hold values from -6 to 6
Outputs:
- smoothed: float32 [4, 128, 32, 1024], P('grp', 'box')
- residual: float32 [4, 128, 32, 1024], P('grp', 'box')
- coarse_rhs: float32 [4, 128, 8, 16, 256], P('grp', 'box')
The draws below stay inside these ranges and needn't reach their ends.
Inputs may be any that keep to these rules, and one draw needn't show every extreme that they name: `old_fields`: components 0, 1, 2 are the solution, the right side and the cell coefficient; the coefficient lies in [0.25, 4]. `old_count`: in each owner group the counts sum to 128, and the sum of the first j counts differs from j * 2 by at most 1 for every j; some device holds 4 boxes and some none. Neighbourhood is symmetric; the x- neighbour of a box lies in the previous run of 2 boxes along the curve, the x+ neighbour in the next run, the y and z neighbours in the box's own run. `parents`: the named coarse box belongs to the owner on the same curve position as the fine box; no two fine boxes name the same octant of the same coarse box.
All inputs are finite; a program needn't handle non-finite values.
Results may differ from the reference program's by a relative error of at most 0.0001.
Values sent between devices are 32-bit elements; how exact they have to be, the bound alone decides.
No kernel may reach another device: no remote copies, remote signals or barrier semaphores. Data moves between devices by JAX's collectives and lax.ppermute only.
A program may use at most 64 MiB of HBM per device.

```python
import math
import jax
import jax.numpy as jnp
from jax import lax

EDGE = 32
BOXES = 2
SLOTS = 4
COARSE_BOXES = 2
OWNERS = 4
CURVE = 64


def draw_old_fields(key, part):
    field_shape = (OWNERS, CURVE * SLOTS, EDGE, EDGE * EDGE)
    solution_key, source_key, weight_key = jax.random.split(key, 3)
    coefficient = jnp.exp(jax.random.uniform(weight_key, field_shape, jnp.float32, math.log(0.25), math.log(4.0)))
    solution = jnp.clip(jax.random.normal(solution_key, field_shape, jnp.float32), -6.0, 6.0)
    right_side = jnp.clip(jax.random.normal(source_key, field_shape, jnp.float32), -6.0, 6.0)
    return jnp.stack([solution, right_side, coefficient]).astype(jnp.float32)


def count_row(row_key):
    drift_key, low_key, high_key = jax.random.split(row_key, 3)
    spread = BOXES // 2
    drift = jax.random.randint(drift_key, (CURVE + 1,), -spread, spread + 1)
    low_place = jax.random.randint(low_key, (), 1, CURVE // 2)
    high_place = jax.random.randint(high_key, (), CURVE // 2 + 1, CURVE - 1)
    places = jnp.arange(CURVE + 1, dtype=jnp.int32)
    drift = jnp.where(places == low_place, -spread, drift)
    drift = jnp.where(places == low_place + 1, spread, drift)
    drift = jnp.where(places == high_place, spread, drift)
    drift = jnp.where(places == high_place + 1, -spread, drift)
    drift = jnp.where((places == 0) | (places == CURVE), 0, drift)
    return (BOXES + drift[1:] - drift[:-1]).astype(jnp.int32)


def draw_old_count(key, part):
    return jax.vmap(count_row)(jax.random.split(key, OWNERS)).astype(jnp.int32)


def neighbour_group(group_key):
    order_key, link_x_key, link_y_key, link_z_key = jax.random.split(group_key, 4)
    placing = jax.vmap(lambda one_key: jax.random.permutation(one_key, BOXES))(jax.random.split(order_key, CURVE)).astype(jnp.int32)
    slot_at = jnp.argsort(placing, axis=1, stable=True).astype(jnp.int32)
    curve_ids = jnp.arange(CURVE, dtype=jnp.int32)[:, None]
    place_ids = jnp.arange(BOXES, dtype=jnp.int32)[None, :]
    keep_x = (jax.random.randint(link_x_key, (CURVE, BOXES), 0, 4) > 0) & (curve_ids < CURVE - 1)
    keep_y = (jax.random.randint(link_y_key, (CURVE, BOXES), 0, 4) > 0) & (place_ids // 2 < BOXES // 2 - 1)
    keep_z = (jax.random.randint(link_z_key, (CURVE, BOXES), 0, 4) > 0) & (place_ids % 2 == 0)

    def lookup(row_step, place_step, linked):
        row_ids = jnp.clip(curve_ids + row_step, 0, CURVE - 1)
        place_new = jnp.clip(placing + place_step, 0, BOXES - 1)
        target = (curve_ids + row_step) * BOXES + slot_at[row_ids, place_new]
        return jnp.where(linked, target, -1)
    low_rows = jnp.clip(curve_ids - 1, 0, CURVE - 1)
    minus_x = lookup(-1, 0, (curve_ids > 0) & keep_x[low_rows, placing])
    plus_x = lookup(1, 0, keep_x[curve_ids, placing])
    minus_y = lookup(0, -2, (placing >= 2) & keep_y[curve_ids, jnp.clip(placing - 2, 0, BOXES - 1)])
    plus_y = lookup(0, 2, keep_y[curve_ids, placing])
    minus_z = lookup(0, -1, (placing % 2 == 1) & keep_z[curve_ids, jnp.clip(placing - 1, 0, BOXES - 1)])
    plus_z = lookup(0, 1, keep_z[curve_ids, placing])
    stacked = jnp.stack([minus_x, plus_x, minus_y, plus_y, minus_z, plus_z], axis=-1)
    return stacked.reshape(CURVE * BOXES, 6).astype(jnp.int32)


def draw_neighbours(key, part):
    return jax.vmap(neighbour_group)(jax.random.split(key, OWNERS)).astype(jnp.int32)


def parent_row(row_key):
    bias_key, score_key, order_key = jax.random.split(row_key, 3)
    triples = OWNERS * COARSE_BOXES * 8
    triple_ids = jnp.arange(triples, dtype=jnp.int32)
    bias = jax.random.randint(bias_key, (OWNERS,), 0, 4)
    owner_of = triple_ids // (COARSE_BOXES * 8)
    score = (jax.random.randint(score_key, (triples,), 0, 2 ** 14) + bias[owner_of] * 2 ** 13) * 1024 + triple_ids
    best_scores, best = lax.top_k(score, OWNERS * BOXES)
    chosen = best[jax.random.permutation(order_key, OWNERS * BOXES)]
    return jnp.stack([chosen // (COARSE_BOXES * 8), chosen // 8 % COARSE_BOXES, chosen % 8], axis=-1)


def draw_parents(key, part):
    rows_all = jax.vmap(parent_row)(jax.random.split(key, CURVE))
    rows_all = rows_all.reshape(CURVE, OWNERS, BOXES, 3).transpose(1, 0, 2, 3)
    return rows_all.reshape(OWNERS, CURVE * BOXES, 3).astype(jnp.int32)


def shard_levels(rng, dims, shards, least, top_value):
    loudness, own = 1.0, jax.random.fold_in(rng, 6)
    for position, shards_of in shards:
        steps = jnp.exp(jax.random.uniform(jax.random.fold_in(own, position), (shards_of,), jnp.float32, least / len(shards), top_value / len(shards)))
        loudness = loudness * jnp.repeat(steps, dims[position] // shards_of).reshape([-1 if axis == position else 1 for axis in range(len(dims))])
    return loudness


def gaussian(stream_key, extent, scale, limit, shards=(), kind=jnp.bfloat16):
    loudness = shard_levels(stream_key, extent, shards, -0.22, 0.18) if shards else 1.0
    values = jax.random.normal(stream_key, extent, jnp.float32) * scale * loudness
    return jnp.minimum(jnp.maximum(values, -limit), limit).astype(kind)


def setup_inputs(seed: int = 0) -> dict:
    seeds = jax.random.split(jax.random.key(seed), 6)
    return {
        "old_fields": draw_old_fields(jax.random.fold_in(seeds[5], 71), 0),
        "old_count": draw_old_count(jax.random.fold_in(seeds[5], 71), 0),
        "neighbours": draw_neighbours(jax.random.fold_in(seeds[5], 71), 0),
        "parents": draw_parents(jax.random.fold_in(seeds[5], 71), 0),
        "coarse_source": gaussian(seeds[4], (OWNERS, CURVE * COARSE_BOXES, 8, EDGE // 2, (EDGE // 2) * (EDGE // 2)), 1.0, 6.0, ((0, 4), (1, 64)), jnp.float32),
    }


MASS_TERM = 0.25


def cube_faces(box_cubes):
    return (box_cubes[:, 0], box_cubes[:, -1], box_cubes[:, :, 0], box_cubes[:, :, -1], box_cubes[:, :, :, 0], box_cubes[:, :, :, -1])


def ghost_faces(box_cubes, link_rows, keep_own):
    box_faces = cube_faces(box_cubes)
    results = []
    for face_id in range(6):
        across = box_faces[face_id ^ 1]
        target = link_rows[:, face_id]
        chosen = jnp.take(across, jnp.clip(target, 0, across.shape[0] - 1), axis=0)
        fallback = box_faces[face_id] if keep_own else jnp.zeros_like(chosen)
        results.append(jnp.where((target >= 0)[:, None, None], chosen, fallback))
    return results


def beside_cubes(box_cubes, ghosts):
    return (
        jnp.concatenate([ghosts[0][:, None], box_cubes[:, :-1]], axis=1),
        jnp.concatenate([box_cubes[:, 1:], ghosts[1][:, None]], axis=1),
        jnp.concatenate([ghosts[2][:, :, None], box_cubes[:, :, :-1]], axis=2),
        jnp.concatenate([box_cubes[:, :, 1:], ghosts[3][:, :, None]], axis=2),
        jnp.concatenate([ghosts[4][:, :, :, None], box_cubes[:, :, :, :-1]], axis=3),
        jnp.concatenate([box_cubes[:, :, :, 1:], ghosts[5][:, :, :, None]], axis=3),
    )


def weighted_sum(weights, nearby):
    running = weights[0] * nearby[0]
    for face_id in range(1, 6):
        running = running + weights[face_id] * nearby[face_id]
    return running


def reference(old_fields, old_count, neighbours, parents, coarse_source):
    box_edge = old_fields.shape[3]
    half_edge = box_edge // 2
    patch_boxes = CURVE * BOXES
    coarse_rhs = coarse_source
    smooth_list = []
    residual_list = []
    positions = jnp.arange(box_edge, dtype=jnp.int32)
    parity = (positions[:, None, None] + positions[None, :, None] + positions[None, None, :]) % 2
    for owner_index in range(OWNERS):
        counts = old_count[owner_index]
        run_ends = jnp.cumsum(counts)
        run_starts = run_ends - counts
        wanted = jnp.arange(patch_boxes, dtype=jnp.int32)
        source = jnp.sum((run_ends[None, :] <= wanted[:, None]).astype(jnp.int32), axis=1)
        old_rows = (source * SLOTS + wanted - jnp.take(run_starts, source)).astype(jnp.int32)
        moved_fields = jnp.take(old_fields[:, owner_index], old_rows, axis=1)
        moved_fields = moved_fields.reshape(3, patch_boxes, box_edge, box_edge, box_edge)
        solution = moved_fields[0]
        right_side = moved_fields[1]
        coefficient = moved_fields[2]
        link_rows = neighbours[owner_index]
        coef_near = beside_cubes(coefficient, ghost_faces(coefficient, link_rows, True))
        weights = [0.5 * (coefficient + nearby_coef) for nearby_coef in coef_near]
        diagonal = MASS_TERM + weights[0]
        for face_id in range(1, 6):
            diagonal = diagonal + weights[face_id]
        for sweep_step in range(4):
            nearby = beside_cubes(solution, ghost_faces(solution, link_rows, False))
            updated = (right_side + weighted_sum(weights, nearby)) / diagonal
            solution = jnp.where(parity == sweep_step % 2, updated, solution)
        nearby = beside_cubes(solution, ghost_faces(solution, link_rows, False))
        residual = right_side - (diagonal * solution - weighted_sum(weights, nearby))
        restricted = residual.reshape(patch_boxes, half_edge, 2, half_edge, 2, half_edge, 2).sum(axis=(2, 4, 6)) * 0.125
        restricted = restricted.reshape(patch_boxes, half_edge, half_edge * half_edge)
        owner_group = parents[owner_index, :, 0]
        coarse_box = (wanted // BOXES) * COARSE_BOXES + parents[owner_index, :, 1]
        coarse_rhs = coarse_rhs.at[owner_group, coarse_box, parents[owner_index, :, 2]].set(restricted)
        smooth_list.append(solution.reshape(patch_boxes, box_edge, box_edge * box_edge))
        residual_list.append(residual.reshape(patch_boxes, box_edge, box_edge * box_edge))
    return jnp.stack(smooth_list), jnp.stack(residual_list), coarse_rhs
```

```python
import jax
import jax.numpy as jnp
from jax import lax
from jax.experimental import pallas as pl
from jax.experimental.pallas import tpu as pltpu
from jax.sharding import PartitionSpec as P

MASS_TERM = 0.25
LANES = 128
SOL, RHS, COEF, ENDS = 0, 16, 48, 80
END_ROWS = 12
PAD, PAIR_PAD = 8, 4
OWN, PAIRS, FIRST = 32, 24, 8

VMEM = pl.BlockSpec(memory_space=pltpu.VMEM)
SMEM = pl.BlockSpec(memory_space=pltpu.SMEM)


def lane_ids(rows):
    return lax.broadcasted_iota(jnp.int32, (rows, LANES), 1)


def row_ids(rows):
    return lax.broadcasted_iota(jnp.int32, (rows, LANES), 0)


def odd_lanes(rows):
    lane = lane_ids(rows)
    return ((lane >> 5) + lane) & 1


def offsets(counts, position):
    count = counts.shape[1]
    start = jnp.int32(0)
    for j in range(count):
        start = start + jnp.where(j < position, counts[0, j], 0)
    here = start - 2 * position
    after = here + counts[0, position] - 2
    before = here - counts[0, jnp.maximum(position - 1, 0)] + 2
    beyond = after + counts[0, jnp.minimum(position + 1, count - 1)] - 2
    return before, here, after, beyond


def link_code(links, box, face, first_box):
    target = links[0, box, face]
    return jnp.where(target < 0, 0, jnp.where(target - first_box == box, 1, 2))


def end_pieces(fields, row, tile, upper):
    lanes = slice(tile * LANES, (tile + 1) * LANES)
    rows = slice(24, 32) if upper else slice(0, 8)
    sol = fields[0, 0, row, rows, lanes]
    rhs = fields[1, 0, row, rows, lanes]
    coef = fields[2, 0, row, rows, lanes]
    mixed = (row_ids(8) + odd_lanes(8)) & 1
    if upper:
        packed = jnp.where(mixed == 0, pltpu.roll(sol, 5, 0), pltpu.roll(sol, 2, 0))
        return packed[:3], rhs[4:], coef[3:]
    packed = jnp.where(mixed == 1, sol, pltpu.roll(sol, 5, 0))
    return packed[:3], rhs[:4], coef[:5]


def store_ends(out, tile, base, pieces):
    out[tile, base : base + 3, :] = pieces[0]
    out[tile, base + 3 : base + 7, :] = pieces[1]
    out[tile, base + 7 : base + 12, :] = pieces[2]


def load_ends(ref, tile, base):
    return (
        ref[tile, base : base + 3, :],
        ref[tile, base + 3 : base + 7, :],
        ref[tile, base + 7 : base + 12, :],
    )


def pack_kernel(counts, links, fields, near_a, near_b, far_a, far_b):
    position = lax.axis_index("box")
    _, here, after, _ = offsets(counts, position)
    tiles = fields.shape[4] // LANES
    first_box = 2 * position
    held = (jnp.maximum(-here, 0), 1 - here)
    move_up = jnp.minimum(2 - here, 3)

    def message(out, upper):
        row = move_up if upper else 0
        mixed = (row_ids(16) + odd_lanes(16)) & 1
        for tile in range(tiles):
            lanes = slice(tile * LANES, (tile + 1) * LANES)
            low = fields[0, 0, row, 0:16, lanes]
            high = pltpu.roll(fields[0, 0, row, 16:32, lanes], 15, 0)
            out[tile, SOL : SOL + 16, :] = jnp.where(mixed == 1, low, high)
            out[tile, RHS : RHS + 32, :] = fields[1, 0, row, :, lanes]
            out[tile, COEF : COEF + 32, :] = fields[2, 0, row, :, lanes]
            for box in range(2):
                packed, rhs, coef = end_pieces(fields, held[box], tile, upper)
                if tile == 0:
                    lane = lane_ids(3)
                    for face in range(2, 6):
                        code = link_code(links, box, face, first_box).astype(jnp.float32)
                        mine = (lane == 2 * (face - 2) + int(upper)) & (row_ids(3) == 2)
                        packed = jnp.where(mine, code, packed)
                store_ends(out, tile, ENDS + END_ROWS * box, (packed, rhs, coef))

    def far_message(out, upper):
        row = move_up if upper else 0
        for tile in range(tiles):
            store_ends(out, tile, 0, end_pieces(fields, row, tile, upper))

    even = position % 2 == 0
    lower = position % 4 < 2

    @pl.when(even)
    def _():
        message(near_a, True)
        message(near_b, False)

    @pl.when(jnp.logical_not(even))
    def _():
        message(near_a, False)
        message(near_b, True)

    @pl.when(lower)
    def _():
        far_message(far_a, True)
        far_message(far_b, False)

    @pl.when(jnp.logical_not(lower))
    def _():
        far_message(far_a, False)
        far_message(far_b, True)


def choose(flag, one, other):
    return tuple(jnp.where(flag, a, b) for a, b in zip(one, other, strict=True))


def smooth_kernel(
    counts,
    links,
    parents,
    fields,
    near_a,
    near_b,
    far_a,
    far_b,
    smoothed,
    residual,
    coarse,
    raw,
    value,
    coef,
    weight,
    source,
    diagonal,
    defect,
    code,
    stage,
):
    position = lax.axis_index("box")
    before, here, after, beyond = offsets(counts, position)
    tiles = fields.shape[4] // LANES
    first_box = 2 * position
    even = position % 2 == 0
    lower = position % 4 < 2

    def place_local(box, row):
        for tile in range(tiles):
            lanes = slice(tile * LANES, (tile + 1) * LANES)
            for field in range(3):
                raw[field, box, tile, PAD : PAD + OWN, :] = fields[field, 0, row, :, lanes]

    def place_moved(box, ref):
        for tile in range(tiles):
            packed = ref[tile, SOL : SOL + 16, :]
            raw[0, box, tile, PAD : PAD + 16, :] = packed
            raw[0, box, tile, PAD + 16 : PAD + 32, :] = pltpu.roll(packed, 1, 0)
            raw[1, box, tile, PAD : PAD + OWN, :] = ref[tile, RHS : RHS + 32, :]
            raw[2, box, tile, PAD : PAD + OWN, :] = ref[tile, COEF : COEF + 32, :]

    from_below = here == 1
    from_above = after == -1

    @pl.when(jnp.logical_not(from_below))
    def _():
        place_local(0, jnp.maximum(-here, 0))

    @pl.when(from_below & even)
    def _():
        place_moved(0, near_b)

    @pl.when(from_below & jnp.logical_not(even))
    def _():
        place_moved(0, near_a)

    @pl.when(jnp.logical_not(from_above))
    def _():
        place_local(1, 1 - here)

    @pl.when(from_above & even)
    def _():
        place_moved(1, near_a)

    @pl.when(from_above & jnp.logical_not(even))
    def _():
        place_moved(1, near_b)

    def crossing(face, run_first):
        ids = [links[0, box, face] for box in range(2)]
        linked = [one >= 0 for one in ids]
        swap = jnp.where(
            linked[0],
            ids[0] - run_first == 1,
            linked[1] & (ids[1] - run_first == 0),
        )
        return linked, swap

    low_linked, low_swap = crossing(0, first_box - 2)
    high_linked, high_swap = crossing(1, first_box + 2)
    zeros = jnp.zeros((8, LANES), jnp.float32)
    for tile in range(tiles):
        ends = [
            choose(even, load_ends(near_b, tile, ENDS + END_ROWS * i), load_ends(near_a, tile, ENDS + END_ROWS * i))
            for i in range(2)
        ]
        far = choose(lower, load_ends(far_b, tile, 0), load_ends(far_a, tile, 0))
        low = (
            choose(before == 1, far, ends[0]),
            choose(here == -1, end_pieces(fields, 0, tile, True), ends[1]),
        )
        ends = [
            choose(even, load_ends(near_a, tile, ENDS + END_ROWS * i), load_ends(near_b, tile, ENDS + END_ROWS * i))
            for i in range(2)
        ]
        far = choose(lower, load_ends(far_a, tile, 0), load_ends(far_b, tile, 0))
        high = (
            choose(after == 1, end_pieces(fields, jnp.minimum(2 - here, 3), tile, False), ends[0]),
            choose(beyond == -1, far, ends[1]),
        )
        for box in range(2):
            sol, rhs, cof = choose(low_swap, low[1 - box], low[box])
            for field in range(3):
                raw[field, box, tile, 0:8, :] = zeros
                raw[field, box, tile, PAD + OWN : PAD + OWN + 8, :] = zeros
            raw[0, box, tile, 3:6, :] = sol
            raw[0, box, tile, 6:8, :] = sol[:2]
            raw[1, box, tile, 4:8, :] = rhs
            raw[2, box, tile, 3:8, :] = cof
            sol, rhs, cof = choose(high_swap, high[1 - box], high[box])
            raw[0, box, tile, 40:43, :] = sol
            raw[0, box, tile, 43:45, :] = sol[:2]
            raw[1, box, tile, 40:44, :] = rhs
            raw[2, box, tile, 40:45, :] = cof

    pair = row_ids(PAIRS)
    for face in range(2, 6):
        slot = 2 * (face - 2)
        ends = []
        for i in range(2):
            at = ENDS + END_ROWS * i + 2
            below = jnp.where(even, near_b[0, at : at + 1, :], near_a[0, at : at + 1, :])[:, slot + 1 : slot + 2]
            above = jnp.where(even, near_a[0, at : at + 1, :], near_b[0, at : at + 1, :])[:, slot : slot + 1]
            ends.append([jnp.broadcast_to(one, (PAIRS, LANES)) for one in (below, above)])
        for box in range(2):
            below = jnp.where(low_swap, ends[1 - box][0], ends[box][0])
            above = jnp.where(high_swap, ends[1 - box][1], ends[box][1])
            own = link_code(links, box, face, first_box).astype(jnp.float32)
            code[box, face - 2] = jnp.where(
                pair < PAIR_PAD, below, jnp.where(pair < PAIR_PAD + 16, own, above)
            )

    odd = odd_lanes(PAIRS)
    for box in range(2):
        for tile in range(tiles):
            for field, out in ((0, value), (2, coef)):
                lo = raw[field, box, tile, pl.ds(0, PAIRS, 2), :]
                hi = raw[field, box, tile, pl.ds(1, PAIRS, 2), :]
                out[0, box, tile, FIRST : FIRST + PAIRS, :] = jnp.where(odd == 1, hi, lo)
                out[1, box, tile, FIRST : FIRST + PAIRS, :] = jnp.where(odd == 1, lo, hi)
            lo = raw[1, box, tile, pl.ds(0, PAIRS, 2), :]
            hi = raw[1, box, tile, pl.ds(1, PAIRS, 2), :]
            source[0, box, tile] = jnp.where(odd == 1, hi, lo)
            source[1, box, tile] = jnp.where(odd == 1, lo, hi)

    lane = lane_ids(PAIRS)
    depth = lane & 31
    mid = slice(FIRST, FIRST + PAIRS)

    def nearby(ref, colour, box, tile):
        other = 1 - colour
        here_ = ref[other, box, tile, mid, :]
        there = ref[other, 1 - box, tile, mid, :]
        across = jnp.where(
            odd == colour,
            ref[other, box, tile, FIRST - 1 : FIRST - 1 + PAIRS, :],
            ref[other, box, tile, FIRST + 1 : FIRST + 1 + PAIRS, :],
        )
        y_low = ref[other, box, (tile - 1) % tiles, mid, :]
        if tile == 0:
            y_low = jnp.where(code[box, 0] == 2, ref[other, 1 - box, tiles - 1, mid, :], y_low)
        y_high = ref[other, box, (tile + 1) % tiles, mid, :]
        if tile == tiles - 1:
            y_high = jnp.where(code[box, 1] == 2, ref[other, 1 - box, 0, mid, :], y_high)
        z_low = jnp.where(code[box, 2] == 2, there, here_)
        z_high = jnp.where(code[box, 3] == 2, there, here_)
        return (
            across,
            here_,
            pltpu.roll(jnp.where(lane >= 96, y_low, here_), 32, 1),
            pltpu.roll(jnp.where(lane < 32, y_high, here_), 96, 1),
            jnp.where(depth == 0, pltpu.roll(z_low, 97, 1), pltpu.roll(here_, 1, 1)),
            jnp.where(depth == 31, pltpu.roll(z_high, 31, 1), pltpu.roll(here_, 127, 1)),
        )

    def weigh(colour, carry):
        for box in range(2):
            cut_low = jnp.logical_not(low_linked[box])
            cut_high = jnp.logical_not(high_linked[box])
            low_rows = ((pair == PAIR_PAD) & cut_low) | ((pair == PAIR_PAD + 16) & cut_high)
            high_rows = ((pair == PAIR_PAD + 15) & cut_high) | ((pair == PAIR_PAD - 1) & cut_low)
            end = jnp.where(odd == colour, low_rows.astype(jnp.int32), high_rows.astype(jnp.int32)) == 1
            none = [code[box, k] == 0 for k in range(4)]
            for tile in range(tiles):
                own = coef[colour, box, tile, mid, :]
                near = nearby(coef, colour, box, tile)
                lost = (
                    end,
                    None,
                    (lane < 32) & none[0] if tile == 0 else None,
                    (lane >= 96) & none[1] if tile == tiles - 1 else None,
                    (depth == 0) & none[2],
                    (depth == 31) & none[3],
                )
                total = jnp.full((PAIRS, LANES), MASS_TERM, jnp.float32)
                kept = []
                for one, gone in zip(near, lost, strict=True):
                    if gone is None:
                        w = 0.5 * (own + one)
                        kept.append(w)
                    else:
                        w = 0.5 * (own + jnp.where(gone, own, one))
                        kept.append(jnp.where(gone, 0.0, w))
                    total = total + w
                inverse = 1.0 / total
                diagonal[colour, box, tile] = total
                source[colour, box, tile] = source[colour, box, tile] * inverse
                for d in range(6):
                    weight[colour, d, box, tile] = kept[d] * inverse
        return carry

    lax.fori_loop(0, 2, weigh, 0)

    def update(colour, box, tile):
        total = source[colour, box, tile]
        for d, one in enumerate(nearby(value, colour, box, tile)):
            total = total + weight[colour, d, box, tile] * one
        return total

    def sweep(step, carry):
        colour = step & 1
        for box in range(2):
            for tile in range(tiles):
                value[colour, box, tile, mid, :] = update(colour, box, tile)
        return carry

    lax.fori_loop(0, 4, sweep, 0)

    def remain(colour, carry):
        for box in range(2):
            for tile in range(tiles):
                defect[colour, box, tile] = diagonal[colour, box, tile] * (
                    update(colour, box, tile) - value[colour, box, tile, mid, :]
                )
        return carry

    lax.fori_loop(0, 2, remain, 0)

    own_pairs = slice(PAIR_PAD, PAIR_PAD + 16)
    own_rows = slice(FIRST + PAIR_PAD, FIRST + PAIR_PAD + 16)
    odd = odd_lanes(16)
    halves = tiles // 2
    gathered = []
    for half in range(2):
        for box in range(2):
            sums = []
            for tile in range(half * halves, (half + 1) * halves):
                lanes = slice(tile * LANES, (tile + 1) * LANES)
                for k, out, red, black in (
                    (0, smoothed, value[0, box, tile, own_rows, :], value[1, box, tile, own_rows, :]),
                    (1, residual, defect[0, box, tile, own_pairs, :], defect[1, box, tile, own_pairs, :]),
                ):
                    stage[k, box, tile, pl.ds(0, 16, 2), :] = jnp.where(odd == 1, black, red)
                    stage[k, box, tile, pl.ds(1, 16, 2), :] = jnp.where(odd == 1, red, black)
                    out[0, box, :, lanes] = stage[k, box, tile]
                sums.append(red + black)
            gathered.append(jnp.concatenate(sums, axis=1))
    whole = jnp.concatenate(gathered, axis=0)
    first = whole.astype(jnp.bfloat16)
    rest = whole - first.astype(jnp.float32)
    second = rest.astype(jnp.bfloat16)
    third = (rest - second.astype(jnp.float32)).astype(jnp.bfloat16)
    width = halves * LANES
    cell = lax.broadcasted_iota(jnp.int32, (width, LANES), 0)
    block = lax.broadcasted_iota(jnp.int32, (width, LANES), 1)
    merge = jnp.where((cell >> 6) * 16 + ((cell & 31) >> 1) == block, 1.0, 0.0).astype(jnp.bfloat16)
    split = jnp.dot(
        jnp.concatenate([first, second, third], axis=0), merge, preferred_element_type=jnp.float32
    )
    mean = (split[:64] + split[64:128] + split[128:]) * 0.125
    for half in range(2):
        coarse[0:32, half * LANES : (half + 1) * LANES] = mean[32 * half : 32 * half + 32]
    for box in range(2):
        label = parents[0, box, 0] * 16 + parents[0, box, 1] * 8 + parents[0, box, 2]
        coarse[32 + 8 * box : 40 + 8 * box, :] = jnp.full((8, 2 * LANES), label.astype(jnp.float32))


def place_kernel(got, source, out):
    group = lax.axis_index("grp")
    base = (group * 16).astype(jnp.float32)
    for octant in range(16):
        kept = source[0, octant // 8, octant % 8]
        for sender in range(got.shape[0]):
            for box in range(2):
                label = got[sender, 32 + 8 * box : 40 + 8 * box, :]
                mine = jnp.concatenate([label, label], axis=0) == base + float(octant)
                kept = jnp.where(mine, got[sender, 16 * box : 16 * box + 16, :], kept)
        out[0, octant // 8, octant % 8] = kept


def per_device(old_fields, old_count, neighbours, parents, coarse_source):
    f32 = jnp.float32
    curve = lax.axis_size("box")
    box_edge, plane_cells = old_fields.shape[3:]
    tiles = plane_cells // LANES
    near = jax.ShapeDtypeStruct((tiles, ENDS + 2 * END_ROWS, LANES), f32)
    far = jax.ShapeDtypeStruct((tiles, END_ROWS, LANES), f32)
    params = pltpu.CompilerParams(vmem_limit_bytes=40 << 20)
    messages = pl.pallas_call(
        pack_kernel,
        out_shape=(near, near, far, far),
        in_specs=[SMEM, SMEM, VMEM],
        out_specs=(VMEM,) * 4,
        compiler_params=params,
        cost_estimate=pl.CostEstimate(flops=10**6, bytes_accessed=3 << 20, transcendentals=0),
        name="pack",
    )(old_count, neighbours, old_fields)

    def pairs(distance, shift):
        ids = [i for i in range(curve) if (i - shift) % (2 * distance) < distance and 0 <= i and i + distance < curve]
        return [(i, i + distance) for i in ids] + [(i + distance, i) for i in ids]

    moved = [
        lax.ppermute(message, "box", pairs(distance, shift))
        for message, distance, shift in zip(messages, (1, 1, 2, 2), (0, 1, 0, 2), strict=True)
    ]
    boxes = neighbours.shape[1]
    fine = jax.ShapeDtypeStruct((1, boxes, box_edge, plane_cells), f32)
    packed = (2, boxes, tiles, PAIRS, LANES)
    smoothed, residual, coarse = pl.pallas_call(
        smooth_kernel,
        out_shape=(fine, fine, jax.ShapeDtypeStruct((48, 2 * LANES), f32)),
        in_specs=[SMEM, SMEM, SMEM] + [VMEM] * 5,
        out_specs=(VMEM,) * 3,
        scratch_shapes=[
            pltpu.VMEM((3, boxes, tiles, OWN + 2 * PAD, LANES), f32),
            pltpu.VMEM((2, boxes, tiles, PAIRS + 2 * FIRST, LANES), f32),
            pltpu.VMEM((2, boxes, tiles, PAIRS + 2 * FIRST, LANES), f32),
            pltpu.VMEM((2, 6, boxes, tiles, PAIRS, LANES), f32),
            pltpu.VMEM(packed, f32),
            pltpu.VMEM(packed, f32),
            pltpu.VMEM(packed, f32),
            pltpu.VMEM((boxes, 4, PAIRS, LANES), f32),
            pltpu.VMEM((2, boxes, tiles, OWN, LANES), f32),
        ],
        compiler_params=params,
        cost_estimate=pl.CostEstimate(flops=10**7, bytes_accessed=6 << 20, transcendentals=0),
        name="smooth",
    )(old_count, neighbours, parents, old_fields, *moved)
    got = lax.all_gather(coarse, "grp")
    coarse_rhs = pl.pallas_call(
        place_kernel,
        out_shape=jax.ShapeDtypeStruct(coarse_source.shape, f32),
        in_specs=[VMEM, VMEM],
        out_specs=VMEM,
        compiler_params=params,
        name="place",
    )(got, coarse_source)
    return smoothed, residual, coarse_rhs


def solution(mesh):
    in_specs = (
        P(None, "grp", "box", None, None),
        P("grp", None),
        P("grp", "box", None),
        P("grp", "box", None),
        P("grp", "box", None, None, None),
    )
    out_specs = (
        P("grp", "box", None, None),
        P("grp", "box", None, None),
        P("grp", "box", None, None, None),
    )
    return jax.shard_map(
        per_device, mesh=mesh, in_specs=in_specs, out_specs=out_specs, check_vma=False
    )
```

```python
import jax
import jax.numpy as jnp
from jax import lax
from jax.experimental import pallas as pl
from jax.experimental.pallas import tpu as pltpu
from jax.sharding import PartitionSpec as P

MASS_TERM = 0.25
LANES = 128
SOL, RHS, COEF, ENDS = 0, 16, 48, 80
END_ROWS = 12
PAD, PAIR_PAD = 8, 4
OWN, PAIRS, FIRST = 32, 24, 8

VMEM = pl.BlockSpec(memory_space=pltpu.VMEM)
SMEM = pl.BlockSpec(memory_space=pltpu.SMEM)
HBM = pl.BlockSpec(memory_space=pltpu.HBM)


def lane_ids(rows):
    return lax.broadcasted_iota(jnp.int32, (rows, LANES), 1)


def row_ids(rows):
    return lax.broadcasted_iota(jnp.int32, (rows, LANES), 0)


def odd_lanes(rows):
    lane = lane_ids(rows)
    return ((lane >> 5) + lane) & 1


def offsets(counts, position):
    count = counts.shape[1]
    start = jnp.int32(0)
    for j in range(count):
        start = start + jnp.where(j < position, counts[0, j], 0)
    here = start - 2 * position
    after = here + counts[0, position] - 2
    before = here - counts[0, jnp.maximum(position - 1, 0)] + 2
    beyond = after + counts[0, jnp.minimum(position + 1, count - 1)] - 2
    return before, here, after, beyond


def link_code(links, box, face, first_box):
    target = links[0, box, face]
    return jnp.where(target < 0, 0, jnp.where(target - first_box == box, 1, 2))


def end_pieces(fields, row, tile, upper):
    lanes = slice(tile * LANES, (tile + 1) * LANES)
    rows = slice(24, 32) if upper else slice(0, 8)
    sol = fields[0, 0, row, rows, lanes]
    rhs = fields[1, 0, row, rows, lanes]
    coef = fields[2, 0, row, rows, lanes]
    mixed = (row_ids(8) + odd_lanes(8)) & 1
    if upper:
        packed = jnp.where(mixed == 0, pltpu.roll(sol, 5, 0), pltpu.roll(sol, 2, 0))
        return packed[:3], rhs[4:], coef[3:]
    packed = jnp.where(mixed == 1, sol, pltpu.roll(sol, 5, 0))
    return packed[:3], rhs[:4], coef[:5]


def store_ends(out, tile, base, pieces):
    out[tile, base : base + 3, :] = pieces[0]
    out[tile, base + 3 : base + 7, :] = pieces[1]
    out[tile, base + 7 : base + 12, :] = pieces[2]


def load_ends(ref, tile, base):
    return (
        ref[tile, base : base + 3, :],
        ref[tile, base + 3 : base + 7, :],
        ref[tile, base + 7 : base + 12, :],
    )


def pack_kernel(counts_hbm, links_hbm, fields_hbm, near_a, near_b, far_a, far_b, counts, links, fields, sems):
    copies = [
        pltpu.make_async_copy(counts_hbm, counts, sems.at[0]),
        pltpu.make_async_copy(links_hbm, links, sems.at[1]),
    ]
    for field in range(3):
        for row in range(fields.shape[2]):
            copies.append(
                pltpu.make_async_copy(
                    fields_hbm.at[field, 0, row], fields.at[field, 0, row], sems.at[len(copies)]
                )
            )
    for copy in copies:
        copy.start()
    for copy in copies:
        copy.wait()
    position = lax.axis_index("box")
    _, here, after, _ = offsets(counts, position)
    tiles = fields.shape[4] // LANES
    first_box = 2 * position
    held = (jnp.maximum(-here, 0), 1 - here)
    move_up = jnp.minimum(2 - here, 3)

    def message(out, upper):
        row = move_up if upper else 0
        mixed = (row_ids(16) + odd_lanes(16)) & 1
        for tile in range(tiles):
            lanes = slice(tile * LANES, (tile + 1) * LANES)
            low = fields[0, 0, row, 0:16, lanes]
            high = pltpu.roll(fields[0, 0, row, 16:32, lanes], 15, 0)
            out[tile, SOL : SOL + 16, :] = jnp.where(mixed == 1, low, high)
            out[tile, RHS : RHS + 32, :] = fields[1, 0, row, :, lanes]
            out[tile, COEF : COEF + 32, :] = fields[2, 0, row, :, lanes]
            for box in range(2):
                packed, rhs, coef = end_pieces(fields, held[box], tile, upper)
                if tile == 0:
                    lane = lane_ids(3)
                    for face in range(2, 6):
                        code = link_code(links, box, face, first_box).astype(jnp.float32)
                        mine = (lane == 2 * (face - 2) + int(upper)) & (row_ids(3) == 2)
                        packed = jnp.where(mine, code, packed)
                store_ends(out, tile, ENDS + END_ROWS * box, (packed, rhs, coef))

    def far_message(out, upper):
        row = move_up if upper else 0
        for tile in range(tiles):
            store_ends(out, tile, 0, end_pieces(fields, row, tile, upper))

    even = position % 2 == 0
    lower = position % 4 < 2

    @pl.when(even)
    def _():
        message(near_a, True)
        message(near_b, False)

    @pl.when(jnp.logical_not(even))
    def _():
        message(near_a, False)
        message(near_b, True)

    @pl.when(lower)
    def _():
        far_message(far_a, True)
        far_message(far_b, False)

    @pl.when(jnp.logical_not(lower))
    def _():
        far_message(far_a, False)
        far_message(far_b, True)


def choose(flag, one, other):
    return tuple(jnp.where(flag, a, b) for a, b in zip(one, other, strict=True))


def smooth_kernel(
    counts,
    links,
    parents,
    fields,
    near_a,
    near_b,
    far_a,
    far_b,
    red_out,
    black_out,
    red_left,
    black_left,
    coarse,
    raw,
    red,
    black,
    red_coef,
    black_coef,
    weight,
    source,
    diagonal,
    code,
):
    value, coef = (red, black), (red_coef, black_coef)
    position = lax.axis_index("box")
    before, here, after, beyond = offsets(counts, position)
    tiles = fields.shape[4] // LANES
    first_box = 2 * position
    even = position % 2 == 0
    lower = position % 4 < 2

    def place_local(box, row):
        for tile in range(tiles):
            lanes = slice(tile * LANES, (tile + 1) * LANES)
            for field in range(3):
                raw[field, box, tile, PAD : PAD + OWN, :] = fields[field, 0, row, :, lanes]

    def place_moved(box, ref):
        for tile in range(tiles):
            packed = ref[tile, SOL : SOL + 16, :]
            raw[0, box, tile, PAD : PAD + 16, :] = packed
            raw[0, box, tile, PAD + 16 : PAD + 32, :] = pltpu.roll(packed, 1, 0)
            raw[1, box, tile, PAD : PAD + OWN, :] = ref[tile, RHS : RHS + 32, :]
            raw[2, box, tile, PAD : PAD + OWN, :] = ref[tile, COEF : COEF + 32, :]

    from_below = here == 1
    from_above = after == -1

    @pl.when(jnp.logical_not(from_below))
    def _():
        place_local(0, jnp.maximum(-here, 0))

    @pl.when(from_below & even)
    def _():
        place_moved(0, near_b)

    @pl.when(from_below & jnp.logical_not(even))
    def _():
        place_moved(0, near_a)

    @pl.when(jnp.logical_not(from_above))
    def _():
        place_local(1, 1 - here)

    @pl.when(from_above & even)
    def _():
        place_moved(1, near_a)

    @pl.when(from_above & jnp.logical_not(even))
    def _():
        place_moved(1, near_b)

    def crossing(face, run_first):
        ids = [links[0, box, face] for box in range(2)]
        linked = [one >= 0 for one in ids]
        swap = jnp.where(
            linked[0],
            ids[0] - run_first == 1,
            linked[1] & (ids[1] - run_first == 0),
        )
        return linked, swap

    low_linked, low_swap = crossing(0, first_box - 2)
    high_linked, high_swap = crossing(1, first_box + 2)
    zeros = jnp.zeros((8, LANES), jnp.float32)
    for tile in range(tiles):
        ends = [
            choose(even, load_ends(near_b, tile, ENDS + END_ROWS * i), load_ends(near_a, tile, ENDS + END_ROWS * i))
            for i in range(2)
        ]
        far = choose(lower, load_ends(far_b, tile, 0), load_ends(far_a, tile, 0))
        low = (
            choose(before == 1, far, ends[0]),
            choose(here == -1, end_pieces(fields, 0, tile, True), ends[1]),
        )
        ends = [
            choose(even, load_ends(near_a, tile, ENDS + END_ROWS * i), load_ends(near_b, tile, ENDS + END_ROWS * i))
            for i in range(2)
        ]
        far = choose(lower, load_ends(far_a, tile, 0), load_ends(far_b, tile, 0))
        high = (
            choose(after == 1, end_pieces(fields, jnp.minimum(2 - here, 3), tile, False), ends[0]),
            choose(beyond == -1, far, ends[1]),
        )
        for box in range(2):
            sol, rhs, cof = choose(low_swap, low[1 - box], low[box])
            for field in range(3):
                raw[field, box, tile, 0:8, :] = zeros
                raw[field, box, tile, PAD + OWN : PAD + OWN + 8, :] = zeros
            raw[0, box, tile, 3:6, :] = sol
            raw[0, box, tile, 6:8, :] = sol[:2]
            raw[1, box, tile, 4:8, :] = rhs
            raw[2, box, tile, 3:8, :] = cof
            sol, rhs, cof = choose(high_swap, high[1 - box], high[box])
            raw[0, box, tile, 40:43, :] = sol
            raw[0, box, tile, 43:45, :] = sol[:2]
            raw[1, box, tile, 40:44, :] = rhs
            raw[2, box, tile, 40:45, :] = cof

    pair = row_ids(PAIRS)
    for face in range(2, 6):
        slot = 2 * (face - 2)
        ends = []
        for i in range(2):
            at = ENDS + END_ROWS * i + 2
            below = jnp.where(even, near_b[0, at : at + 1, :], near_a[0, at : at + 1, :])[:, slot + 1 : slot + 2]
            above = jnp.where(even, near_a[0, at : at + 1, :], near_b[0, at : at + 1, :])[:, slot : slot + 1]
            ends.append([jnp.broadcast_to(one, (PAIRS, LANES)) for one in (below, above)])
        for box in range(2):
            below = jnp.where(low_swap, ends[1 - box][0], ends[box][0])
            above = jnp.where(high_swap, ends[1 - box][1], ends[box][1])
            own = link_code(links, box, face, first_box).astype(jnp.float32)
            code[box, face - 2] = jnp.where(
                pair < PAIR_PAD, below, jnp.where(pair < PAIR_PAD + 16, own, above)
            )

    odd = odd_lanes(PAIRS)
    for box in range(2):
        for tile in range(tiles):
            for field, out in ((0, value), (2, coef)):
                lo = raw[field, box, tile, pl.ds(0, PAIRS, 2), :]
                hi = raw[field, box, tile, pl.ds(1, PAIRS, 2), :]
                out[0][box, tile, FIRST : FIRST + PAIRS, :] = jnp.where(odd == 1, hi, lo)
                out[1][box, tile, FIRST : FIRST + PAIRS, :] = jnp.where(odd == 1, lo, hi)
            lo = raw[1, box, tile, pl.ds(0, PAIRS, 2), :]
            hi = raw[1, box, tile, pl.ds(1, PAIRS, 2), :]
            source[0, box, tile] = jnp.where(odd == 1, hi, lo)
            source[1, box, tile] = jnp.where(odd == 1, lo, hi)

    lane = lane_ids(PAIRS)
    depth = lane & 31
    mid = slice(FIRST, FIRST + PAIRS)

    def nearby(ref, colour, box, tile):
        ref = ref[1 - colour]
        here_ = ref[box, tile, mid, :]
        there = ref[1 - box, tile, mid, :]
        across = jnp.where(
            odd == colour,
            ref[box, tile, FIRST - 1 : FIRST - 1 + PAIRS, :],
            ref[box, tile, FIRST + 1 : FIRST + 1 + PAIRS, :],
        )
        y_low = ref[box, (tile - 1) % tiles, mid, :]
        if tile == 0:
            y_low = jnp.where(code[box, 0] == 2, ref[1 - box, tiles - 1, mid, :], y_low)
        y_high = ref[box, (tile + 1) % tiles, mid, :]
        if tile == tiles - 1:
            y_high = jnp.where(code[box, 1] == 2, ref[1 - box, 0, mid, :], y_high)
        z_low = jnp.where(code[box, 2] == 2, there, here_)
        z_high = jnp.where(code[box, 3] == 2, there, here_)
        return (
            across,
            here_,
            pltpu.roll(jnp.where(lane >= 96, y_low, here_), 32, 1),
            pltpu.roll(jnp.where(lane < 32, y_high, here_), 96, 1),
            jnp.where(depth == 0, pltpu.roll(z_low, 97, 1), pltpu.roll(here_, 1, 1)),
            jnp.where(depth == 31, pltpu.roll(z_high, 31, 1), pltpu.roll(here_, 127, 1)),
        )

    for colour in range(2):
        for box in range(2):
            cut_low = jnp.logical_not(low_linked[box])
            cut_high = jnp.logical_not(high_linked[box])
            low_rows = ((pair == PAIR_PAD) & cut_low) | ((pair == PAIR_PAD + 16) & cut_high)
            high_rows = ((pair == PAIR_PAD + 15) & cut_high) | ((pair == PAIR_PAD - 1) & cut_low)
            end = jnp.where(odd == colour, low_rows.astype(jnp.int32), high_rows.astype(jnp.int32)) == 1
            none = [code[box, k] == 0 for k in range(4)]
            for tile in range(tiles):
                own = coef[colour][box, tile, mid, :]
                near = nearby(coef, colour, box, tile)
                lost = (
                    end,
                    None,
                    (lane < 32) & none[0] if tile == 0 else None,
                    (lane >= 96) & none[1] if tile == tiles - 1 else None,
                    (depth == 0) & none[2],
                    (depth == 31) & none[3],
                )
                total = jnp.full((PAIRS, LANES), MASS_TERM, jnp.float32)
                kept = []
                for one, gone in zip(near, lost, strict=True):
                    if gone is None:
                        w = 0.5 * (own + one)
                        kept.append(w)
                    else:
                        w = 0.5 * (own + jnp.where(gone, own, one))
                        kept.append(jnp.where(gone, 0.0, w))
                    total = total + w
                inverse = 1.0 / total
                diagonal[colour, box, tile] = total
                source[colour, box, tile] = source[colour, box, tile] * inverse
                for d in range(6):
                    weight[colour, d, box, tile] = kept[d] * inverse

    def update(colour, box, tile):
        total = source[colour, box, tile]
        for d, one in enumerate(nearby(value, colour, box, tile)):
            total = total + weight[colour, d, box, tile] * one
        return total

    def sweep(step, carry):
        for colour in range(2):
            for box in range(2):
                for tile in range(tiles):
                    value[colour][box, tile, mid, :] = update(colour, box, tile)
        return carry

    lax.fori_loop(0, 2, sweep, 0)

    own_pairs = slice(PAIR_PAD, PAIR_PAD + 16)
    own_rows = slice(FIRST + PAIR_PAD, FIRST + PAIR_PAD + 16)
    halves = tiles // 2
    gathered = []
    for half in range(2):
        for box in range(2):
            sums = []
            for tile in range(half * halves, (half + 1) * halves):
                total = None
                for colour, out, left in ((0, red_out, red_left), (1, black_out, black_left)):
                    kept = value[colour][box, tile, own_rows, :]
                    out[box, tile] = kept
                    rest = diagonal[colour, box, tile, own_pairs, :] * (
                        update(colour, box, tile)[own_pairs] - kept
                    )
                    left[box, tile] = rest
                    total = rest if total is None else total + rest
                sums.append(total)
            gathered.append(jnp.concatenate(sums, axis=1))
    whole = jnp.concatenate(gathered, axis=0)
    first = whole.astype(jnp.bfloat16)
    rest = whole - first.astype(jnp.float32)
    second = rest.astype(jnp.bfloat16)
    third = (rest - second.astype(jnp.float32)).astype(jnp.bfloat16)
    width = halves * LANES
    cell = lax.broadcasted_iota(jnp.int32, (width, LANES), 0)
    block = lax.broadcasted_iota(jnp.int32, (width, LANES), 1)
    merge = jnp.where((cell >> 6) * 16 + ((cell & 31) >> 1) == block, 1.0, 0.0).astype(jnp.bfloat16)
    split = jnp.dot(
        jnp.concatenate([first, second, third], axis=0), merge, preferred_element_type=jnp.float32
    )
    mean = (split[:64] + split[64:128] + split[128:]) * 0.125
    for half in range(2):
        coarse[0:32, half * LANES : (half + 1) * LANES] = mean[32 * half : 32 * half + 32]
    for box in range(2):
        label = parents[0, box, 0] * 16 + parents[0, box, 1] * 8 + parents[0, box, 2]
        coarse[32 + 8 * box : 40 + 8 * box, :] = jnp.full((8, 2 * LANES), label.astype(jnp.float32))


def unpack_kernel(red, black, red_left, black_left, smoothed, residual, stage):
    boxes, tiles = red.shape[:2]
    odd = odd_lanes(red.shape[2])
    for k, one, two, out in ((0, red, black, smoothed), (1, red_left, black_left, residual)):
        for box in range(boxes):
            for tile in range(tiles):
                low, high = one[box, tile], two[box, tile]
                stage[k, box, tile, pl.ds(0, 16, 2), :] = jnp.where(odd == 1, high, low)
                stage[k, box, tile, pl.ds(1, 16, 2), :] = jnp.where(odd == 1, low, high)
                out[0, box, :, tile * LANES : (tile + 1) * LANES] = stage[k, box, tile]


def place_kernel(*refs):
    *got, source, out = refs
    group = lax.axis_index("grp")
    base = (group * 16).astype(jnp.float32)
    for octant in range(16):
        kept = source[0, octant // 8, octant % 8]
        for sender in got:
            for box in range(2):
                label = sender[32 + 8 * box : 40 + 8 * box, :]
                mine = jnp.concatenate([label, label], axis=0) == base + float(octant)
                kept = jnp.where(mine, sender[16 * box : 16 * box + 16, :], kept)
        out[0, octant // 8, octant % 8] = kept


def per_device(old_fields, old_count, neighbours, parents, coarse_source):
    f32 = jnp.float32
    curve = lax.axis_size("box")
    box_edge, plane_cells = old_fields.shape[3:]
    tiles = plane_cells // LANES
    near = jax.ShapeDtypeStruct((tiles, ENDS + 2 * END_ROWS, LANES), f32)
    far = jax.ShapeDtypeStruct((tiles, END_ROWS, LANES), f32)
    params = pltpu.CompilerParams(vmem_limit_bytes=40 << 20)
    messages = pl.pallas_call(
        pack_kernel,
        out_shape=(near, near, far, far),
        in_specs=[HBM] * 3,
        out_specs=(VMEM,) * 4,
        scratch_shapes=[
            pltpu.SMEM(old_count.shape, old_count.dtype),
            pltpu.SMEM(neighbours.shape, neighbours.dtype),
            pltpu.VMEM(old_fields.shape, f32),
            pltpu.SemaphoreType.DMA((2 + 3 * old_fields.shape[2],)),
        ],
        compiler_params=params,
        cost_estimate=pl.CostEstimate(flops=10**6, bytes_accessed=3 << 20, transcendentals=0),
        name="pack",
    )(*[pltpu.with_memory_space_constraint(x, pltpu.HBM) for x in (old_count, neighbours, old_fields)])

    def pairs(distance, shift):
        ids = [i for i in range(curve) if (i - shift) % (2 * distance) < distance and 0 <= i and i + distance < curve]
        return [(i, i + distance) for i in ids] + [(i + distance, i) for i in ids]

    moved = [
        lax.ppermute(message, "box", pairs(distance, shift))
        for message, distance, shift in zip(messages, (1, 1, 2, 2), (0, 1, 0, 2), strict=True)
    ]
    boxes = neighbours.shape[1]
    fine = jax.ShapeDtypeStruct((1, boxes, box_edge, plane_cells), f32)
    packed = (2, boxes, tiles, PAIRS, LANES)
    column = (boxes, tiles, PAIRS + 2 * FIRST, LANES)
    half = jax.ShapeDtypeStruct((boxes, tiles, box_edge // 2, LANES), f32)
    *halves, coarse = pl.pallas_call(
        smooth_kernel,
        out_shape=(half, half, half, half, jax.ShapeDtypeStruct((48, 2 * LANES), f32)),
        in_specs=[SMEM, SMEM, SMEM] + [VMEM] * 5,
        out_specs=(VMEM,) * 5,
        scratch_shapes=[
            pltpu.VMEM((3, boxes, tiles, OWN + 2 * PAD, LANES), f32),
            pltpu.VMEM(column, f32),
            pltpu.VMEM(column, f32),
            pltpu.VMEM(column, f32),
            pltpu.VMEM(column, f32),
            pltpu.VMEM((2, 6, boxes, tiles, PAIRS, LANES), f32),
            pltpu.VMEM(packed, f32),
            pltpu.VMEM(packed, f32),
            pltpu.VMEM((boxes, 4, PAIRS, LANES), f32),
        ],
        compiler_params=params,
        cost_estimate=pl.CostEstimate(flops=10**7, bytes_accessed=6 << 20, transcendentals=0),
        name="smooth",
    )(old_count, neighbours, parents, old_fields, *moved)
    groups = lax.axis_size("grp")
    got = [coarse] + [
        lax.ppermute(coarse, "grp", [(i, (i + k) % groups) for i in range(groups)])
        for k in range(1, groups)
    ]
    smoothed, residual = pl.pallas_call(
        unpack_kernel,
        out_shape=(fine, fine),
        in_specs=[VMEM] * 4,
        out_specs=(VMEM,) * 2,
        scratch_shapes=[pltpu.VMEM((2, boxes, tiles, OWN, LANES), f32)],
        compiler_params=params,
        cost_estimate=pl.CostEstimate(flops=10**6, bytes_accessed=3 << 20, transcendentals=0),
        name="unpack",
    )(*halves)
    coarse_rhs = pl.pallas_call(
        place_kernel,
        out_shape=jax.ShapeDtypeStruct(coarse_source.shape, f32),
        in_specs=[VMEM] * (groups + 1),
        out_specs=VMEM,
        compiler_params=params,
        cost_estimate=pl.CostEstimate(flops=10**6, bytes_accessed=1 << 20, transcendentals=0),
        name="place",
    )(*got, coarse_source)
    return smoothed, residual, coarse_rhs


def solution(mesh):
    in_specs = (
        P(None, "grp", "box", None, None),
        P("grp", None),
        P("grp", "box", None),
        P("grp", "box", None),
        P("grp", "box", None, None, None),
    )
    out_specs = (
        P("grp", "box", None, None),
        P("grp", "box", None, None),
        P("grp", "box", None, None, None),
    )
    return jax.shard_map(
        per_device, mesh=mesh, in_specs=in_specs, out_specs=out_specs, check_vma=False
    )
```

```python
import jax
import jax.numpy as jnp
from jax import lax
from jax.experimental import pallas as pl
from jax.experimental.pallas import tpu as pltpu
from jax.sharding import PartitionSpec as P

MASS_TERM = 0.25
LANES = 128
PAD, PAIR_PAD = 8, 4
OWN, PAIRS, FIRST = 32, 24, 8
TILES = 8
SIDE_END, VALUE_END = 8, 2
SIDE = OWN * TILES
SIDE_ENDS = SIDE + OWN * TILES
LINKS = SIDE_ENDS + 2 * SIDE_END * TILES
FIRST_ROWS = LINKS + 8
VALUE_ENDS = OWN // 2 * TILES
REST_ROWS = VALUE_ENDS + 2 * VALUE_END * TILES
FAR_VALUES = SIDE_END * TILES
FAR_ROWS = FAR_VALUES + VALUE_END * TILES

VMEM = pl.BlockSpec(memory_space=pltpu.VMEM)
SMEM = pl.BlockSpec(memory_space=pltpu.SMEM)
HBM = pl.BlockSpec(memory_space=pltpu.HBM)


def lane_ids(rows):
    return lax.broadcasted_iota(jnp.int32, (rows, LANES), 1)


def row_ids(rows):
    return lax.broadcasted_iota(jnp.int32, (rows, LANES), 0)


def odd_lanes(rows):
    lane = lane_ids(rows)
    return ((lane >> 5) + lane) & 1


def offsets(counts, position):
    count = counts.shape[1]
    start = jnp.int32(0)
    for j in range(count):
        start = start + jnp.where(j < position, counts[0, j], 0)
    here = start - 2 * position
    after = here + counts[0, position] - 2
    before = here - counts[0, jnp.maximum(position - 1, 0)] + 2
    beyond = after + counts[0, jnp.minimum(position + 1, count - 1)] - 2
    return before, here, after, beyond


def link_code(links, box, face, first_box):
    target = links[0, box, face]
    return jnp.where(target < 0, 0, jnp.where(target - first_box == box, 1, 2))


def swap_depth(cells):
    odd = lane_ids(cells.shape[0]) & 1
    return jnp.where(odd == 1, pltpu.roll(cells, 1, 1), pltpu.roll(cells, LANES - 1, 1))


def end_tiles(fields, row, tile, upper):
    lanes = slice(tile * LANES, (tile + 1) * LANES)
    rows = slice(OWN - 8, OWN) if upper else slice(0, 8)
    return [fields[field, 0, row, rows, lanes] for field in range(3)]


def side_end(fields, row, tile, upper):
    sol, rhs, coef = end_tiles(fields, row, tile, upper)
    towards = 1 if upper else 7
    next_coef = pltpu.roll(coef, towards, 0)
    folded = rhs + 0.5 * (coef + next_coef) * pltpu.roll(sol, towards, 0)
    mixed = jnp.where(odd_lanes(8) == int(not upper), folded, swap_depth(next_coef))
    side = jnp.where(row_ids(8) == (4 if upper else 3), mixed, rhs)
    rows = slice(4, 8) if upper else slice(0, 4)
    return coef[rows], side[rows]


def value_end(fields, row, tile, upper):
    sol, _, _ = end_tiles(fields, row, tile, upper)
    packed = jnp.where(odd_lanes(8) == 1, sol, pltpu.roll(sol, 7, 0))
    return (packed[4:5], packed[6:7]) if upper else (packed[0:1], packed[2:3])


def store_rows(out, base, pieces):
    for piece in pieces:
        out[base : base + piece.shape[0], :] = piece
        base += piece.shape[0]


def load_rows(ref, base, sizes):
    pieces = []
    for size in sizes:
        pieces.append(ref[base : base + size, :])
        base += size
    return tuple(pieces)


SIDE_SIZES, VALUE_SIZES = (4, 4), (1, 1)


def slots(here):
    return (jnp.maximum(-here, 0), 1 - here), jnp.minimum(2 - here, 3)


def pack_first_kernel(counts_hbm, links_hbm, fields_hbm, near_a, near_b, shifts, counts, links, fields, sems):
    copies = []

    def fetch(source, target):
        copies.append(pltpu.make_async_copy(source, target, sems.at[len(copies)]))

    fetch(counts_hbm, counts)
    fetch(links_hbm, links)
    for row in range(fields.shape[2]):
        for field in (2, 1):
            fetch(fields_hbm.at[field, 0, row], fields.at[field, 0, row])
    for row in range(3):
        for rows in (pl.ds(0, 8), pl.ds(OWN - 8, 8)):
            fetch(fields_hbm.at[0, 0, row, rows], fields.at[0, 0, row, rows])
    for copy in copies:
        copy.start()
    for copy in copies:
        copy.wait()
    position = lax.axis_index("box")
    found = offsets(counts, position)
    for k in range(4):
        shifts[k] = found[k]
    here = found[1]
    held, move_up = slots(here)
    codes = jnp.zeros((8, LANES), jnp.float32)
    for box in range(2):
        for face in range(2, 6):
            mine = (row_ids(8) == box) & (lane_ids(8) == face - 2)
            codes = jnp.where(mine, link_code(links, box, face, 2 * position).astype(jnp.float32), codes)

    def message(out, upper):
        row = move_up if upper else 0
        for tile in range(TILES):
            lanes = slice(tile * LANES, (tile + 1) * LANES)
            out[OWN * tile : OWN * (tile + 1), :] = fields[2, 0, row, :, lanes]
            out[SIDE + OWN * tile : SIDE + OWN * (tile + 1), :] = fields[1, 0, row, :, lanes]
            for box in range(2):
                store_rows(
                    out, SIDE_ENDS + SIDE_END * (2 * tile + box), side_end(fields, held[box], tile, upper)
                )
        out[LINKS : LINKS + 8, :] = codes

    even = position % 2 == 0

    @pl.when(even)
    def _():
        message(near_a, True)
        message(near_b, False)

    @pl.when(jnp.logical_not(even))
    def _():
        message(near_a, False)
        message(near_b, True)


def pack_rest_kernel(shifts, fields, near_a, near_b, far_a, far_b):
    position = lax.axis_index("box")
    here = shifts[1]
    held, move_up = slots(here)

    def message(out, upper):
        row = move_up if upper else 0
        mixed = (row_ids(16) + odd_lanes(16)) & 1
        for tile in range(TILES):
            lanes = slice(tile * LANES, (tile + 1) * LANES)
            low = fields[0, 0, row, 0:16, lanes]
            high = pltpu.roll(fields[0, 0, row, 16:32, lanes], 15, 0)
            out[16 * tile : 16 * tile + 16, :] = jnp.where(mixed == 1, low, high)
            for box in range(2):
                store_rows(
                    out, VALUE_ENDS + VALUE_END * (2 * tile + box), value_end(fields, held[box], tile, upper)
                )

    def far_message(out, upper):
        row = move_up if upper else 0
        for tile in range(TILES):
            store_rows(out, SIDE_END * tile, side_end(fields, row, tile, upper))
            store_rows(out, FAR_VALUES + VALUE_END * tile, value_end(fields, row, tile, upper))

    even = position % 2 == 0
    lower = position % 4 < 2

    @pl.when(lower)
    def _():
        far_message(far_a, True)
        far_message(far_b, False)

    @pl.when(jnp.logical_not(lower))
    def _():
        far_message(far_a, False)
        far_message(far_b, True)

    @pl.when(even)
    def _():
        message(near_a, True)
        message(near_b, False)

    @pl.when(jnp.logical_not(even))
    def _():
        message(near_a, False)
        message(near_b, True)


def choose(flag, one, other):
    return tuple(jnp.where(flag, a, b) for a, b in zip(one, other, strict=True))


def crossing(links, face, run_first):
    ids = [links[0, box, face] for box in range(2)]
    linked = [one >= 0 for one in ids]
    swap = jnp.where(linked[0], ids[0] - run_first == 1, linked[1] & (ids[1] - run_first == 0))
    return linked, swap


def neighbour_ends(offset, even, lower, swaps, fields, near, far, tile, start, far_start, sizes, local):
    before, here, after, beyond = offset
    near_a, near_b = near
    far_a, far_b = far
    at = [start + sum(sizes) * (2 * tile + i) for i in range(2)]
    far_at = far_start + sum(sizes) * tile
    below = [choose(even, load_rows(near_b, at[i], sizes), load_rows(near_a, at[i], sizes)) for i in range(2)]
    above = [choose(even, load_rows(near_a, at[i], sizes), load_rows(near_b, at[i], sizes)) for i in range(2)]
    far_below = choose(lower, load_rows(far_b, far_at, sizes), load_rows(far_a, far_at, sizes))
    far_above = choose(lower, load_rows(far_a, far_at, sizes), load_rows(far_b, far_at, sizes))
    below = (choose(before == 1, far_below, below[0]), choose(here == -1, local(fields, 0, tile, True), below[1]))
    above = (
        choose(after == 1, local(fields, jnp.minimum(2 - here, 3), tile, False), above[0]),
        choose(beyond == -1, far_above, above[1]),
    )
    return [
        (choose(swaps[0], below[1 - box], below[box]), choose(swaps[1], above[1 - box], above[box]))
        for box in range(2)
    ]


def place_own(here, after, even, place_local, place_moved, near):
    from_below = here == 1
    from_above = after == -1
    held = slots(here)[0]
    for box, moved, first, second in ((0, from_below, near[1], near[0]), (1, from_above, near[0], near[1])):

        @pl.when(jnp.logical_not(moved))
        def _(box=box):
            place_local(box, held[box])

        @pl.when(moved & even)
        def _(box=box, ref=first):
            place_moved(box, ref)

        @pl.when(moved & jnp.logical_not(even))
        def _(box=box, ref=second):
            place_moved(box, ref)


def split_colours(raw, box, tile):
    odd = odd_lanes(PAIRS)
    low = raw[box, tile, pl.ds(0, PAIRS, 2), :]
    high = raw[box, tile, pl.ds(1, PAIRS, 2), :]
    return jnp.where(odd == 1, high, low), jnp.where(odd == 1, low, high)


def nearby(ref, code, colour, box, tile):
    mid = slice(FIRST, FIRST + PAIRS)
    lane = lane_ids(PAIRS)
    depth = lane & 31
    ref = ref[1 - colour]
    here_ = ref[box, tile, mid, :]
    there = ref[1 - box, tile, mid, :]
    across = jnp.where(
        odd_lanes(PAIRS) == colour,
        ref[box, tile, FIRST - 1 : FIRST - 1 + PAIRS, :],
        ref[box, tile, FIRST + 1 : FIRST + 1 + PAIRS, :],
    )
    y_low = ref[box, (tile - 1) % TILES, mid, :]
    if tile == 0:
        y_low = jnp.where(code[box, 0] == 2, ref[1 - box, TILES - 1, mid, :], y_low)
    y_high = ref[box, (tile + 1) % TILES, mid, :]
    if tile == TILES - 1:
        y_high = jnp.where(code[box, 1] == 2, ref[1 - box, 0, mid, :], y_high)
    z_low = jnp.where(code[box, 2] == 2, there, here_)
    z_high = jnp.where(code[box, 3] == 2, there, here_)
    return (
        across,
        here_,
        pltpu.roll(jnp.where(lane >= 96, y_low, here_), 32, 1),
        pltpu.roll(jnp.where(lane < 32, y_high, here_), 96, 1),
        jnp.where(depth == 0, pltpu.roll(z_low, 97, 1), pltpu.roll(here_, 1, 1)),
        jnp.where(depth == 31, pltpu.roll(z_high, 31, 1), pltpu.roll(here_, 127, 1)),
    )


def weigh_kernel(
    shifts,
    links,
    fields,
    near_a,
    near_b,
    far_a,
    far_b,
    weight,
    source,
    diagonal,
    code,
    raw,
    raw_side,
    red_coef,
    black_coef,
):
    coef = (red_coef, black_coef)
    position = lax.axis_index("box")
    offset = [shifts[k] for k in range(4)]
    _, here, after, _ = offset
    first_box = 2 * position
    even = position % 2 == 0
    lower = position % 4 < 2

    def place_local(box, row):
        for tile in range(TILES):
            lanes = slice(tile * LANES, (tile + 1) * LANES)
            raw[box, tile, PAD : PAD + OWN, :] = fields[2, 0, row, :, lanes]
            raw_side[box, tile, PAD : PAD + OWN, :] = fields[1, 0, row, :, lanes]

    def place_moved(box, ref):
        for tile in range(TILES):
            raw[box, tile, PAD : PAD + OWN, :] = ref[OWN * tile : OWN * (tile + 1), :]
            raw_side[box, tile, PAD : PAD + OWN, :] = ref[SIDE + OWN * tile : SIDE + OWN * (tile + 1), :]

    place_own(here, after, even, place_local, place_moved, (near_a, near_b))
    low_linked, low_swap = crossing(links, 0, first_box - 2)
    high_linked, high_swap = crossing(links, 1, first_box + 2)
    ones = jnp.ones((8, LANES), jnp.float32)
    odd = odd_lanes(1)
    for tile in range(TILES):
        ends = neighbour_ends(
            offset, even, lower, (low_swap, high_swap), fields, (near_a, near_b), (far_a, far_b), tile,
            SIDE_ENDS, 0, SIDE_SIZES, side_end,
        )
        for box in range(2):
            (below, side_below), (above, side_above) = ends[box]
            for one in (raw, raw_side):
                one[box, tile, 0:8, :] = ones
                one[box, tile, PAD + OWN : PAD + OWN + 8, :] = ones
            raw[box, tile, 3:4, :] = jnp.where(odd == 0, swap_depth(side_below[0:1]), below[0:1])
            raw[box, tile, 4:8, :] = below
            raw_side[box, tile, 4:8, :] = side_below
            raw[box, tile, 40:44, :] = above
            raw[box, tile, 44:45, :] = jnp.where(odd == 1, swap_depth(side_above[3:4]), above[3:4])
            raw_side[box, tile, 40:44, :] = side_above

    pair = row_ids(PAIRS)
    tile_a, tile_b = near_a[LINKS : LINKS + 8, :], near_b[LINKS : LINKS + 8, :]
    codes_below, codes_above = jnp.where(even, tile_b, tile_a), jnp.where(even, tile_a, tile_b)
    for face in range(4):
        spread = [
            [jnp.broadcast_to(one[i : i + 1, face : face + 1], (PAIRS, LANES)) for i in range(2)]
            for one in (codes_below, codes_above)
        ]
        for box in range(2):
            below = jnp.where(low_swap, spread[0][1 - box], spread[0][box])
            above = jnp.where(high_swap, spread[1][1 - box], spread[1][box])
            own = link_code(links, box, face + 2, first_box).astype(jnp.float32)
            code[box, face] = jnp.where(
                pair < PAIR_PAD, below, jnp.where(pair < PAIR_PAD + 16, own, above)
            )

    odd = odd_lanes(PAIRS)
    lane = lane_ids(PAIRS)
    depth = lane & 31
    mid = slice(FIRST, FIRST + PAIRS)
    for box in range(2):
        for tile in range(TILES):
            red_coef[box, tile, mid, :], black_coef[box, tile, mid, :] = split_colours(raw, box, tile)
            source[0, box, tile], source[1, box, tile] = split_colours(raw_side, box, tile)

    for colour in range(2):
        for box in range(2):
            cut_low = jnp.logical_not(low_linked[box])
            cut_high = jnp.logical_not(high_linked[box])
            low_rows = ((pair == PAIR_PAD) & cut_low) | ((pair == PAIR_PAD + 16) & cut_high)
            high_rows = ((pair == PAIR_PAD + 15) & cut_high) | ((pair == PAIR_PAD - 1) & cut_low)
            end = jnp.where(odd == colour, low_rows.astype(jnp.int32), high_rows.astype(jnp.int32)) == 1
            none = [code[box, k] == 0 for k in range(4)]
            for tile in range(TILES):
                own = coef[colour][box, tile, mid, :]
                near = nearby(coef, code, colour, box, tile)
                lost = (
                    end,
                    None,
                    (lane < 32) & none[0] if tile == 0 else None,
                    (lane >= 96) & none[1] if tile == TILES - 1 else None,
                    (depth == 0) & none[2],
                    (depth == 31) & none[3],
                )
                total = jnp.full((PAIRS, LANES), MASS_TERM, jnp.float32)
                kept = []
                for one, gone in zip(near, lost, strict=True):
                    if gone is None:
                        w = 0.5 * (own + one)
                        kept.append(w)
                    else:
                        w = 0.5 * (own + jnp.where(gone, own, one))
                        kept.append(jnp.where(gone, 0.0, w))
                    total = total + w
                inverse = 1.0 / total
                diagonal[colour, box, tile] = total
                source[colour, box, tile] = source[colour, box, tile] * inverse
                for d in range(6):
                    weight[colour, d, box, tile] = kept[d] * inverse


def smooth_kernel(
    shifts,
    links,
    parents,
    fields,
    near_a,
    near_b,
    far_a,
    far_b,
    weight,
    source,
    diagonal,
    code,
    red_out,
    black_out,
    red_left,
    black_left,
    coarse,
    raw,
    red,
    black,
):
    value = (red, black)
    position = lax.axis_index("box")
    offset = [shifts[k] for k in range(4)]
    _, here, after, _ = offset
    first_box = 2 * position
    even = position % 2 == 0
    lower = position % 4 < 2

    def place_local(box, row):
        for tile in range(TILES):
            raw[box, tile, PAD : PAD + OWN, :] = fields[0, 0, row, :, tile * LANES : (tile + 1) * LANES]

    def place_moved(box, ref):
        for tile in range(TILES):
            packed = ref[16 * tile : 16 * tile + 16, :]
            raw[box, tile, PAD : PAD + 16, :] = packed
            raw[box, tile, PAD + 16 : PAD + 32, :] = pltpu.roll(packed, 1, 0)

    place_own(here, after, even, place_local, place_moved, (near_a, near_b))
    swaps = (crossing(links, 0, first_box - 2)[1], crossing(links, 1, first_box + 2)[1])
    zeros = jnp.zeros((8, LANES), jnp.float32)
    for tile in range(TILES):
        ends = neighbour_ends(
            offset, even, lower, swaps, fields, (near_a, near_b), (far_a, far_b), tile,
            VALUE_ENDS, FAR_VALUES, VALUE_SIZES, value_end,
        )
        for box in range(2):
            raw[box, tile, 0:8, :] = zeros
            raw[box, tile, PAD + OWN : PAD + OWN + 8, :] = zeros
            for base, pieces in zip((4, PAD + OWN), ends[box], strict=True):
                for k in range(4):
                    raw[box, tile, base + k : base + k + 1, :] = pieces[k // 2]

    mid = slice(FIRST, FIRST + PAIRS)
    for box in range(2):
        for tile in range(TILES):
            red[box, tile, mid, :], black[box, tile, mid, :] = split_colours(raw, box, tile)

    def update(colour, box, tile):
        total = source[colour, box, tile]
        for d, one in enumerate(nearby(value, code, colour, box, tile)):
            total = total + weight[colour, d, box, tile] * one
        return total

    def sweep(step, carry):
        for colour in range(2):
            for box in range(2):
                for tile in range(TILES):
                    value[colour][box, tile, mid, :] = update(colour, box, tile)
        return carry

    lax.fori_loop(0, 2, sweep, 0)

    own_pairs = slice(PAIR_PAD, PAIR_PAD + 16)
    own_rows = slice(FIRST + PAIR_PAD, FIRST + PAIR_PAD + 16)
    halves = TILES // 2
    gathered = []
    for half in range(2):
        for box in range(2):
            sums = []
            for tile in range(half * halves, (half + 1) * halves):
                total = None
                for colour, out, left in ((0, red_out, red_left), (1, black_out, black_left)):
                    kept = value[colour][box, tile, own_rows, :]
                    out[box, tile] = kept
                    rest = diagonal[colour, box, tile, own_pairs, :] * (
                        update(colour, box, tile)[own_pairs] - kept
                    )
                    left[box, tile] = rest
                    total = rest if total is None else total + rest
                sums.append(total)
            gathered.append(jnp.concatenate(sums, axis=1))
    whole = jnp.concatenate(gathered, axis=0)
    first = whole.astype(jnp.bfloat16)
    rest = whole - first.astype(jnp.float32)
    second = rest.astype(jnp.bfloat16)
    third = (rest - second.astype(jnp.float32)).astype(jnp.bfloat16)
    width = halves * LANES
    cell = lax.broadcasted_iota(jnp.int32, (width, LANES), 0)
    block = lax.broadcasted_iota(jnp.int32, (width, LANES), 1)
    merge = jnp.where((cell >> 6) * 16 + ((cell & 31) >> 1) == block, 1.0, 0.0).astype(jnp.bfloat16)
    split = jnp.dot(
        jnp.concatenate([first, second, third], axis=0), merge, preferred_element_type=jnp.float32
    )
    mean = (split[:64] + split[64:128] + split[128:]) * 0.125
    for half in range(2):
        coarse[0:32, half * LANES : (half + 1) * LANES] = mean[32 * half : 32 * half + 32]
    for box in range(2):
        label = parents[0, box, 0] * 16 + parents[0, box, 1] * 8 + parents[0, box, 2]
        coarse[32 + 8 * box : 40 + 8 * box, :] = jnp.full((8, 2 * LANES), label.astype(jnp.float32))


def unpack_kernel(red, black, red_left, black_left, smoothed, residual, stage):
    boxes, tiles = red.shape[:2]
    odd = odd_lanes(red.shape[2])
    for k, one, two, out in ((0, red, black, smoothed), (1, red_left, black_left, residual)):
        for box in range(boxes):
            for tile in range(tiles):
                low, high = one[box, tile], two[box, tile]
                stage[k, box, tile, pl.ds(0, 16, 2), :] = jnp.where(odd == 1, high, low)
                stage[k, box, tile, pl.ds(1, 16, 2), :] = jnp.where(odd == 1, low, high)
                out[0, box, :, tile * LANES : (tile + 1) * LANES] = stage[k, box, tile]


def place_kernel(*refs):
    *got, source, out = refs
    group = lax.axis_index("grp")
    base = (group * 16).astype(jnp.float32)
    for octant in range(16):
        kept = source[0, octant // 8, octant % 8]
        for sender in got:
            for box in range(2):
                label = sender[32 + 8 * box : 40 + 8 * box, :]
                mine = jnp.concatenate([label, label], axis=0) == base + float(octant)
                kept = jnp.where(mine, sender[16 * box : 16 * box + 16, :], kept)
        out[0, octant // 8, octant % 8] = kept


def per_device(old_fields, old_count, neighbours, parents, coarse_source):
    f32 = jnp.float32
    curve = lax.axis_size("box")
    box_edge, plane_cells = old_fields.shape[3:]
    boxes = neighbours.shape[1]
    params = pltpu.CompilerParams(vmem_limit_bytes=40 << 20)

    def cost(flops, size):
        return pl.CostEstimate(flops=flops, bytes_accessed=size, transcendentals=0)

    def rows(count):
        return jax.ShapeDtypeStruct((count, LANES), f32)

    def swap(message, distance, shift):
        ids = [i for i in range(curve - distance) if (i - shift) % (2 * distance) < distance]
        both = [(i, i + distance) for i in ids] + [(i + distance, i) for i in ids]
        return lax.ppermute(message, "box", both)

    *first, shifts = pl.pallas_call(
        pack_first_kernel,
        out_shape=(rows(FIRST_ROWS),) * 2 + (jax.ShapeDtypeStruct((4,), jnp.int32),),
        in_specs=[HBM] * 3,
        out_specs=(VMEM, VMEM, SMEM),
        scratch_shapes=[
            pltpu.SMEM(old_count.shape, old_count.dtype),
            pltpu.SMEM(neighbours.shape, neighbours.dtype),
            pltpu.VMEM(old_fields.shape, f32),
            pltpu.SemaphoreType.DMA((2 + 2 * old_fields.shape[2] + 6,)),
        ],
        compiler_params=params,
        cost_estimate=cost(10**6, 2 << 20),
        name="pack_first",
    )(*[pltpu.with_memory_space_constraint(x, pltpu.HBM) for x in (old_count, neighbours, old_fields)])
    rest = pl.pallas_call(
        pack_rest_kernel,
        out_shape=(rows(REST_ROWS),) * 2 + (rows(FAR_ROWS),) * 2,
        in_specs=[SMEM, VMEM],
        out_specs=(VMEM,) * 4,
        compiler_params=params,
        cost_estimate=cost(10**6, 2 << 20),
        name="pack_rest",
    )(shifts, old_fields)
    first = [swap(message, 1, shift) for shift, message in enumerate(first)]
    far = [swap(rest[2], 2, 0), swap(rest[3], 2, 2)]
    rest = [swap(message, 1, shift) for shift, message in enumerate(rest[:2])]
    packed = (2, boxes, TILES, PAIRS, LANES)
    column = pltpu.VMEM((boxes, TILES, PAIRS + 2 * FIRST, LANES), f32)
    raw = pltpu.VMEM((boxes, TILES, OWN + 2 * PAD, LANES), f32)
    weights = pl.pallas_call(
        weigh_kernel,
        out_shape=[
            jax.ShapeDtypeStruct(shape, f32)
            for shape in ((2, 6, boxes, TILES, PAIRS, LANES), packed, packed, (boxes, 4, PAIRS, LANES))
        ],
        in_specs=[SMEM, SMEM] + [VMEM] * 5,
        out_specs=[VMEM] * 4,
        scratch_shapes=[raw, raw, column, column],
        compiler_params=params,
        cost_estimate=cost(10**7, 4 << 20),
        name="weigh",
    )(shifts, neighbours, old_fields, *first, *far)
    fine = jax.ShapeDtypeStruct((1, boxes, box_edge, plane_cells), f32)
    half = jax.ShapeDtypeStruct((boxes, TILES, box_edge // 2, LANES), f32)
    *halves, coarse = pl.pallas_call(
        smooth_kernel,
        out_shape=(half, half, half, half, jax.ShapeDtypeStruct((48, 2 * LANES), f32)),
        in_specs=[SMEM, SMEM, SMEM] + [VMEM] * 9,
        out_specs=(VMEM,) * 5,
        scratch_shapes=[raw, column, column],
        compiler_params=params,
        cost_estimate=cost(10**7, 6 << 20),
        name="smooth",
    )(shifts, neighbours, parents, old_fields, *rest, *far, *weights)
    groups = lax.axis_size("grp")
    got = [coarse] + [
        lax.ppermute(coarse, "grp", [(i, i ^ k) for i in range(groups)]) for k in range(1, groups)
    ]
    smoothed, residual = pl.pallas_call(
        unpack_kernel,
        out_shape=(fine, fine),
        in_specs=[VMEM] * 4,
        out_specs=(VMEM,) * 2,
        scratch_shapes=[pltpu.VMEM((2, boxes, TILES, OWN, LANES), f32)],
        compiler_params=params,
        cost_estimate=pl.CostEstimate(flops=10**6, bytes_accessed=3 << 20, transcendentals=0),
        name="unpack",
    )(*halves)
    coarse_rhs = pl.pallas_call(
        place_kernel,
        out_shape=jax.ShapeDtypeStruct(coarse_source.shape, f32),
        in_specs=[VMEM] * (groups + 1),
        out_specs=VMEM,
        compiler_params=params,
        cost_estimate=pl.CostEstimate(flops=10**6, bytes_accessed=1 << 20, transcendentals=0),
        name="place",
    )(*got, coarse_source)
    return smoothed, residual, coarse_rhs


def solution(mesh):
    in_specs = (
        P(None, "grp", "box", None, None),
        P("grp", None),
        P("grp", "box", None),
        P("grp", "box", None),
        P("grp", "box", None, None, None),
    )
    out_specs = (
        P("grp", "box", None, None),
        P("grp", "box", None, None),
        P("grp", "box", None, None, None),
    )
    return jax.shard_map(
        per_device, mesh=mesh, in_specs=in_specs, out_specs=out_specs, check_vma=False
    )
```

```python
import jax
import jax.numpy as jnp
from jax import lax
from jax.experimental import pallas as pl
from jax.experimental.pallas import tpu as pltpu
from jax.sharding import PartitionSpec as P

MASS_TERM = 0.25
LANES = 128
PAD, PAIR_PAD = 8, 4
OWN, PAIRS, FIRST = 32, 24, 8
TILES = 8
SIDE_END, VALUE_END = 8, 2
SIDE = OWN * TILES
SIDE_ENDS = SIDE + OWN * TILES
LINKS = SIDE_ENDS + 2 * SIDE_END * TILES
VALUE = LINKS + 8
VALUE_ENDS = VALUE + OWN // 2 * TILES
NEAR_ROWS = VALUE_ENDS + 2 * VALUE_END * TILES
FAR_VALUES = SIDE_END * TILES
FAR_ROWS = FAR_VALUES + VALUE_END * TILES

VMEM = pl.BlockSpec(memory_space=pltpu.VMEM)
SMEM = pl.BlockSpec(memory_space=pltpu.SMEM)
HBM = pl.BlockSpec(memory_space=pltpu.HBM)


def lane_ids(rows):
    return lax.broadcasted_iota(jnp.int32, (rows, LANES), 1)


def row_ids(rows):
    return lax.broadcasted_iota(jnp.int32, (rows, LANES), 0)


def odd_lanes(rows):
    lane = lane_ids(rows)
    return ((lane >> 5) + lane) & 1


def offsets(counts, position):
    count = counts.shape[1]
    start = jnp.int32(0)
    for j in range(count):
        start = start + jnp.where(j < position, counts[0, j], 0)
    here = start - 2 * position
    after = here + counts[0, position] - 2
    before = here - counts[0, jnp.maximum(position - 1, 0)] + 2
    beyond = after + counts[0, jnp.minimum(position + 1, count - 1)] - 2
    return before, here, after, beyond


def link_code(links, box, face, first_box):
    target = links[0, box, face]
    return jnp.where(target < 0, 0, jnp.where(target - first_box == box, 1, 2))


def swap_depth(cells):
    odd = lane_ids(cells.shape[0]) & 1
    return jnp.where(odd == 1, pltpu.roll(cells, 1, 1), pltpu.roll(cells, LANES - 1, 1))


def end_tiles(fields, row, tile, upper):
    lanes = slice(tile * LANES, (tile + 1) * LANES)
    rows = slice(OWN - 8, OWN) if upper else slice(0, 8)
    return [fields[field, 0, row, rows, lanes] for field in range(3)]


def side_end(fields, row, tile, upper):
    sol, rhs, coef = end_tiles(fields, row, tile, upper)
    towards = 1 if upper else 7
    next_coef = pltpu.roll(coef, towards, 0)
    folded = rhs + 0.5 * (coef + next_coef) * pltpu.roll(sol, towards, 0)
    mixed = jnp.where(odd_lanes(8) == int(not upper), folded, swap_depth(next_coef))
    side = jnp.where(row_ids(8) == (4 if upper else 3), mixed, rhs)
    rows = slice(4, 8) if upper else slice(0, 4)
    return coef[rows], side[rows]


def value_end(fields, row, tile, upper):
    sol, _, _ = end_tiles(fields, row, tile, upper)
    packed = jnp.where(odd_lanes(8) == 1, sol, pltpu.roll(sol, 7, 0))
    return (packed[4:5], packed[6:7]) if upper else (packed[0:1], packed[2:3])


def store_rows(out, base, pieces):
    for piece in pieces:
        out[base : base + piece.shape[0], :] = piece
        base += piece.shape[0]


def load_rows(ref, base, sizes):
    pieces = []
    for size in sizes:
        pieces.append(ref[base : base + size, :])
        base += size
    return tuple(pieces)


SIDE_SIZES, VALUE_SIZES = (4, 4), (1, 1)


def slots(here):
    return (jnp.maximum(-here, 0), 1 - here), jnp.minimum(2 - here, 3)


def pack_kernel(counts_hbm, links_hbm, fields_hbm, near_a, near_b, shifts, counts, links, fields, sems):
    copies = []

    def fetch(source, target):
        copies.append(pltpu.make_async_copy(source, target, sems.at[len(copies)]))

    fetch(counts_hbm, counts)
    fetch(links_hbm, links)
    for row in range(fields.shape[2]):
        for field in range(3):
            fetch(fields_hbm.at[field, 0, row], fields.at[field, 0, row])
    for copy in copies:
        copy.start()
    for copy in copies:
        copy.wait()
    position = lax.axis_index("box")
    found = offsets(counts, position)
    for k in range(4):
        shifts[k] = found[k]
    here = found[1]
    held, move_up = slots(here)
    codes = jnp.zeros((8, LANES), jnp.float32)
    for box in range(2):
        for face in range(2, 6):
            mine = (row_ids(8) == box) & (lane_ids(8) == face - 2)
            codes = jnp.where(mine, link_code(links, box, face, 2 * position).astype(jnp.float32), codes)

    mixed = (row_ids(16) + odd_lanes(16)) & 1

    def message(out, upper):
        row = move_up if upper else 0
        for tile in range(TILES):
            lanes = slice(tile * LANES, (tile + 1) * LANES)
            low = fields[0, 0, row, 0:16, lanes]
            high = pltpu.roll(fields[0, 0, row, 16:32, lanes], 15, 0)
            out[VALUE + 16 * tile : VALUE + 16 * tile + 16, :] = jnp.where(mixed == 1, low, high)
            out[OWN * tile : OWN * (tile + 1), :] = fields[2, 0, row, :, lanes]
            out[SIDE + OWN * tile : SIDE + OWN * (tile + 1), :] = fields[1, 0, row, :, lanes]
            for box in range(2):
                store_rows(
                    out, SIDE_ENDS + SIDE_END * (2 * tile + box), side_end(fields, held[box], tile, upper)
                )
                store_rows(
                    out, VALUE_ENDS + VALUE_END * (2 * tile + box), value_end(fields, held[box], tile, upper)
                )
        out[LINKS : LINKS + 8, :] = codes

    even = position % 2 == 0

    @pl.when(even)
    def _():
        message(near_a, True)
        message(near_b, False)

    @pl.when(jnp.logical_not(even))
    def _():
        message(near_a, False)
        message(near_b, True)


def pack_far_kernel(shifts, fields, far_a, far_b):
    position = lax.axis_index("box")
    move_up = slots(shifts[1])[1]

    def far_message(out, upper):
        row = move_up if upper else 0
        for tile in range(TILES):
            store_rows(out, SIDE_END * tile, side_end(fields, row, tile, upper))
            store_rows(out, FAR_VALUES + VALUE_END * tile, value_end(fields, row, tile, upper))

    lower = position % 4 < 2

    @pl.when(lower)
    def _():
        far_message(far_a, True)
        far_message(far_b, False)

    @pl.when(jnp.logical_not(lower))
    def _():
        far_message(far_a, False)
        far_message(far_b, True)


def choose(flag, one, other):
    return tuple(jnp.where(flag, a, b) for a, b in zip(one, other, strict=True))


def crossing(links, face, run_first):
    ids = [links[0, box, face] for box in range(2)]
    linked = [one >= 0 for one in ids]
    swap = jnp.where(linked[0], ids[0] - run_first == 1, linked[1] & (ids[1] - run_first == 0))
    return linked, swap


def neighbour_ends(offset, even, lower, swaps, fields, near, far, tile, start, far_start, sizes, local):
    before, here, after, beyond = offset
    near_a, near_b = near
    far_a, far_b = far
    at = [start + sum(sizes) * (2 * tile + i) for i in range(2)]
    far_at = far_start + sum(sizes) * tile
    below = [choose(even, load_rows(near_b, at[i], sizes), load_rows(near_a, at[i], sizes)) for i in range(2)]
    above = [choose(even, load_rows(near_a, at[i], sizes), load_rows(near_b, at[i], sizes)) for i in range(2)]
    far_below = choose(lower, load_rows(far_b, far_at, sizes), load_rows(far_a, far_at, sizes))
    far_above = choose(lower, load_rows(far_a, far_at, sizes), load_rows(far_b, far_at, sizes))
    below = (choose(before == 1, far_below, below[0]), choose(here == -1, local(fields, 0, tile, True), below[1]))
    above = (
        choose(after == 1, local(fields, jnp.minimum(2 - here, 3), tile, False), above[0]),
        choose(beyond == -1, far_above, above[1]),
    )
    return [
        (choose(swaps[0], below[1 - box], below[box]), choose(swaps[1], above[1 - box], above[box]))
        for box in range(2)
    ]


def place_own(here, after, even, place_local, place_moved, near):
    from_below = here == 1
    from_above = after == -1
    held = slots(here)[0]
    for box, moved, first, second in ((0, from_below, near[1], near[0]), (1, from_above, near[0], near[1])):

        @pl.when(jnp.logical_not(moved))
        def _(box=box):
            place_local(box, held[box])

        @pl.when(moved & even)
        def _(box=box, ref=first):
            place_moved(box, ref)

        @pl.when(moved & jnp.logical_not(even))
        def _(box=box, ref=second):
            place_moved(box, ref)


def split_colours(raw, box, tile):
    odd = odd_lanes(PAIRS)
    low = raw[box, tile, pl.ds(0, PAIRS, 2), :]
    high = raw[box, tile, pl.ds(1, PAIRS, 2), :]
    return jnp.where(odd == 1, high, low), jnp.where(odd == 1, low, high)


def nearby(ref, code, colour, box, tile):
    mid = slice(FIRST, FIRST + PAIRS)
    lane = lane_ids(PAIRS)
    depth = lane & 31
    ref = ref[1 - colour]
    here_ = ref[box, tile, mid, :]
    there = ref[1 - box, tile, mid, :]
    across = jnp.where(
        odd_lanes(PAIRS) == colour,
        ref[box, tile, FIRST - 1 : FIRST - 1 + PAIRS, :],
        ref[box, tile, FIRST + 1 : FIRST + 1 + PAIRS, :],
    )
    y_low = ref[box, (tile - 1) % TILES, mid, :]
    if tile == 0:
        y_low = jnp.where(code[box, 0] == 2, ref[1 - box, TILES - 1, mid, :], y_low)
    y_high = ref[box, (tile + 1) % TILES, mid, :]
    if tile == TILES - 1:
        y_high = jnp.where(code[box, 1] == 2, ref[1 - box, 0, mid, :], y_high)
    z_low = jnp.where(code[box, 2] == 2, there, here_)
    z_high = jnp.where(code[box, 3] == 2, there, here_)
    return (
        across,
        here_,
        pltpu.roll(jnp.where(lane >= 96, y_low, here_), 32, 1),
        pltpu.roll(jnp.where(lane < 32, y_high, here_), 96, 1),
        jnp.where(depth == 0, pltpu.roll(z_low, 97, 1), pltpu.roll(here_, 1, 1)),
        jnp.where(depth == 31, pltpu.roll(z_high, 31, 1), pltpu.roll(here_, 127, 1)),
    )


def make_weights(
    shifts, links, fields, near_a, near_b, far_a, far_b, weight, source, diagonal, code, raw, raw_side, coef
):
    red_coef, black_coef = coef
    position = lax.axis_index("box")
    offset = [shifts[k] for k in range(4)]
    _, here, after, _ = offset
    first_box = 2 * position
    even = position % 2 == 0
    lower = position % 4 < 2

    def place_local(box, row):
        for tile in range(TILES):
            lanes = slice(tile * LANES, (tile + 1) * LANES)
            raw[box, tile, PAD : PAD + OWN, :] = fields[2, 0, row, :, lanes]
            raw_side[box, tile, PAD : PAD + OWN, :] = fields[1, 0, row, :, lanes]

    def place_moved(box, ref):
        for tile in range(TILES):
            raw[box, tile, PAD : PAD + OWN, :] = ref[OWN * tile : OWN * (tile + 1), :]
            raw_side[box, tile, PAD : PAD + OWN, :] = ref[SIDE + OWN * tile : SIDE + OWN * (tile + 1), :]

    place_own(here, after, even, place_local, place_moved, (near_a, near_b))
    low_linked, low_swap = crossing(links, 0, first_box - 2)
    high_linked, high_swap = crossing(links, 1, first_box + 2)
    ones = jnp.ones((8, LANES), jnp.float32)
    odd = odd_lanes(1)
    for tile in range(TILES):
        ends = neighbour_ends(
            offset, even, lower, (low_swap, high_swap), fields, (near_a, near_b), (far_a, far_b), tile,
            SIDE_ENDS, 0, SIDE_SIZES, side_end,
        )
        for box in range(2):
            (below, side_below), (above, side_above) = ends[box]
            for one in (raw, raw_side):
                one[box, tile, 0:8, :] = ones
                one[box, tile, PAD + OWN : PAD + OWN + 8, :] = ones
            raw[box, tile, 3:4, :] = jnp.where(odd == 0, swap_depth(side_below[0:1]), below[0:1])
            raw[box, tile, 4:8, :] = below
            raw_side[box, tile, 4:8, :] = side_below
            raw[box, tile, 40:44, :] = above
            raw[box, tile, 44:45, :] = jnp.where(odd == 1, swap_depth(side_above[3:4]), above[3:4])
            raw_side[box, tile, 40:44, :] = side_above

    pair = row_ids(PAIRS)
    tile_a, tile_b = near_a[LINKS : LINKS + 8, :], near_b[LINKS : LINKS + 8, :]
    codes_below, codes_above = jnp.where(even, tile_b, tile_a), jnp.where(even, tile_a, tile_b)
    for face in range(4):
        spread = [
            [jnp.broadcast_to(one[i : i + 1, face : face + 1], (PAIRS, LANES)) for i in range(2)]
            for one in (codes_below, codes_above)
        ]
        for box in range(2):
            below = jnp.where(low_swap, spread[0][1 - box], spread[0][box])
            above = jnp.where(high_swap, spread[1][1 - box], spread[1][box])
            own = link_code(links, box, face + 2, first_box).astype(jnp.float32)
            code[box, face] = jnp.where(
                pair < PAIR_PAD, below, jnp.where(pair < PAIR_PAD + 16, own, above)
            )

    odd = odd_lanes(PAIRS)
    lane = lane_ids(PAIRS)
    depth = lane & 31
    mid = slice(FIRST, FIRST + PAIRS)
    for box in range(2):
        for tile in range(TILES):
            red_coef[box, tile, mid, :], black_coef[box, tile, mid, :] = split_colours(raw, box, tile)
            source[0, box, tile], source[1, box, tile] = split_colours(raw_side, box, tile)

    for colour in range(2):
        for box in range(2):
            cut_low = jnp.logical_not(low_linked[box])
            cut_high = jnp.logical_not(high_linked[box])
            low_rows = ((pair == PAIR_PAD) & cut_low) | ((pair == PAIR_PAD + 16) & cut_high)
            high_rows = ((pair == PAIR_PAD + 15) & cut_high) | ((pair == PAIR_PAD - 1) & cut_low)
            end = jnp.where(odd == colour, low_rows.astype(jnp.int32), high_rows.astype(jnp.int32)) == 1
            none = [code[box, k] == 0 for k in range(4)]
            for tile in range(TILES):
                own = coef[colour][box, tile, mid, :]
                near = nearby(coef, code, colour, box, tile)
                lost = (
                    end,
                    None,
                    (lane < 32) & none[0] if tile == 0 else None,
                    (lane >= 96) & none[1] if tile == TILES - 1 else None,
                    (depth == 0) & none[2],
                    (depth == 31) & none[3],
                )
                total = jnp.full((PAIRS, LANES), MASS_TERM, jnp.float32)
                kept = []
                for one, gone in zip(near, lost, strict=True):
                    if gone is None:
                        w = 0.5 * (own + one)
                        kept.append(w)
                    else:
                        w = 0.5 * (own + jnp.where(gone, own, one))
                        kept.append(jnp.where(gone, 0.0, w))
                    total = total + w
                inverse = 1.0 / total
                diagonal[colour, box, tile] = total
                source[colour, box, tile] = source[colour, box, tile] * inverse
                for d in range(6):
                    weight[colour, d, box, tile] = kept[d] * inverse


def smooth_kernel(
    shifts,
    links,
    parents,
    fields,
    near_a,
    near_b,
    far_a,
    far_b,
    red_out,
    black_out,
    red_left,
    black_left,
    coarse,
    raw_coef,
    raw_side,
    raw,
    red_coef,
    black_coef,
    red,
    black,
    weight,
    source,
    diagonal,
    code,
):
    make_weights(
        shifts, links, fields, near_a, near_b, far_a, far_b,
        weight, source, diagonal, code, raw_coef, raw_side, (red_coef, black_coef),
    )
    value = (red, black)
    position = lax.axis_index("box")
    offset = [shifts[k] for k in range(4)]
    _, here, after, _ = offset
    first_box = 2 * position
    even = position % 2 == 0
    lower = position % 4 < 2

    def place_local(box, row):
        for tile in range(TILES):
            raw[box, tile, PAD : PAD + OWN, :] = fields[0, 0, row, :, tile * LANES : (tile + 1) * LANES]

    def place_moved(box, ref):
        for tile in range(TILES):
            packed = ref[VALUE + 16 * tile : VALUE + 16 * tile + 16, :]
            raw[box, tile, PAD : PAD + 16, :] = packed
            raw[box, tile, PAD + 16 : PAD + 32, :] = pltpu.roll(packed, 1, 0)

    place_own(here, after, even, place_local, place_moved, (near_a, near_b))
    swaps = (crossing(links, 0, first_box - 2)[1], crossing(links, 1, first_box + 2)[1])
    zeros = jnp.zeros((8, LANES), jnp.float32)
    for tile in range(TILES):
        ends = neighbour_ends(
            offset, even, lower, swaps, fields, (near_a, near_b), (far_a, far_b), tile,
            VALUE_ENDS, FAR_VALUES, VALUE_SIZES, value_end,
        )
        for box in range(2):
            raw[box, tile, 0:8, :] = zeros
            raw[box, tile, PAD + OWN : PAD + OWN + 8, :] = zeros
            for base, pieces in zip((4, PAD + OWN), ends[box], strict=True):
                for k in range(4):
                    raw[box, tile, base + k : base + k + 1, :] = pieces[k // 2]

    mid = slice(FIRST, FIRST + PAIRS)
    for box in range(2):
        for tile in range(TILES):
            red[box, tile, mid, :], black[box, tile, mid, :] = split_colours(raw, box, tile)

    def update(colour, box, tile):
        total = source[colour, box, tile]
        for d, one in enumerate(nearby(value, code, colour, box, tile)):
            total = total + weight[colour, d, box, tile] * one
        return total

    def sweep(step, carry):
        for colour in range(2):
            for box in range(2):
                for tile in range(TILES):
                    value[colour][box, tile, mid, :] = update(colour, box, tile)
        return carry

    lax.fori_loop(0, 2, sweep, 0)

    own_pairs = slice(PAIR_PAD, PAIR_PAD + 16)
    own_rows = slice(FIRST + PAIR_PAD, FIRST + PAIR_PAD + 16)
    halves = TILES // 2
    gathered = []
    for half in range(2):
        for box in range(2):
            sums = []
            for tile in range(half * halves, (half + 1) * halves):
                total = None
                for colour, out, left in ((0, red_out, red_left), (1, black_out, black_left)):
                    kept = value[colour][box, tile, own_rows, :]
                    out[box, tile] = kept
                    rest = diagonal[colour, box, tile, own_pairs, :] * (
                        update(colour, box, tile)[own_pairs] - kept
                    )
                    left[box, tile] = rest
                    total = rest if total is None else total + rest
                sums.append(total)
            gathered.append(jnp.concatenate(sums, axis=1))
    whole = jnp.concatenate(gathered, axis=0)
    first = whole.astype(jnp.bfloat16)
    rest = whole - first.astype(jnp.float32)
    second = rest.astype(jnp.bfloat16)
    third = (rest - second.astype(jnp.float32)).astype(jnp.bfloat16)
    width = halves * LANES
    cell = lax.broadcasted_iota(jnp.int32, (width, LANES), 0)
    block = lax.broadcasted_iota(jnp.int32, (width, LANES), 1)
    merge = jnp.where((cell >> 6) * 16 + ((cell & 31) >> 1) == block, 1.0, 0.0).astype(jnp.bfloat16)
    split = jnp.dot(
        jnp.concatenate([first, second, third], axis=0), merge, preferred_element_type=jnp.float32
    )
    mean = (split[:64] + split[64:128] + split[128:]) * 0.125
    for half in range(2):
        coarse[0:32, half * LANES : (half + 1) * LANES] = mean[32 * half : 32 * half + 32]
    for box in range(2):
        label = parents[0, box, 0] * 16 + parents[0, box, 1] * 8 + parents[0, box, 2]
        coarse[32 + 8 * box : 40 + 8 * box, :] = jnp.full((8, 2 * LANES), label.astype(jnp.float32))


def unpack_kernel(red, black, red_left, black_left, smoothed, residual, stage):
    boxes, tiles = red.shape[:2]
    odd = odd_lanes(red.shape[2])
    for k, one, two, out in ((0, red, black, smoothed), (1, red_left, black_left, residual)):
        for box in range(boxes):
            for tile in range(tiles):
                low, high = one[box, tile], two[box, tile]
                stage[k, box, tile, pl.ds(0, 16, 2), :] = jnp.where(odd == 1, high, low)
                stage[k, box, tile, pl.ds(1, 16, 2), :] = jnp.where(odd == 1, low, high)
                out[0, box, :, tile * LANES : (tile + 1) * LANES] = stage[k, box, tile]


def place_kernel(*refs):
    *got, source, out = refs
    group = lax.axis_index("grp")
    base = (group * 16).astype(jnp.float32)
    for octant in range(16):
        kept = source[0, octant // 8, octant % 8]
        for sender in got:
            for box in range(2):
                label = sender[32 + 8 * box : 40 + 8 * box, :]
                mine = jnp.concatenate([label, label], axis=0) == base + float(octant)
                kept = jnp.where(mine, sender[16 * box : 16 * box + 16, :], kept)
        out[0, octant // 8, octant % 8] = kept


def per_device(old_fields, old_count, neighbours, parents, coarse_source):
    f32 = jnp.float32
    curve = lax.axis_size("box")
    box_edge, plane_cells = old_fields.shape[3:]
    boxes = neighbours.shape[1]
    params = pltpu.CompilerParams(vmem_limit_bytes=40 << 20)

    def cost(flops, size):
        return pl.CostEstimate(flops=flops, bytes_accessed=size, transcendentals=0)

    def rows(count):
        return jax.ShapeDtypeStruct((count, LANES), f32)

    def swap(message, distance, shift):
        ids = [i for i in range(curve - distance) if (i - shift) % (2 * distance) < distance]
        both = [(i, i + distance) for i in ids] + [(i + distance, i) for i in ids]
        return lax.ppermute(message, "box", both)

    near_a, near_b, shifts = pl.pallas_call(
        pack_kernel,
        out_shape=(rows(NEAR_ROWS), rows(NEAR_ROWS), jax.ShapeDtypeStruct((4,), jnp.int32)),
        in_specs=[HBM] * 3,
        out_specs=(VMEM, VMEM, SMEM),
        scratch_shapes=[
            pltpu.SMEM(old_count.shape, old_count.dtype),
            pltpu.SMEM(neighbours.shape, neighbours.dtype),
            pltpu.VMEM(old_fields.shape, f32),
            pltpu.SemaphoreType.DMA((2 + 3 * old_fields.shape[2],)),
        ],
        compiler_params=params,
        cost_estimate=cost(10**6, 2 << 20),
        name="pack",
    )(*[pltpu.with_memory_space_constraint(x, pltpu.HBM) for x in (old_count, neighbours, old_fields)])
    far_a, far_b = pl.pallas_call(
        pack_far_kernel,
        out_shape=(rows(FAR_ROWS),) * 2,
        in_specs=[SMEM, VMEM],
        out_specs=(VMEM,) * 2,
        compiler_params=params,
        cost_estimate=cost(10**6, 2 << 20),
        name="pack_far",
    )(shifts, old_fields)
    moved = [swap(near_a, 1, 0), swap(near_b, 1, 1), swap(far_a, 2, 0), swap(far_b, 2, 2)]
    packed = pltpu.VMEM((2, boxes, TILES, PAIRS, LANES), f32)
    column = pltpu.VMEM((boxes, TILES, PAIRS + 2 * FIRST, LANES), f32)
    raw = pltpu.VMEM((boxes, TILES, OWN + 2 * PAD, LANES), f32)
    weight = pltpu.VMEM((2, 6, boxes, TILES, PAIRS, LANES), f32)
    code = pltpu.VMEM((boxes, 4, PAIRS, LANES), f32)
    fine = jax.ShapeDtypeStruct((1, boxes, box_edge, plane_cells), f32)
    half = jax.ShapeDtypeStruct((boxes, TILES, box_edge // 2, LANES), f32)
    *halves, coarse = pl.pallas_call(
        smooth_kernel,
        out_shape=(half, half, half, half, jax.ShapeDtypeStruct((48, 2 * LANES), f32)),
        in_specs=[SMEM, SMEM, SMEM] + [VMEM] * 5,
        out_specs=(VMEM,) * 5,
        scratch_shapes=[raw] * 3 + [column] * 4 + [weight, packed, packed, code],
        compiler_params=params,
        cost_estimate=cost(10**7, 6 << 20),
        name="smooth",
    )(shifts, neighbours, parents, old_fields, *moved)
    def across(message, bit):
        return lax.ppermute(message, "grp", [(i, i ^ bit) for i in range(groups)])

    groups = lax.axis_size("grp")
    over_link = across(coarse, 2)
    got = [coarse, across(coarse, 1), over_link, across(over_link, 1)]
    smoothed, residual = pl.pallas_call(
        unpack_kernel,
        out_shape=(fine, fine),
        in_specs=[VMEM] * 4,
        out_specs=(VMEM,) * 2,
        scratch_shapes=[pltpu.VMEM((2, boxes, TILES, OWN, LANES), f32)],
        compiler_params=params,
        cost_estimate=pl.CostEstimate(flops=10**6, bytes_accessed=3 << 20, transcendentals=0),
        name="unpack",
    )(*halves)
    coarse_rhs = pl.pallas_call(
        place_kernel,
        out_shape=jax.ShapeDtypeStruct(coarse_source.shape, f32),
        in_specs=[VMEM] * (len(got) + 1),
        out_specs=VMEM,
        compiler_params=params,
        cost_estimate=pl.CostEstimate(flops=10**6, bytes_accessed=1 << 20, transcendentals=0),
        name="place",
    )(*got, coarse_source)
    return smoothed, residual, coarse_rhs


def solution(mesh):
    in_specs = (
        P(None, "grp", "box", None, None),
        P("grp", None),
        P("grp", "box", None),
        P("grp", "box", None),
        P("grp", "box", None, None, None),
    )
    out_specs = (
        P("grp", "box", None, None),
        P("grp", "box", None, None),
        P("grp", "box", None, None, None),
    )
    return jax.shard_map(
        per_device, mesh=mesh, in_specs=in_specs, out_specs=out_specs, check_vma=False
    )
```

```python
import jax
import jax.numpy as jnp
from jax import lax
from jax.experimental import pallas as pl
from jax.experimental.pallas import tpu as pltpu
from jax.sharding import PartitionSpec as P

MASS_TERM = 0.25
LANES = 128
OWN, ROWS, PAIRS, FIRST = 32, 48, 24, 8
LOAD_AHEAD, TURN_AHEAD = 20, 4
TILES = 8
SIDE_END, VALUE_END = 8, 2
SIDE = OWN * TILES
SIDE_ENDS = SIDE + OWN * TILES
LINKS = SIDE_ENDS + 2 * SIDE_END * TILES
VALUE = LINKS + 8
VALUE_ENDS = VALUE + OWN // 2 * TILES
NEAR_ROWS = VALUE_ENDS + 2 * VALUE_END * TILES
FAR_VALUES = SIDE_END * TILES
FAR_ROWS = FAR_VALUES + VALUE_END * TILES

VMEM = pl.BlockSpec(memory_space=pltpu.VMEM)
SMEM = pl.BlockSpec(memory_space=pltpu.SMEM)
HBM = pl.BlockSpec(memory_space=pltpu.HBM)


def lane_ids(rows):
    return lax.broadcasted_iota(jnp.int32, (rows, LANES), 1)


def row_ids(rows):
    return lax.broadcasted_iota(jnp.int32, (rows, LANES), 0)


def odd_lanes(rows):
    lane = lane_ids(rows)
    return ((lane >> 5) + lane) & 1


def offsets(counts, position):
    count = counts.shape[1]
    start = jnp.int32(0)
    for j in range(count):
        start = start + jnp.where(j < position, counts[0, j], 0)
    here = start - 2 * position
    after = here + counts[0, position] - 2
    before = here - counts[0, jnp.maximum(position - 1, 0)] + 2
    beyond = after + counts[0, jnp.minimum(position + 1, count - 1)] - 2
    return before, here, after, beyond


def link_code(links, box, face, first_box):
    target = links[0, box, face]
    return jnp.where(target < 0, 0, jnp.where(target - first_box == box, 1, 2))


def swap_depth(cells):
    odd = lane_ids(cells.shape[0]) & 1
    return jnp.where(odd == 1, pltpu.roll(cells, 1, 1), pltpu.roll(cells, LANES - 1, 1))


def end_tiles(fields, row, tile, upper):
    lanes = slice(tile * LANES, (tile + 1) * LANES)
    rows = slice(OWN - 8, OWN) if upper else slice(0, 8)
    return [fields[field, 0, row, rows, lanes] for field in range(3)]


def side_end(fields, row, tile, upper):
    sol, rhs, coef = end_tiles(fields, row, tile, upper)
    towards = 1 if upper else 7
    next_coef = pltpu.roll(coef, towards, 0)
    folded = rhs + 0.5 * (coef + next_coef) * pltpu.roll(sol, towards, 0)
    mixed = jnp.where(odd_lanes(8) == int(not upper), folded, swap_depth(next_coef))
    side = jnp.where(row_ids(8) == (4 if upper else 3), mixed, rhs)
    rows = slice(4, 8) if upper else slice(0, 4)
    return coef[rows], side[rows]


def value_end(fields, row, tile, upper):
    sol, _, _ = end_tiles(fields, row, tile, upper)
    packed = jnp.where(odd_lanes(8) == 1, sol, pltpu.roll(sol, 7, 0))
    return (packed[4:5], packed[6:7]) if upper else (packed[0:1], packed[2:3])


def store_rows(out, base, pieces):
    for piece in pieces:
        out[base : base + piece.shape[0], :] = piece
        base += piece.shape[0]


def load_rows(ref, base, sizes):
    pieces = []
    for size in sizes:
        pieces.append(ref[base : base + size, :])
        base += size
    return tuple(pieces)


SIDE_SIZES, VALUE_SIZES = (4, 4), (1, 1)


def slots(here):
    return (jnp.maximum(-here, 0), 1 - here), jnp.minimum(2 - here, 3)


def pack_kernel(counts_hbm, links_hbm, fields_hbm, near_a, near_b, counts, links, fields, sems):
    copies = []

    def fetch(source, target):
        copies.append(pltpu.make_async_copy(source, target, sems.at[len(copies)]))

    fetch(counts_hbm, counts)
    fetch(links_hbm, links)
    for row in range(fields.shape[2]):
        for field in range(3):
            fetch(fields_hbm.at[field, 0, row], fields.at[field, 0, row])
    for copy in copies:
        copy.start()
    for copy in copies:
        copy.wait()
    position = lax.axis_index("box")
    here = offsets(counts, position)[1]
    held, move_up = slots(here)
    codes = jnp.zeros((8, LANES), jnp.float32)
    for box in range(2):
        for face in range(2, 6):
            mine = (row_ids(8) == box) & (lane_ids(8) == face - 2)
            codes = jnp.where(mine, link_code(links, box, face, 2 * position).astype(jnp.float32), codes)

    mixed = (row_ids(16) + odd_lanes(16)) & 1

    def message(out, upper):
        row = move_up if upper else 0
        for tile in range(TILES):
            lanes = slice(tile * LANES, (tile + 1) * LANES)
            low = fields[0, 0, row, 0:16, lanes]
            high = pltpu.roll(fields[0, 0, row, 16:32, lanes], 15, 0)
            out[VALUE + 16 * tile : VALUE + 16 * tile + 16, :] = jnp.where(mixed == 1, low, high)
            out[OWN * tile : OWN * (tile + 1), :] = fields[2, 0, row, :, lanes]
            out[SIDE + OWN * tile : SIDE + OWN * (tile + 1), :] = fields[1, 0, row, :, lanes]
            for box in range(2):
                store_rows(
                    out, SIDE_ENDS + SIDE_END * (2 * tile + box), side_end(fields, held[box], tile, upper)
                )
                store_rows(
                    out, VALUE_ENDS + VALUE_END * (2 * tile + box), value_end(fields, held[box], tile, upper)
                )
        out[LINKS : LINKS + 8, :] = codes

    even = position % 2 == 0

    @pl.when(even)
    def _():
        message(near_a, True)
        message(near_b, False)

    @pl.when(jnp.logical_not(even))
    def _():
        message(near_a, False)
        message(near_b, True)


def pack_far_kernel(counts, fields, _, far_a, far_b):
    position = lax.axis_index("box")
    move_up = slots(offsets(counts, position)[1])[1]

    def far_message(out, upper):
        row = move_up if upper else 0
        for tile in range(TILES):
            store_rows(out, SIDE_END * tile, side_end(fields, row, tile, upper))
            store_rows(out, FAR_VALUES + VALUE_END * tile, value_end(fields, row, tile, upper))

    lower = position % 4 < 2

    @pl.when(lower)
    def _():
        far_message(far_a, True)
        far_message(far_b, False)

    @pl.when(jnp.logical_not(lower))
    def _():
        far_message(far_a, False)
        far_message(far_b, True)


def choose(flag, one, other):
    return tuple(jnp.where(flag, a, b) for a, b in zip(one, other, strict=True))


def crossing(links, face, run_first):
    ids = [links[0, box, face] for box in range(2)]
    linked = [one >= 0 for one in ids]
    swap = jnp.where(linked[0], ids[0] - run_first == 1, linked[1] & (ids[1] - run_first == 0))
    return linked, swap


def neighbour_ends(offset, even, lower, swaps, fields, near, far, tile, start, far_start, sizes, local):
    before, here, after, beyond = offset
    near_a, near_b = near
    far_a, far_b = far
    at = [start + sum(sizes) * (2 * tile + i) for i in range(2)]
    far_at = far_start + sum(sizes) * tile
    below = [choose(even, load_rows(near_b, at[i], sizes), load_rows(near_a, at[i], sizes)) for i in range(2)]
    above = [choose(even, load_rows(near_a, at[i], sizes), load_rows(near_b, at[i], sizes)) for i in range(2)]
    far_below = choose(lower, load_rows(far_b, far_at, sizes), load_rows(far_a, far_at, sizes))
    far_above = choose(lower, load_rows(far_a, far_at, sizes), load_rows(far_b, far_at, sizes))
    below = (choose(before == 1, far_below, below[0]), choose(here == -1, local(fields, 0, tile, True), below[1]))
    above = (
        choose(after == 1, local(fields, jnp.minimum(2 - here, 3), tile, False), above[0]),
        choose(beyond == -1, far_above, above[1]),
    )
    return [
        (choose(swaps[0], below[1 - box], below[box]), choose(swaps[1], above[1 - box], above[box]))
        for box in range(2)
    ]


def place_own(here, after, even, place_local, place_moved, near):
    from_below = here == 1
    from_above = after == -1
    held = slots(here)[0]
    for box, moved, first, second in ((0, from_below, near[1], near[0]), (1, from_above, near[0], near[1])):

        @pl.when(jnp.logical_not(moved))
        def _(box=box):
            place_local(box, held[box])

        @pl.when(moved & even)
        def _(box=box, ref=first):
            place_moved(box, ref)

        @pl.when(moved & jnp.logical_not(even))
        def _(box=box, ref=second):
            place_moved(box, ref)


def split_colours(raw, box, tile):
    odd = odd_lanes(PAIRS)
    low = raw[box, tile, pl.ds(0, PAIRS, 2), :]
    high = raw[box, tile, pl.ds(1, PAIRS, 2), :]
    return jnp.where(odd == 1, high, low), jnp.where(odd == 1, low, high)


def store_column(out, box, tile, cells):
    out[box, tile, FIRST : FIRST + PAIRS, :] = cells
    out[box, tile, FIRST - 1 : FIRST, :] = cells[PAIRS - 1 : PAIRS]
    out[box, tile, FIRST + PAIRS : FIRST + PAIRS + 1, :] = cells[0:1]


def block_rows(block, by=0):
    return slice(FIRST + 8 * block + by, FIRST + 8 * block + 8 + by)


def around(ref, colour, blocks, code, use):
    lane = lane_ids(8)
    depth = lane & 31
    low_layer = odd_lanes(8) == colour
    cells, up, down, turned = {}, {}, {}, {}

    def load(block, tile):
        for box in range(2):
            at = block, box, tile
            cells[at] = ref[box, tile, block_rows(block), :]
            up[at] = pltpu.roll(cells[at], 32, 1)
            down[at] = pltpu.roll(cells[at], 96, 1)

    def turn(block, tile):
        for box in range(2):
            at, there = (block, box, tile), (block, 1 - box, tile)
            z_low = jnp.where(code(block, box, 2) == 2, down[there], down[at])
            z_high = jnp.where(code(block, box, 3) == 2, up[there], up[at])
            turned[at] = (
                pltpu.roll(jnp.where(depth == 31, z_low, cells[at]), 1, 1),
                pltpu.roll(jnp.where(depth == 0, z_high, cells[at]), LANES - 1, 1),
            )

    def finish(block, tile):
        for box in range(2):
            at = block, box, tile
            y_low, y_high = up[block, box, (tile - 1) % TILES], down[block, box, (tile + 1) % TILES]
            if tile == 0:
                y_low = jnp.where(code(block, box, 0) == 2, up[block, 1 - box, TILES - 1], y_low)
            if tile == TILES - 1:
                y_high = jnp.where(code(block, box, 1) == 2, down[block, 1 - box, 0], y_high)
            across = jnp.where(
                low_layer, ref[box, tile, block_rows(block, -1), :], ref[box, tile, block_rows(block, 1), :]
            )
            use(
                block,
                box,
                tile,
                (
                    across,
                    cells[at],
                    jnp.where(lane >= 32, up[at], y_low),
                    jnp.where(lane < 96, down[at], y_high),
                    *turned[at],
                ),
            )

    loads = [(block, (tile - 1) % TILES) for block in range(blocks) for tile in range(TILES)]
    steps = [(block, tile) for block in range(blocks) for tile in range(TILES)]
    for k in range(len(steps) + LOAD_AHEAD):
        if k < len(loads):
            load(*loads[k])
        if 0 <= k - LOAD_AHEAD + TURN_AHEAD < len(steps):
            turn(*steps[k - LOAD_AHEAD + TURN_AHEAD])
        if k >= LOAD_AHEAD:
            finish(*steps[k - LOAD_AHEAD])


def smooth_kernel(
    counts,
    links,
    parents,
    fields,
    near_a,
    near_b,
    far_a,
    far_b,
    red_out,
    black_out,
    red_left,
    black_left,
    coarse,
    raw_coef,
    raw_side,
    raw_value,
    red_coef,
    black_coef,
    red,
    black,
    weight,
    source,
    diagonal,
    halo_code,
    sums,
):
    value, coef = (red, black), (red_coef, black_coef)
    position = lax.axis_index("box")
    offset = offsets(counts, position)
    _, here, after, _ = offset
    first_box = 2 * position
    even = position % 2 == 0
    lower = position % 4 < 2
    near, far = (near_a, near_b), (far_a, far_b)

    def place_local(box, row):
        for tile in range(TILES):
            lanes = slice(tile * LANES, (tile + 1) * LANES)
            raw_value[box, tile, 0:OWN, :] = fields[0, 0, row, :, lanes]
            raw_side[box, tile, 0:OWN, :] = fields[1, 0, row, :, lanes]
            raw_coef[box, tile, 0:OWN, :] = fields[2, 0, row, :, lanes]

    def place_moved(box, ref):
        for tile in range(TILES):
            packed = ref[VALUE + 16 * tile : VALUE + 16 * tile + 16, :]
            raw_value[box, tile, 0:16, :] = packed
            raw_value[box, tile, 16:32, :] = pltpu.roll(packed, 1, 0)
            raw_side[box, tile, 0:OWN, :] = ref[SIDE + OWN * tile : SIDE + OWN * (tile + 1), :]
            raw_coef[box, tile, 0:OWN, :] = ref[OWN * tile : OWN * (tile + 1), :]

    place_own(here, after, even, place_local, place_moved, near)
    low_linked, low_swap = crossing(links, 0, first_box - 2)
    high_linked, high_swap = crossing(links, 1, first_box + 2)
    swaps = (low_swap, high_swap)
    ones = jnp.ones((16, LANES), jnp.float32)
    zeros = jnp.zeros((16, LANES), jnp.float32)
    odd = odd_lanes(1)
    for tile in range(TILES):
        sides = neighbour_ends(
            offset, even, lower, swaps, fields, near, far, tile, SIDE_ENDS, 0, SIDE_SIZES, side_end
        )
        values = neighbour_ends(
            offset, even, lower, swaps, fields, near, far, tile, VALUE_ENDS, FAR_VALUES, VALUE_SIZES, value_end
        )
        for box in range(2):
            (below, side_below), (above, side_above) = sides[box]
            raw_coef[box, tile, 32:48, :] = ones
            raw_side[box, tile, 32:48, :] = ones
            raw_value[box, tile, 32:48, :] = zeros
            raw_coef[box, tile, 43:44, :] = jnp.where(odd == 0, swap_depth(side_below[0:1]), below[0:1])
            raw_coef[box, tile, 44:48, :] = below
            raw_side[box, tile, 44:48, :] = side_below
            raw_coef[box, tile, 32:36, :] = above
            raw_coef[box, tile, 36:37, :] = jnp.where(odd == 1, swap_depth(side_above[3:4]), above[3:4])
            raw_side[box, tile, 32:36, :] = side_above
            for base, pieces in zip((44, 32), values[box], strict=True):
                for k in range(4):
                    raw_value[box, tile, base + k : base + k + 1, :] = pieces[k // 2]

    own_code = [[link_code(links, box, face, first_box) for face in range(2, 6)] for box in range(2)]
    tile_a, tile_b = near_a[LINKS : LINKS + 8, :], near_b[LINKS : LINKS + 8, :]
    codes_below, codes_above = jnp.where(even, tile_b, tile_a), jnp.where(even, tile_a, tile_b)
    for face in range(4):
        spread = [
            [jnp.broadcast_to(one[i : i + 1, face : face + 1], (8, LANES)) for i in range(2)]
            for one in (codes_below, codes_above)
        ]
        for box in range(2):
            below = jnp.where(low_swap, spread[0][1 - box], spread[0][box])
            above = jnp.where(high_swap, spread[1][1 - box], spread[1][box])
            halo_code[box, face] = jnp.where(row_ids(8) < 4, above, below)

    def code(block, box, face):
        return own_code[box][face] if block < 2 else halo_code[box, face]

    for box in range(2):
        for tile in range(TILES):
            for raw, out in ((raw_value, value), (raw_coef, coef)):
                for colour, cells in enumerate(split_colours(raw, box, tile)):
                    store_column(out[colour], box, tile, cells)
            source[0, box, tile], source[1, box, tile] = split_colours(raw_side, box, tile)

    lane = lane_ids(8)
    depth = lane & 31
    row = row_ids(8)

    def weigh(colour):
        low_layer = odd_lanes(8) == colour

        def use(block, box, tile, near_coef):
            rows = slice(8 * block, 8 * block + 8)
            cut_low = jnp.logical_not(low_linked[box])
            cut_high = jnp.logical_not(high_linked[box])
            first_row, last_row = (row == 0) & low_layer, (row == 7) & jnp.logical_not(low_layer)
            end = (
                first_row & cut_low,
                last_row & cut_high,
                (first_row & cut_high) | (last_row & cut_low),
            )[block]
            lost = (
                end,
                None,
                (lane < 32) & (code(block, box, 0) == 0) if tile == 0 else None,
                (lane >= 96) & (code(block, box, 1) == 0) if tile == TILES - 1 else None,
                (depth == 0) & (code(block, box, 2) == 0),
                (depth == 31) & (code(block, box, 3) == 0),
            )
            own = coef[colour][box, tile, block_rows(block), :]
            total = jnp.full((8, LANES), MASS_TERM, jnp.float32)
            kept = []
            for one, gone in zip(near_coef, lost, strict=True):
                if gone is None:
                    w = 0.5 * (own + one)
                    kept.append(w)
                else:
                    w = 0.5 * (own + jnp.where(gone, own, one))
                    kept.append(jnp.where(gone, 0.0, w))
                total = total + w
            inverse = 1.0 / total
            diagonal[colour, box, tile, rows, :] = total
            source[colour, box, tile, rows, :] = source[colour, box, tile, rows, :] * inverse
            for d in range(6):
                weight[colour, d, box, tile, rows, :] = kept[d] * inverse

        around(coef[1 - colour], colour, 3, code, use)

    weigh(0)
    weigh(1)

    def update(colour, blocks, take):
        def use(block, box, tile, near_value):
            rows = slice(8 * block, 8 * block + 8)
            terms = [weight[colour, d, box, tile, rows, :] * one for d, one in enumerate(near_value)]
            total = (terms[0] + terms[1]) + (terms[2] + terms[3]) + (terms[4] + terms[5])
            take(block, box, tile, rows, source[colour, box, tile, rows, :] + total)

        around(value[1 - colour], colour, blocks, code, use)

    def sweep(step, carry):
        for colour in range(2):

            def take(block, box, tile, rows, fresh, out=value[colour]):
                out[box, tile, block_rows(block), :] = fresh
                if block == 0:
                    out[box, tile, FIRST + PAIRS : FIRST + PAIRS + 1, :] = fresh[0:1]
                if block == 2:
                    out[box, tile, FIRST - 1 : FIRST, :] = fresh[7:8]

            update(colour, 3, take)
        return carry

    lax.fori_loop(0, 2, sweep, 0)

    halves = TILES // 2
    for colour, out, left in ((0, red_out, red_left), (1, black_out, black_left)):

        def take(block, box, tile, rows, fresh, colour=colour, out=out, left=left):
            kept = value[colour][box, tile, block_rows(block), :]
            rest = diagonal[colour, box, tile, rows, :] * (fresh - kept)
            out[box, tile, rows, :] = kept
            left[box, tile, rows, :] = rest
            if colour == 1:
                at = 32 * (tile // halves) + 16 * box + 8 * block
                lanes = slice(tile % halves * LANES, (tile % halves + 1) * LANES)
                sums[at : at + 8, lanes] = red_left[box, tile, rows, :] + rest

        update(colour, 2, take)
    whole = sums[...]
    first = whole.astype(jnp.bfloat16)
    rest = whole - first.astype(jnp.float32)
    second = rest.astype(jnp.bfloat16)
    third = (rest - second.astype(jnp.float32)).astype(jnp.bfloat16)
    width = halves * LANES
    cell = lax.broadcasted_iota(jnp.int32, (width, LANES), 0)
    block = lax.broadcasted_iota(jnp.int32, (width, LANES), 1)
    merge = jnp.where((cell >> 6) * 16 + ((cell & 31) >> 1) == block, 1.0, 0.0).astype(jnp.bfloat16)
    split = jnp.dot(
        jnp.concatenate([first, second, third], axis=0), merge, preferred_element_type=jnp.float32
    )
    mean = (split[:64] + split[64:128] + split[128:]) * 0.125
    for half in range(2):
        coarse[0:32, half * LANES : (half + 1) * LANES] = mean[32 * half : 32 * half + 32]
    for box in range(2):
        label = parents[0, box, 0] * 16 + parents[0, box, 1] * 8 + parents[0, box, 2]
        coarse[32 + 8 * box : 40 + 8 * box, :] = jnp.full((8, 2 * LANES), label.astype(jnp.float32))


def unpack_kernel(red, black, red_left, black_left, smoothed, residual, stage):
    boxes, tiles = red.shape[:2]
    odd = odd_lanes(red.shape[2])
    for k, one, two, out in ((0, red, black, smoothed), (1, red_left, black_left, residual)):
        for box in range(boxes):
            for tile in range(tiles):
                low, high = one[box, tile], two[box, tile]
                stage[k, box, tile, pl.ds(0, 16, 2), :] = jnp.where(odd == 1, high, low)
                stage[k, box, tile, pl.ds(1, 16, 2), :] = jnp.where(odd == 1, low, high)
                out[0, box, :, tile * LANES : (tile + 1) * LANES] = stage[k, box, tile]


def place_kernel(*refs):
    *got, source, out = refs
    group = lax.axis_index("grp")
    base = (group * 16).astype(jnp.float32)
    for octant in range(16):
        kept = source[0, octant // 8, octant % 8]
        for sender in got:
            for box in range(2):
                label = sender[32 + 8 * box : 40 + 8 * box, :]
                mine = jnp.concatenate([label, label], axis=0) == base + float(octant)
                kept = jnp.where(mine, sender[16 * box : 16 * box + 16, :], kept)
        out[0, octant // 8, octant % 8] = kept


def per_device(old_fields, old_count, neighbours, parents, coarse_source):
    f32 = jnp.float32
    curve = lax.axis_size("box")
    box_edge, plane_cells = old_fields.shape[3:]
    boxes = neighbours.shape[1]
    params = pltpu.CompilerParams(vmem_limit_bytes=40 << 20)

    def cost(flops, size):
        return pl.CostEstimate(flops=flops, bytes_accessed=size, transcendentals=0)

    def rows(count):
        return jax.ShapeDtypeStruct((count, LANES), f32)

    def swap(message, distance, shift):
        ids = [i for i in range(curve - distance) if (i - shift) % (2 * distance) < distance]
        both = [(i, i + distance) for i in ids] + [(i + distance, i) for i in ids]
        return lax.ppermute(message, "box", both)

    near_a, near_b = pl.pallas_call(
        pack_kernel,
        out_shape=(rows(NEAR_ROWS),) * 2,
        in_specs=[HBM] * 3,
        out_specs=(VMEM,) * 2,
        scratch_shapes=[
            pltpu.SMEM(old_count.shape, old_count.dtype),
            pltpu.SMEM(neighbours.shape, neighbours.dtype),
            pltpu.VMEM(old_fields.shape, f32),
            pltpu.SemaphoreType.DMA((2 + 3 * old_fields.shape[2],)),
        ],
        compiler_params=params,
        cost_estimate=cost(10**6, 2 << 20),
        name="pack",
    )(*[pltpu.with_memory_space_constraint(x, pltpu.HBM) for x in (old_count, neighbours, old_fields)])
    far_a, far_b = pl.pallas_call(
        pack_far_kernel,
        out_shape=(rows(FAR_ROWS),) * 2,
        in_specs=[SMEM, VMEM, pl.BlockSpec(memory_space=pl.ANY)],
        out_specs=(VMEM,) * 2,
        compiler_params=params,
        cost_estimate=cost(10**6, 2 << 20),
        name="pack_far",
    )(old_count, old_fields, near_a)
    moved = [swap(near_a, 1, 0), swap(near_b, 1, 1), swap(far_a, 2, 0), swap(far_b, 2, 2)]
    packed = pltpu.VMEM((2, boxes, TILES, PAIRS, LANES), f32)
    column = pltpu.VMEM((boxes, TILES, PAIRS + 2 * FIRST, LANES), f32)
    raw = pltpu.VMEM((boxes, TILES, ROWS, LANES), f32)
    weight = pltpu.VMEM((2, 6, boxes, TILES, PAIRS, LANES), f32)
    code = pltpu.VMEM((boxes, 4, 8, LANES), f32)
    sums = pltpu.VMEM((32 * boxes, TILES // 2 * LANES), f32)
    fine = jax.ShapeDtypeStruct((1, boxes, box_edge, plane_cells), f32)
    half = jax.ShapeDtypeStruct((boxes, TILES, box_edge // 2, LANES), f32)
    *halves, coarse = pl.pallas_call(
        smooth_kernel,
        out_shape=(half, half, half, half, jax.ShapeDtypeStruct((48, 2 * LANES), f32)),
        in_specs=[SMEM, SMEM, SMEM] + [VMEM] * 5,
        out_specs=(VMEM,) * 5,
        scratch_shapes=[raw] * 3 + [column] * 4 + [weight, packed, packed, code, sums],
        compiler_params=params,
        cost_estimate=cost(10**7, 6 << 20),
        name="smooth",
    )(old_count, neighbours, parents, old_fields, *moved)
    groups = lax.axis_size("grp")
    got = [coarse] + [
        lax.ppermute(coarse, "grp", [(i, (i + k) % groups) for i in range(groups)])
        for k in range(1, groups)
    ]
    smoothed, residual = pl.pallas_call(
        unpack_kernel,
        out_shape=(fine, fine),
        in_specs=[VMEM] * 4,
        out_specs=(VMEM,) * 2,
        scratch_shapes=[pltpu.VMEM((2, boxes, TILES, OWN, LANES), f32)],
        compiler_params=params,
        cost_estimate=pl.CostEstimate(flops=10**6, bytes_accessed=3 << 20, transcendentals=0),
        name="unpack",
    )(*halves)
    coarse_rhs = pl.pallas_call(
        place_kernel,
        out_shape=jax.ShapeDtypeStruct(coarse_source.shape, f32),
        in_specs=[VMEM] * (len(got) + 1),
        out_specs=VMEM,
        compiler_params=params,
        cost_estimate=pl.CostEstimate(flops=10**6, bytes_accessed=1 << 20, transcendentals=0),
        name="place",
    )(*got, coarse_source)
    return smoothed, residual, coarse_rhs


def solution(mesh):
    in_specs = (
        P(None, "grp", "box", None, None),
        P("grp", None),
        P("grp", "box", None),
        P("grp", "box", None),
        P("grp", "box", None, None, None),
    )
    out_specs = (
        P("grp", "box", None, None),
        P("grp", "box", None, None),
        P("grp", "box", None, None, None),
    )
    return jax.shard_map(
        per_device, mesh=mesh, in_specs=in_specs, out_specs=out_specs, check_vma=False
    )
```

```python
import jax
import jax.numpy as jnp
from jax import lax
from jax.experimental import pallas as pl
from jax.experimental.pallas import tpu as pltpu
from jax.sharding import PartitionSpec as P

MASS_TERM = 0.25
LANES = 128
OWN, ROWS, PAIRS, FIRST = 32, 48, 24, 8
LOAD_AHEAD, TURN_AHEAD = 20, 4
TILES = 8
SIDE_END, VALUE_END = 8, 2
SIDE = OWN * TILES
SIDE_ENDS = SIDE + OWN * TILES
LINKS = SIDE_ENDS + 2 * SIDE_END * TILES
VALUE = LINKS + 8
VALUE_ENDS = VALUE + OWN // 2 * TILES
NEAR_ROWS = VALUE_ENDS + 2 * VALUE_END * TILES
FAR_VALUES = SIDE_END * TILES
FAR_ROWS = FAR_VALUES + VALUE_END * TILES

VMEM = pl.BlockSpec(memory_space=pltpu.VMEM)
SMEM = pl.BlockSpec(memory_space=pltpu.SMEM)
HBM = pl.BlockSpec(memory_space=pltpu.HBM)


def lane_ids(rows):
    return lax.broadcasted_iota(jnp.int32, (rows, LANES), 1)


def row_ids(rows):
    return lax.broadcasted_iota(jnp.int32, (rows, LANES), 0)


def odd_lanes(rows):
    lane = lane_ids(rows)
    return ((lane >> 5) + lane) & 1


def offsets(counts, position):
    count = counts.shape[1]
    start = jnp.int32(0)
    for j in range(count):
        start = start + jnp.where(j < position, counts[0, j], 0)
    here = start - 2 * position
    after = here + counts[0, position] - 2
    before = here - counts[0, jnp.maximum(position - 1, 0)] + 2
    beyond = after + counts[0, jnp.minimum(position + 1, count - 1)] - 2
    return before, here, after, beyond


def link_code(links, box, face, first_box):
    target = links[0, box, face]
    return jnp.where(target < 0, 0, jnp.where(target - first_box == box, 1, 2))


def swap_depth(cells):
    odd = lane_ids(cells.shape[0]) & 1
    return jnp.where(odd == 1, pltpu.roll(cells, 1, 1), pltpu.roll(cells, LANES - 1, 1))


def end_tiles(fields, row, tile, upper):
    lanes = slice(tile * LANES, (tile + 1) * LANES)
    rows = slice(OWN - 8, OWN) if upper else slice(0, 8)
    return [fields[field, 0, row, rows, lanes] for field in range(3)]


def side_end(fields, row, tile, upper):
    sol, rhs, coef = end_tiles(fields, row, tile, upper)
    towards = 1 if upper else 7
    next_coef = pltpu.roll(coef, towards, 0)
    folded = rhs + 0.5 * (coef + next_coef) * pltpu.roll(sol, towards, 0)
    mixed = jnp.where(odd_lanes(8) == int(not upper), folded, swap_depth(next_coef))
    side = jnp.where(row_ids(8) == (4 if upper else 3), mixed, rhs)
    rows = slice(4, 8) if upper else slice(0, 4)
    return coef[rows], side[rows]


def value_end(fields, row, tile, upper):
    sol, _, _ = end_tiles(fields, row, tile, upper)
    packed = jnp.where(odd_lanes(8) == 1, sol, pltpu.roll(sol, 7, 0))
    return (packed[4:5], packed[6:7]) if upper else (packed[0:1], packed[2:3])


def store_rows(out, base, pieces):
    for piece in pieces:
        out[base : base + piece.shape[0], :] = piece
        base += piece.shape[0]


def load_rows(ref, base, sizes):
    pieces = []
    for size in sizes:
        pieces.append(ref[base : base + size, :])
        base += size
    return tuple(pieces)


SIDE_SIZES, VALUE_SIZES = (4, 4), (1, 1)


def slots(here):
    return (jnp.maximum(-here, 0), 1 - here), jnp.minimum(2 - here, 3)


def pack_kernel(counts_hbm, links_hbm, fields_hbm, near_a, near_b, counts, links, fields, sems):
    copies = []

    def fetch(source, target):
        copies.append(pltpu.make_async_copy(source, target, sems.at[len(copies)]))

    fetch(counts_hbm, counts)
    fetch(links_hbm, links)
    for row in range(fields.shape[2]):
        for field in range(3):
            fetch(fields_hbm.at[field, 0, row], fields.at[field, 0, row])
    for copy in copies:
        copy.start()
    for copy in copies:
        copy.wait()
    position = lax.axis_index("box")
    here = offsets(counts, position)[1]
    held, move_up = slots(here)
    codes = jnp.zeros((8, LANES), jnp.float32)
    for box in range(2):
        for face in range(2, 6):
            mine = (row_ids(8) == box) & (lane_ids(8) == face - 2)
            codes = jnp.where(mine, link_code(links, box, face, 2 * position).astype(jnp.float32), codes)

    mixed = (row_ids(16) + odd_lanes(16)) & 1

    def message(out, upper):
        row = move_up if upper else 0
        for tile in range(TILES):
            lanes = slice(tile * LANES, (tile + 1) * LANES)
            low = fields[0, 0, row, 0:16, lanes]
            high = pltpu.roll(fields[0, 0, row, 16:32, lanes], 15, 0)
            out[VALUE + 16 * tile : VALUE + 16 * tile + 16, :] = jnp.where(mixed == 1, low, high)
            out[OWN * tile : OWN * (tile + 1), :] = fields[2, 0, row, :, lanes]
            out[SIDE + OWN * tile : SIDE + OWN * (tile + 1), :] = fields[1, 0, row, :, lanes]
            for box in range(2):
                store_rows(
                    out, SIDE_ENDS + SIDE_END * (2 * tile + box), side_end(fields, held[box], tile, upper)
                )
                store_rows(
                    out, VALUE_ENDS + VALUE_END * (2 * tile + box), value_end(fields, held[box], tile, upper)
                )
        out[LINKS : LINKS + 8, :] = codes

    even = position % 2 == 0

    @pl.when(even)
    def _():
        message(near_a, True)
        message(near_b, False)

    @pl.when(jnp.logical_not(even))
    def _():
        message(near_a, False)
        message(near_b, True)


def pack_far_kernel(counts, fields, _, far_a, far_b):
    position = lax.axis_index("box")
    move_up = slots(offsets(counts, position)[1])[1]

    def far_message(out, upper):
        row = move_up if upper else 0
        for tile in range(TILES):
            store_rows(out, SIDE_END * tile, side_end(fields, row, tile, upper))
            store_rows(out, FAR_VALUES + VALUE_END * tile, value_end(fields, row, tile, upper))

    lower = position % 4 < 2

    @pl.when(lower)
    def _():
        far_message(far_a, True)
        far_message(far_b, False)

    @pl.when(jnp.logical_not(lower))
    def _():
        far_message(far_a, False)
        far_message(far_b, True)


def choose(flag, one, other):
    return tuple(jnp.where(flag, a, b) for a, b in zip(one, other, strict=True))


def crossing(links, face, run_first):
    ids = [links[0, box, face] for box in range(2)]
    linked = [one >= 0 for one in ids]
    swap = jnp.where(linked[0], ids[0] - run_first == 1, linked[1] & (ids[1] - run_first == 0))
    return linked, swap


def neighbour_ends(offset, even, lower, swaps, fields, near, far, tile, start, far_start, sizes, local):
    before, here, after, beyond = offset
    near_a, near_b = near
    far_a, far_b = far
    at = [start + sum(sizes) * (2 * tile + i) for i in range(2)]
    far_at = far_start + sum(sizes) * tile
    below = [choose(even, load_rows(near_b, at[i], sizes), load_rows(near_a, at[i], sizes)) for i in range(2)]
    above = [choose(even, load_rows(near_a, at[i], sizes), load_rows(near_b, at[i], sizes)) for i in range(2)]
    far_below = choose(lower, load_rows(far_b, far_at, sizes), load_rows(far_a, far_at, sizes))
    far_above = choose(lower, load_rows(far_a, far_at, sizes), load_rows(far_b, far_at, sizes))
    below = (choose(before == 1, far_below, below[0]), choose(here == -1, local(fields, 0, tile, True), below[1]))
    above = (
        choose(after == 1, local(fields, jnp.minimum(2 - here, 3), tile, False), above[0]),
        choose(beyond == -1, far_above, above[1]),
    )
    return [
        (choose(swaps[0], below[1 - box], below[box]), choose(swaps[1], above[1 - box], above[box]))
        for box in range(2)
    ]


def place_own(here, after, even, place_local, place_moved, near):
    from_below = here == 1
    from_above = after == -1
    held = slots(here)[0]
    for box, moved, first, second in ((0, from_below, near[1], near[0]), (1, from_above, near[0], near[1])):

        @pl.when(jnp.logical_not(moved))
        def _(box=box):
            place_local(box, held[box])

        @pl.when(moved & even)
        def _(box=box, ref=first):
            place_moved(box, ref)

        @pl.when(moved & jnp.logical_not(even))
        def _(box=box, ref=second):
            place_moved(box, ref)


def split_colours(raw, box, tile):
    odd = odd_lanes(PAIRS)
    low = raw[box, tile, pl.ds(0, PAIRS, 2), :]
    high = raw[box, tile, pl.ds(1, PAIRS, 2), :]
    return jnp.where(odd == 1, high, low), jnp.where(odd == 1, low, high)


def store_column(out, box, tile, cells):
    out[box, tile, FIRST : FIRST + PAIRS, :] = cells
    out[box, tile, FIRST - 1 : FIRST, :] = cells[PAIRS - 1 : PAIRS]
    out[box, tile, FIRST + PAIRS : FIRST + PAIRS + 1, :] = cells[0:1]


def block_rows(block, by=0):
    return slice(FIRST + 8 * block + by, FIRST + 8 * block + 8 + by)


def around(ref, colour, blocks, code, use):
    lane = lane_ids(8)
    depth = lane & 31
    low_layer = odd_lanes(8) == colour
    cells, up, down, turned = {}, {}, {}, {}

    def load(block, tile):
        for box in range(2):
            at = block, box, tile
            cells[at] = ref[box, tile, block_rows(block), :]
            up[at] = pltpu.roll(cells[at], 32, 1)
            down[at] = pltpu.roll(cells[at], 96, 1)

    def turn(block, tile):
        for box in range(2):
            at, there = (block, box, tile), (block, 1 - box, tile)
            z_low = jnp.where(code(block, box, 2) == 2, down[there], down[at])
            z_high = jnp.where(code(block, box, 3) == 2, up[there], up[at])
            turned[at] = (
                pltpu.roll(jnp.where(depth == 31, z_low, cells[at]), 1, 1),
                pltpu.roll(jnp.where(depth == 0, z_high, cells[at]), LANES - 1, 1),
            )

    def finish(block, tile):
        for box in range(2):
            at = block, box, tile
            y_low, y_high = up[block, box, (tile - 1) % TILES], down[block, box, (tile + 1) % TILES]
            if tile == 0:
                y_low = jnp.where(code(block, box, 0) == 2, up[block, 1 - box, TILES - 1], y_low)
            if tile == TILES - 1:
                y_high = jnp.where(code(block, box, 1) == 2, down[block, 1 - box, 0], y_high)
            across = jnp.where(
                low_layer, ref[box, tile, block_rows(block, -1), :], ref[box, tile, block_rows(block, 1), :]
            )
            use(
                block,
                box,
                tile,
                (
                    across,
                    cells[at],
                    jnp.where(lane >= 32, up[at], y_low),
                    jnp.where(lane < 96, down[at], y_high),
                    *turned[at],
                ),
            )

    loads = [(block, (tile - 1) % TILES) for block in range(blocks) for tile in range(TILES)]
    steps = [(block, tile) for block in range(blocks) for tile in range(TILES)]
    for k in range(len(steps) + LOAD_AHEAD):
        if k < len(loads):
            load(*loads[k])
        if 0 <= k - LOAD_AHEAD + TURN_AHEAD < len(steps):
            turn(*steps[k - LOAD_AHEAD + TURN_AHEAD])
        if k >= LOAD_AHEAD:
            finish(*steps[k - LOAD_AHEAD])


def smooth_kernel(
    counts,
    links,
    parents,
    fields,
    near_a,
    near_b,
    far_a,
    far_b,
    red_out,
    black_out,
    red_left,
    black_left,
    coarse,
    raw_coef,
    raw_side,
    raw_value,
    red_coef,
    black_coef,
    red,
    black,
    weight,
    source,
    diagonal,
    halo_code,
    sums,
):
    value, coef = (red, black), (red_coef, black_coef)
    position = lax.axis_index("box")
    offset = offsets(counts, position)
    _, here, after, _ = offset
    first_box = 2 * position
    even = position % 2 == 0
    lower = position % 4 < 2
    near, far = (near_a, near_b), (far_a, far_b)

    def place_local(box, row):
        for tile in range(TILES):
            lanes = slice(tile * LANES, (tile + 1) * LANES)
            raw_value[box, tile, 0:OWN, :] = fields[0, 0, row, :, lanes]
            raw_side[box, tile, 0:OWN, :] = fields[1, 0, row, :, lanes]
            raw_coef[box, tile, 0:OWN, :] = fields[2, 0, row, :, lanes]

    def place_moved(box, ref):
        for tile in range(TILES):
            packed = ref[VALUE + 16 * tile : VALUE + 16 * tile + 16, :]
            raw_value[box, tile, 0:16, :] = packed
            raw_value[box, tile, 16:32, :] = pltpu.roll(packed, 1, 0)
            raw_side[box, tile, 0:OWN, :] = ref[SIDE + OWN * tile : SIDE + OWN * (tile + 1), :]
            raw_coef[box, tile, 0:OWN, :] = ref[OWN * tile : OWN * (tile + 1), :]

    place_own(here, after, even, place_local, place_moved, near)
    low_linked, low_swap = crossing(links, 0, first_box - 2)
    high_linked, high_swap = crossing(links, 1, first_box + 2)
    swaps = (low_swap, high_swap)
    ones = jnp.ones((16, LANES), jnp.float32)
    zeros = jnp.zeros((16, LANES), jnp.float32)
    odd = odd_lanes(1)
    for tile in range(TILES):
        sides = neighbour_ends(
            offset, even, lower, swaps, fields, near, far, tile, SIDE_ENDS, 0, SIDE_SIZES, side_end
        )
        values = neighbour_ends(
            offset, even, lower, swaps, fields, near, far, tile, VALUE_ENDS, FAR_VALUES, VALUE_SIZES, value_end
        )
        for box in range(2):
            (below, side_below), (above, side_above) = sides[box]
            raw_coef[box, tile, 32:48, :] = ones
            raw_side[box, tile, 32:48, :] = ones
            raw_value[box, tile, 32:48, :] = zeros
            raw_coef[box, tile, 43:44, :] = jnp.where(odd == 0, swap_depth(side_below[0:1]), below[0:1])
            raw_coef[box, tile, 44:48, :] = below
            raw_side[box, tile, 44:48, :] = side_below
            raw_coef[box, tile, 32:36, :] = above
            raw_coef[box, tile, 36:37, :] = jnp.where(odd == 1, swap_depth(side_above[3:4]), above[3:4])
            raw_side[box, tile, 32:36, :] = side_above
            for base, pieces in zip((44, 32), values[box], strict=True):
                for k in range(4):
                    raw_value[box, tile, base + k : base + k + 1, :] = pieces[k // 2]

    own_code = [[link_code(links, box, face, first_box) for face in range(2, 6)] for box in range(2)]
    tile_a, tile_b = near_a[LINKS : LINKS + 8, :], near_b[LINKS : LINKS + 8, :]
    codes_below, codes_above = jnp.where(even, tile_b, tile_a), jnp.where(even, tile_a, tile_b)
    for face in range(4):
        spread = [
            [jnp.broadcast_to(one[i : i + 1, face : face + 1], (8, LANES)) for i in range(2)]
            for one in (codes_below, codes_above)
        ]
        for box in range(2):
            below = jnp.where(low_swap, spread[0][1 - box], spread[0][box])
            above = jnp.where(high_swap, spread[1][1 - box], spread[1][box])
            halo_code[box, face] = jnp.where(row_ids(8) < 4, above, below)

    def code(block, box, face):
        return own_code[box][face] if block < 2 else halo_code[box, face]

    for box in range(2):
        for tile in range(TILES):
            for raw, out in ((raw_value, value), (raw_coef, coef)):
                for colour, cells in enumerate(split_colours(raw, box, tile)):
                    store_column(out[colour], box, tile, cells)
            source[0, box, tile], source[1, box, tile] = split_colours(raw_side, box, tile)

    lane = lane_ids(8)
    depth = lane & 31
    row = row_ids(8)

    def weigh(colour):
        low_layer = odd_lanes(8) == colour

        def use(block, box, tile, near_coef):
            rows = slice(8 * block, 8 * block + 8)
            cut_low = jnp.logical_not(low_linked[box])
            cut_high = jnp.logical_not(high_linked[box])
            first_row, last_row = (row == 0) & low_layer, (row == 7) & jnp.logical_not(low_layer)
            end = (
                first_row & cut_low,
                last_row & cut_high,
                (first_row & cut_high) | (last_row & cut_low),
            )[block]
            lost = (
                end,
                None,
                (lane < 32) & (code(block, box, 0) == 0) if tile == 0 else None,
                (lane >= 96) & (code(block, box, 1) == 0) if tile == TILES - 1 else None,
                (depth == 0) & (code(block, box, 2) == 0),
                (depth == 31) & (code(block, box, 3) == 0),
            )
            own = coef[colour][box, tile, block_rows(block), :]
            total = jnp.full((8, LANES), MASS_TERM, jnp.float32)
            kept = []
            for one, gone in zip(near_coef, lost, strict=True):
                if gone is None:
                    w = 0.5 * (own + one)
                    kept.append(w)
                else:
                    w = 0.5 * (own + jnp.where(gone, own, one))
                    kept.append(jnp.where(gone, 0.0, w))
                total = total + w
            inverse = 1.0 / total
            diagonal[colour, box, tile, rows, :] = total
            source[colour, box, tile, rows, :] = source[colour, box, tile, rows, :] * inverse
            for d in range(6):
                weight[colour, d, box, tile, rows, :] = kept[d] * inverse

        around(coef[1 - colour], colour, 3, code, use)

    weigh(0)
    weigh(1)

    def update(colour, blocks, take):
        def use(block, box, tile, near_value):
            rows = slice(8 * block, 8 * block + 8)
            terms = [weight[colour, d, box, tile, rows, :] * one for d, one in enumerate(near_value)]
            total = (terms[0] + terms[1]) + (terms[2] + terms[3]) + (terms[4] + terms[5])
            take(block, box, tile, rows, source[colour, box, tile, rows, :] + total)

        around(value[1 - colour], colour, blocks, code, use)

    def sweep(step, carry):
        for colour in range(2):

            def take(block, box, tile, rows, fresh, out=value[colour]):
                out[box, tile, block_rows(block), :] = fresh
                if block == 0:
                    out[box, tile, FIRST + PAIRS : FIRST + PAIRS + 1, :] = fresh[0:1]
                if block == 2:
                    out[box, tile, FIRST - 1 : FIRST, :] = fresh[7:8]

            update(colour, 3, take)
        return carry

    lax.fori_loop(0, 2, sweep, 0)

    halves = TILES // 2
    for colour, out, left in ((0, red_out, red_left), (1, black_out, black_left)):

        def take(block, box, tile, rows, fresh, colour=colour, out=out, left=left):
            kept = value[colour][box, tile, block_rows(block), :]
            rest = diagonal[colour, box, tile, rows, :] * (fresh - kept)
            out[box, tile, rows, :] = kept
            left[box, tile, rows, :] = rest
            if colour == 1:
                at = 32 * (tile // halves) + 16 * box + 8 * block
                lanes = slice(tile % halves * LANES, (tile % halves + 1) * LANES)
                sums[at : at + 8, lanes] = red_left[box, tile, rows, :] + rest

        update(colour, 2, take)
    whole = sums[...]
    first = whole.astype(jnp.bfloat16)
    rest = whole - first.astype(jnp.float32)
    second = rest.astype(jnp.bfloat16)
    third = (rest - second.astype(jnp.float32)).astype(jnp.bfloat16)
    width = halves * LANES
    cell = lax.broadcasted_iota(jnp.int32, (width, LANES), 0)
    block = lax.broadcasted_iota(jnp.int32, (width, LANES), 1)
    merge = jnp.where((cell >> 6) * 16 + ((cell & 31) >> 1) == block, 1.0, 0.0).astype(jnp.bfloat16)
    split = jnp.dot(
        jnp.concatenate([first, second, third], axis=0), merge, preferred_element_type=jnp.float32
    )
    mean = (split[:64] + split[64:128] + split[128:]) * 0.125
    for half in range(2):
        coarse[0:32, half * LANES : (half + 1) * LANES] = mean[32 * half : 32 * half + 32]
    for box in range(2):
        label = parents[0, box, 0] * 16 + parents[0, box, 1] * 8 + parents[0, box, 2]
        coarse[32 + 8 * box : 40 + 8 * box, :] = jnp.full((8, 2 * LANES), label.astype(jnp.float32))


def unpack_kernel(red, black, red_left, black_left, smoothed, residual, stage):
    boxes, tiles = red.shape[:2]
    odd = odd_lanes(red.shape[2])
    for k, one, two, out in ((0, red, black, smoothed), (1, red_left, black_left, residual)):
        for box in range(boxes):
            for tile in range(tiles):
                low, high = one[box, tile], two[box, tile]
                stage[k, box, tile, pl.ds(0, 16, 2), :] = jnp.where(odd == 1, high, low)
                stage[k, box, tile, pl.ds(1, 16, 2), :] = jnp.where(odd == 1, low, high)
                out[0, box, :, tile * LANES : (tile + 1) * LANES] = stage[k, box, tile]


def place_kernel(*refs):
    *got, source, out = refs
    group = lax.axis_index("grp")
    base = (group * 16).astype(jnp.float32)
    for octant in range(16):
        kept = source[0, octant // 8, octant % 8]
        for sender in got:
            for box in range(2):
                label = sender[32 + 8 * box : 40 + 8 * box, :]
                mine = jnp.concatenate([label, label], axis=0) == base + float(octant)
                kept = jnp.where(mine, sender[16 * box : 16 * box + 16, :], kept)
        out[0, octant // 8, octant % 8] = kept


def per_device(old_fields, old_count, neighbours, parents, coarse_source):
    f32 = jnp.float32
    curve = lax.axis_size("box")
    box_edge, plane_cells = old_fields.shape[3:]
    boxes = neighbours.shape[1]
    params = pltpu.CompilerParams(vmem_limit_bytes=40 << 20)

    def cost(flops, size):
        return pl.CostEstimate(flops=flops, bytes_accessed=size, transcendentals=0)

    def rows(count):
        return jax.ShapeDtypeStruct((count, LANES), f32)

    def swap(message, distance, shift):
        ids = [i for i in range(curve - distance) if (i - shift) % (2 * distance) < distance]
        both = [(i, i + distance) for i in ids] + [(i + distance, i) for i in ids]
        return lax.ppermute(message, "box", both)

    near_a, near_b = pl.pallas_call(
        pack_kernel,
        out_shape=(rows(NEAR_ROWS),) * 2,
        in_specs=[HBM] * 3,
        out_specs=(VMEM,) * 2,
        scratch_shapes=[
            pltpu.SMEM(old_count.shape, old_count.dtype),
            pltpu.SMEM(neighbours.shape, neighbours.dtype),
            pltpu.VMEM(old_fields.shape, f32),
            pltpu.SemaphoreType.DMA((2 + 3 * old_fields.shape[2],)),
        ],
        compiler_params=params,
        cost_estimate=cost(10**6, 2 << 20),
        name="pack",
    )(*[pltpu.with_memory_space_constraint(x, pltpu.HBM) for x in (old_count, neighbours, old_fields)])
    far_a, far_b = pl.pallas_call(
        pack_far_kernel,
        out_shape=(rows(FAR_ROWS),) * 2,
        in_specs=[SMEM, VMEM, pl.BlockSpec(memory_space=pl.ANY)],
        out_specs=(VMEM,) * 2,
        compiler_params=params,
        cost_estimate=cost(10**6, 2 << 20),
        name="pack_far",
    )(old_count, old_fields, near_b)
    moved = [swap(near_a, 1, 0), swap(near_b, 1, 1), swap(far_a, 2, 0), swap(far_b, 2, 2)]
    packed = pltpu.VMEM((2, boxes, TILES, PAIRS, LANES), f32)
    column = pltpu.VMEM((boxes, TILES, PAIRS + 2 * FIRST, LANES), f32)
    raw = pltpu.VMEM((boxes, TILES, ROWS, LANES), f32)
    weight = pltpu.VMEM((2, 6, boxes, TILES, PAIRS, LANES), f32)
    code = pltpu.VMEM((boxes, 4, 8, LANES), f32)
    sums = pltpu.VMEM((32 * boxes, TILES // 2 * LANES), f32)
    fine = jax.ShapeDtypeStruct((1, boxes, box_edge, plane_cells), f32)
    half = jax.ShapeDtypeStruct((boxes, TILES, box_edge // 2, LANES), f32)
    *halves, coarse = pl.pallas_call(
        smooth_kernel,
        out_shape=(half, half, half, half, jax.ShapeDtypeStruct((48, 2 * LANES), f32)),
        in_specs=[SMEM, SMEM, SMEM] + [VMEM] * 5,
        out_specs=(VMEM,) * 5,
        scratch_shapes=[raw] * 3 + [column] * 4 + [weight, packed, packed, code, sums],
        compiler_params=params,
        cost_estimate=cost(10**7, 6 << 20),
        name="smooth",
    )(old_count, neighbours, parents, old_fields, *moved)
    groups = lax.axis_size("grp")
    got = [coarse] + [
        lax.ppermute(coarse, "grp", [(i, (i + k) % groups) for i in range(groups)])
        for k in range(1, groups)
    ]
    smoothed, residual = pl.pallas_call(
        unpack_kernel,
        out_shape=(fine, fine),
        in_specs=[VMEM] * 4,
        out_specs=(VMEM,) * 2,
        scratch_shapes=[pltpu.VMEM((2, boxes, TILES, OWN, LANES), f32)],
        compiler_params=params,
        cost_estimate=pl.CostEstimate(flops=10**6, bytes_accessed=3 << 20, transcendentals=0),
        name="unpack",
    )(*halves)
    coarse_rhs = pl.pallas_call(
        place_kernel,
        out_shape=jax.ShapeDtypeStruct(coarse_source.shape, f32),
        in_specs=[VMEM] * (len(got) + 1),
        out_specs=VMEM,
        compiler_params=params,
        cost_estimate=pl.CostEstimate(flops=10**6, bytes_accessed=1 << 20, transcendentals=0),
        name="place",
    )(*got, coarse_source)
    return smoothed, residual, coarse_rhs


def solution(mesh):
    in_specs = (
        P(None, "grp", "box", None, None),
        P("grp", None),
        P("grp", "box", None),
        P("grp", "box", None),
        P("grp", "box", None, None, None),
    )
    out_specs = (
        P("grp", "box", None, None),
        P("grp", "box", None, None),
        P("grp", "box", None, None, None),
    )
    return jax.shard_map(
        per_device, mesh=mesh, in_specs=in_specs, out_specs=out_specs, check_vma=False
    )
```

```python
import jax
import jax.numpy as jnp
from jax import lax
from jax.experimental import pallas as pl
from jax.experimental.pallas import tpu as pltpu
from jax.sharding import PartitionSpec as P

MASS_TERM = 0.25
LANES = 128
OWN, ROWS, PAIRS, FIRST = 32, 48, 24, 8
LOAD_AHEAD, TURN_AHEAD = 20, 4
TILES = 8
SIDE_END, VALUE_END = 8, 2
SIDE = OWN * TILES
SIDE_ENDS = SIDE + OWN * TILES
LINKS = SIDE_ENDS + 2 * SIDE_END * TILES
VALUE = LINKS + 8
VALUE_ENDS = VALUE + OWN // 2 * TILES
NEAR_ROWS = VALUE_ENDS + 2 * VALUE_END * TILES
FAR_VALUES = SIDE_END * TILES
FAR_ROWS = FAR_VALUES + VALUE_END * TILES

VMEM = pl.BlockSpec(memory_space=pltpu.VMEM)
SMEM = pl.BlockSpec(memory_space=pltpu.SMEM)
HBM = pl.BlockSpec(memory_space=pltpu.HBM)


def lane_ids(rows):
    return lax.broadcasted_iota(jnp.int32, (rows, LANES), 1)


def row_ids(rows):
    return lax.broadcasted_iota(jnp.int32, (rows, LANES), 0)


def odd_lanes(rows):
    lane = lane_ids(rows)
    return ((lane >> 5) + lane) & 1


def offsets(counts, position):
    count = counts.shape[1]
    start = jnp.int32(0)
    for j in range(count):
        start = start + jnp.where(j < position, counts[0, j], 0)
    here = start - 2 * position
    after = here + counts[0, position] - 2
    before = here - counts[0, jnp.maximum(position - 1, 0)] + 2
    beyond = after + counts[0, jnp.minimum(position + 1, count - 1)] - 2
    return before, here, after, beyond


def link_code(links, box, face, first_box):
    target = links[0, box, face]
    return jnp.where(target < 0, 0, jnp.where(target - first_box == box, 1, 2))


def swap_depth(cells):
    odd = lane_ids(cells.shape[0]) & 1
    return jnp.where(odd == 1, pltpu.roll(cells, 1, 1), pltpu.roll(cells, LANES - 1, 1))


def end_tiles(fields, row, tile, upper):
    lanes = slice(tile * LANES, (tile + 1) * LANES)
    rows = slice(OWN - 8, OWN) if upper else slice(0, 8)
    return [fields[field, 0, row, rows, lanes] for field in range(3)]


def side_end(fields, row, tile, upper):
    sol, rhs, coef = end_tiles(fields, row, tile, upper)
    towards = 1 if upper else 7
    next_coef = pltpu.roll(coef, towards, 0)
    folded = rhs + 0.5 * (coef + next_coef) * pltpu.roll(sol, towards, 0)
    mixed = jnp.where(odd_lanes(8) == int(not upper), folded, swap_depth(next_coef))
    side = jnp.where(row_ids(8) == (4 if upper else 3), mixed, rhs)
    rows = slice(4, 8) if upper else slice(0, 4)
    return coef[rows], side[rows]


def value_end(fields, row, tile, upper):
    sol, _, _ = end_tiles(fields, row, tile, upper)
    packed = jnp.where(odd_lanes(8) == 1, sol, pltpu.roll(sol, 7, 0))
    return (packed[4:5], packed[6:7]) if upper else (packed[0:1], packed[2:3])


def store_rows(out, base, pieces):
    for piece in pieces:
        out[base : base + piece.shape[0], :] = piece
        base += piece.shape[0]


def load_rows(ref, base, sizes):
    pieces = []
    for size in sizes:
        pieces.append(ref[base : base + size, :])
        base += size
    return tuple(pieces)


SIDE_SIZES, VALUE_SIZES = (4, 4), (1, 1)


def slots(here):
    return (jnp.maximum(-here, 0), 1 - here), jnp.minimum(2 - here, 3)


def near_messages(counts, links, fields, position):
    here = offsets(counts, position)[1]
    held, move_up = slots(here)
    codes = jnp.zeros((8, LANES), jnp.float32)
    for box in range(2):
        for face in range(2, 6):
            mine = (row_ids(8) == box) & (lane_ids(8) == face - 2)
            codes = jnp.where(mine, link_code(links, box, face, 2 * position).astype(jnp.float32), codes)

    mixed = (row_ids(16) + odd_lanes(16)) & 1

    def message(out, upper):
        row = move_up if upper else 0
        for tile in range(TILES):
            lanes = slice(tile * LANES, (tile + 1) * LANES)
            low = fields[0, 0, row, 0:16, lanes]
            high = pltpu.roll(fields[0, 0, row, 16:32, lanes], 15, 0)
            out[VALUE + 16 * tile : VALUE + 16 * tile + 16, :] = jnp.where(mixed == 1, low, high)
            out[OWN * tile : OWN * (tile + 1), :] = fields[2, 0, row, :, lanes]
            out[SIDE + OWN * tile : SIDE + OWN * (tile + 1), :] = fields[1, 0, row, :, lanes]
            for box in range(2):
                store_rows(
                    out, SIDE_ENDS + SIDE_END * (2 * tile + box), side_end(fields, held[box], tile, upper)
                )
                store_rows(
                    out, VALUE_ENDS + VALUE_END * (2 * tile + box), value_end(fields, held[box], tile, upper)
                )
        out[LINKS : LINKS + 8, :] = codes

    return message


def pack_kernel(counts_hbm, links_hbm, fields_hbm, near_a, counts, links, fields, sems):
    copies = []

    def fetch(source, target):
        copies.append(pltpu.make_async_copy(source, target, sems.at[len(copies)]))

    fetch(counts_hbm, counts)
    fetch(links_hbm, links)
    for row in range(fields.shape[2]):
        for field in range(3):
            fetch(fields_hbm.at[field, 0, row], fields.at[field, 0, row])
    for copy in copies:
        copy.start()
    for copy in copies:
        copy.wait()
    position = lax.axis_index("box")
    message = near_messages(counts, links, fields, position)
    even = position % 2 == 0

    @pl.when(even)
    def _():
        message(near_a, True)

    @pl.when(jnp.logical_not(even))
    def _():
        message(near_a, False)


def pack_rest_kernel(counts, links, fields, _, near_b, far_a, far_b):
    position = lax.axis_index("box")
    move_up = slots(offsets(counts, position)[1])[1]
    message = near_messages(counts, links, fields, position)
    even = position % 2 == 0

    @pl.when(even)
    def _():
        message(near_b, False)

    @pl.when(jnp.logical_not(even))
    def _():
        message(near_b, True)

    def far_message(out, upper):
        row = move_up if upper else 0
        for tile in range(TILES):
            store_rows(out, SIDE_END * tile, side_end(fields, row, tile, upper))
            store_rows(out, FAR_VALUES + VALUE_END * tile, value_end(fields, row, tile, upper))

    lower = position % 4 < 2

    @pl.when(lower)
    def _():
        far_message(far_a, True)
        far_message(far_b, False)

    @pl.when(jnp.logical_not(lower))
    def _():
        far_message(far_a, False)
        far_message(far_b, True)


def choose(flag, one, other):
    return tuple(jnp.where(flag, a, b) for a, b in zip(one, other, strict=True))


def crossing(links, face, run_first):
    ids = [links[0, box, face] for box in range(2)]
    linked = [one >= 0 for one in ids]
    swap = jnp.where(linked[0], ids[0] - run_first == 1, linked[1] & (ids[1] - run_first == 0))
    return linked, swap


def neighbour_ends(offset, even, lower, swaps, fields, near, far, tile, start, far_start, sizes, local):
    before, here, after, beyond = offset
    near_a, near_b = near
    far_a, far_b = far
    at = [start + sum(sizes) * (2 * tile + i) for i in range(2)]
    far_at = far_start + sum(sizes) * tile
    below = [choose(even, load_rows(near_b, at[i], sizes), load_rows(near_a, at[i], sizes)) for i in range(2)]
    above = [choose(even, load_rows(near_a, at[i], sizes), load_rows(near_b, at[i], sizes)) for i in range(2)]
    far_below = choose(lower, load_rows(far_b, far_at, sizes), load_rows(far_a, far_at, sizes))
    far_above = choose(lower, load_rows(far_a, far_at, sizes), load_rows(far_b, far_at, sizes))
    below = (choose(before == 1, far_below, below[0]), choose(here == -1, local(fields, 0, tile, True), below[1]))
    above = (
        choose(after == 1, local(fields, jnp.minimum(2 - here, 3), tile, False), above[0]),
        choose(beyond == -1, far_above, above[1]),
    )
    return [
        (choose(swaps[0], below[1 - box], below[box]), choose(swaps[1], above[1 - box], above[box]))
        for box in range(2)
    ]


def place_own(here, after, even, place_local, place_moved, near):
    from_below = here == 1
    from_above = after == -1
    held = slots(here)[0]
    for box, moved, first, second in ((0, from_below, near[1], near[0]), (1, from_above, near[0], near[1])):

        @pl.when(jnp.logical_not(moved))
        def _(box=box):
            place_local(box, held[box])

        @pl.when(moved & even)
        def _(box=box, ref=first):
            place_moved(box, ref)

        @pl.when(moved & jnp.logical_not(even))
        def _(box=box, ref=second):
            place_moved(box, ref)


def split_colours(raw, box, tile):
    odd = odd_lanes(PAIRS)
    low = raw[box, tile, pl.ds(0, PAIRS, 2), :]
    high = raw[box, tile, pl.ds(1, PAIRS, 2), :]
    return jnp.where(odd == 1, high, low), jnp.where(odd == 1, low, high)


def store_column(out, box, tile, cells):
    out[box, tile, FIRST : FIRST + PAIRS, :] = cells
    out[box, tile, FIRST - 1 : FIRST, :] = cells[PAIRS - 1 : PAIRS]
    out[box, tile, FIRST + PAIRS : FIRST + PAIRS + 1, :] = cells[0:1]


def block_rows(block, by=0):
    return slice(FIRST + 8 * block + by, FIRST + 8 * block + 8 + by)


def around(ref, colour, blocks, code, use):
    lane = lane_ids(8)
    depth = lane & 31
    low_layer = odd_lanes(8) == colour
    cells, up, down, turned = {}, {}, {}, {}

    def load(block, tile):
        for box in range(2):
            at = block, box, tile
            cells[at] = ref[box, tile, block_rows(block), :]
            up[at] = pltpu.roll(cells[at], 32, 1)
            down[at] = pltpu.roll(cells[at], 96, 1)

    def turn(block, tile):
        for box in range(2):
            at, there = (block, box, tile), (block, 1 - box, tile)
            z_low = jnp.where(code(block, box, 2) == 2, down[there], down[at])
            z_high = jnp.where(code(block, box, 3) == 2, up[there], up[at])
            turned[at] = (
                pltpu.roll(jnp.where(depth == 31, z_low, cells[at]), 1, 1),
                pltpu.roll(jnp.where(depth == 0, z_high, cells[at]), LANES - 1, 1),
            )

    def finish(block, tile):
        for box in range(2):
            at = block, box, tile
            y_low, y_high = up[block, box, (tile - 1) % TILES], down[block, box, (tile + 1) % TILES]
            if tile == 0:
                y_low = jnp.where(code(block, box, 0) == 2, up[block, 1 - box, TILES - 1], y_low)
            if tile == TILES - 1:
                y_high = jnp.where(code(block, box, 1) == 2, down[block, 1 - box, 0], y_high)
            across = jnp.where(
                low_layer, ref[box, tile, block_rows(block, -1), :], ref[box, tile, block_rows(block, 1), :]
            )
            use(
                block,
                box,
                tile,
                (
                    across,
                    cells[at],
                    jnp.where(lane >= 32, up[at], y_low),
                    jnp.where(lane < 96, down[at], y_high),
                    *turned[at],
                ),
            )

    loads = [(block, (tile - 1) % TILES) for block in range(blocks) for tile in range(TILES)]
    steps = [(block, tile) for block in range(blocks) for tile in range(TILES)]
    for k in range(len(steps) + LOAD_AHEAD):
        if k < len(loads):
            load(*loads[k])
        if 0 <= k - LOAD_AHEAD + TURN_AHEAD < len(steps):
            turn(*steps[k - LOAD_AHEAD + TURN_AHEAD])
        if k >= LOAD_AHEAD:
            finish(*steps[k - LOAD_AHEAD])


def smooth_kernel(
    counts,
    links,
    parents,
    fields,
    near_a,
    near_b,
    far_a,
    far_b,
    red_out,
    black_out,
    red_left,
    black_left,
    coarse,
    raw_coef,
    raw_side,
    raw_value,
    red_coef,
    black_coef,
    red,
    black,
    weight,
    source,
    diagonal,
    halo_code,
    sums,
):
    value, coef = (red, black), (red_coef, black_coef)
    position = lax.axis_index("box")
    offset = offsets(counts, position)
    _, here, after, _ = offset
    first_box = 2 * position
    even = position % 2 == 0
    lower = position % 4 < 2
    near, far = (near_a, near_b), (far_a, far_b)

    def place_local(box, row):
        for tile in range(TILES):
            lanes = slice(tile * LANES, (tile + 1) * LANES)
            raw_value[box, tile, 0:OWN, :] = fields[0, 0, row, :, lanes]
            raw_side[box, tile, 0:OWN, :] = fields[1, 0, row, :, lanes]
            raw_coef[box, tile, 0:OWN, :] = fields[2, 0, row, :, lanes]

    def place_moved(box, ref):
        for tile in range(TILES):
            packed = ref[VALUE + 16 * tile : VALUE + 16 * tile + 16, :]
            raw_value[box, tile, 0:16, :] = packed
            raw_value[box, tile, 16:32, :] = pltpu.roll(packed, 1, 0)
            raw_side[box, tile, 0:OWN, :] = ref[SIDE + OWN * tile : SIDE + OWN * (tile + 1), :]
            raw_coef[box, tile, 0:OWN, :] = ref[OWN * tile : OWN * (tile + 1), :]

    place_own(here, after, even, place_local, place_moved, near)
    low_linked, low_swap = crossing(links, 0, first_box - 2)
    high_linked, high_swap = crossing(links, 1, first_box + 2)
    swaps = (low_swap, high_swap)
    ones = jnp.ones((16, LANES), jnp.float32)
    zeros = jnp.zeros((16, LANES), jnp.float32)
    odd = odd_lanes(1)
    for tile in range(TILES):
        sides = neighbour_ends(
            offset, even, lower, swaps, fields, near, far, tile, SIDE_ENDS, 0, SIDE_SIZES, side_end
        )
        values = neighbour_ends(
            offset, even, lower, swaps, fields, near, far, tile, VALUE_ENDS, FAR_VALUES, VALUE_SIZES, value_end
        )
        for box in range(2):
            (below, side_below), (above, side_above) = sides[box]
            raw_coef[box, tile, 32:48, :] = ones
            raw_side[box, tile, 32:48, :] = ones
            raw_value[box, tile, 32:48, :] = zeros
            raw_coef[box, tile, 43:44, :] = jnp.where(odd == 0, swap_depth(side_below[0:1]), below[0:1])
            raw_coef[box, tile, 44:48, :] = below
            raw_side[box, tile, 44:48, :] = side_below
            raw_coef[box, tile, 32:36, :] = above
            raw_coef[box, tile, 36:37, :] = jnp.where(odd == 1, swap_depth(side_above[3:4]), above[3:4])
            raw_side[box, tile, 32:36, :] = side_above
            for base, pieces in zip((44, 32), values[box], strict=True):
                for k in range(4):
                    raw_value[box, tile, base + k : base + k + 1, :] = pieces[k // 2]

    own_code = [[link_code(links, box, face, first_box) for face in range(2, 6)] for box in range(2)]
    tile_a, tile_b = near_a[LINKS : LINKS + 8, :], near_b[LINKS : LINKS + 8, :]
    codes_below, codes_above = jnp.where(even, tile_b, tile_a), jnp.where(even, tile_a, tile_b)
    for face in range(4):
        spread = [
            [jnp.broadcast_to(one[i : i + 1, face : face + 1], (8, LANES)) for i in range(2)]
            for one in (codes_below, codes_above)
        ]
        for box in range(2):
            below = jnp.where(low_swap, spread[0][1 - box], spread[0][box])
            above = jnp.where(high_swap, spread[1][1 - box], spread[1][box])
            halo_code[box, face] = jnp.where(row_ids(8) < 4, above, below)

    def code(block, box, face):
        return own_code[box][face] if block < 2 else halo_code[box, face]

    for box in range(2):
        for tile in range(TILES):
            for raw, out in ((raw_value, value), (raw_coef, coef)):
                for colour, cells in enumerate(split_colours(raw, box, tile)):
                    store_column(out[colour], box, tile, cells)
            source[0, box, tile], source[1, box, tile] = split_colours(raw_side, box, tile)

    lane = lane_ids(8)
    depth = lane & 31
    row = row_ids(8)

    def weigh(colour):
        low_layer = odd_lanes(8) == colour

        def use(block, box, tile, near_coef):
            rows = slice(8 * block, 8 * block + 8)
            cut_low = jnp.logical_not(low_linked[box])
            cut_high = jnp.logical_not(high_linked[box])
            first_row, last_row = (row == 0) & low_layer, (row == 7) & jnp.logical_not(low_layer)
            end = (
                first_row & cut_low,
                last_row & cut_high,
                (first_row & cut_high) | (last_row & cut_low),
            )[block]
            lost = (
                end,
                None,
                (lane < 32) & (code(block, box, 0) == 0) if tile == 0 else None,
                (lane >= 96) & (code(block, box, 1) == 0) if tile == TILES - 1 else None,
                (depth == 0) & (code(block, box, 2) == 0),
                (depth == 31) & (code(block, box, 3) == 0),
            )
            own = coef[colour][box, tile, block_rows(block), :]
            total = jnp.full((8, LANES), MASS_TERM, jnp.float32)
            kept = []
            for one, gone in zip(near_coef, lost, strict=True):
                if gone is None:
                    w = 0.5 * (own + one)
                    kept.append(w)
                else:
                    w = 0.5 * (own + jnp.where(gone, own, one))
                    kept.append(jnp.where(gone, 0.0, w))
                total = total + w
            inverse = 1.0 / total
            diagonal[colour, box, tile, rows, :] = total
            source[colour, box, tile, rows, :] = source[colour, box, tile, rows, :] * inverse
            for d in range(6):
                weight[colour, d, box, tile, rows, :] = kept[d] * inverse

        around(coef[1 - colour], colour, 3, code, use)

    weigh(0)
    weigh(1)

    def update(colour, blocks, take):
        def use(block, box, tile, near_value):
            rows = slice(8 * block, 8 * block + 8)
            terms = [weight[colour, d, box, tile, rows, :] * one for d, one in enumerate(near_value)]
            total = (terms[0] + terms[1]) + (terms[2] + terms[3]) + (terms[4] + terms[5])
            take(block, box, tile, rows, source[colour, box, tile, rows, :] + total)

        around(value[1 - colour], colour, blocks, code, use)

    def sweep(step, carry):
        for colour in range(2):

            def take(block, box, tile, rows, fresh, out=value[colour]):
                out[box, tile, block_rows(block), :] = fresh
                if block == 0:
                    out[box, tile, FIRST + PAIRS : FIRST + PAIRS + 1, :] = fresh[0:1]
                if block == 2:
                    out[box, tile, FIRST - 1 : FIRST, :] = fresh[7:8]

            update(colour, 3, take)
        return carry

    lax.fori_loop(0, 2, sweep, 0)

    halves = TILES // 2
    for colour, out, left in ((0, red_out, red_left), (1, black_out, black_left)):

        def take(block, box, tile, rows, fresh, colour=colour, out=out, left=left):
            kept = value[colour][box, tile, block_rows(block), :]
            rest = diagonal[colour, box, tile, rows, :] * (fresh - kept)
            out[box, tile, rows, :] = kept
            left[box, tile, rows, :] = rest
            if colour == 1:
                at = 32 * (tile // halves) + 16 * box + 8 * block
                lanes = slice(tile % halves * LANES, (tile % halves + 1) * LANES)
                sums[at : at + 8, lanes] = red_left[box, tile, rows, :] + rest

        update(colour, 2, take)
    whole = sums[...]
    first = whole.astype(jnp.bfloat16)
    rest = whole - first.astype(jnp.float32)
    second = rest.astype(jnp.bfloat16)
    third = (rest - second.astype(jnp.float32)).astype(jnp.bfloat16)
    width = halves * LANES
    cell = lax.broadcasted_iota(jnp.int32, (width, LANES), 0)
    block = lax.broadcasted_iota(jnp.int32, (width, LANES), 1)
    merge = jnp.where((cell >> 6) * 16 + ((cell & 31) >> 1) == block, 1.0, 0.0).astype(jnp.bfloat16)
    split = jnp.dot(
        jnp.concatenate([first, second, third], axis=0), merge, preferred_element_type=jnp.float32
    )
    mean = (split[:64] + split[64:128] + split[128:]) * 0.125
    for half in range(2):
        coarse[0:32, half * LANES : (half + 1) * LANES] = mean[32 * half : 32 * half + 32]
    for box in range(2):
        label = parents[0, box, 0] * 16 + parents[0, box, 1] * 8 + parents[0, box, 2]
        coarse[32 + 4 * box : 36 + 4 * box, :] = jnp.full((4, 2 * LANES), label.astype(jnp.float32))


def unpack_kernel(red, black, red_left, black_left, smoothed, residual, stage):
    boxes, tiles = red.shape[:2]
    odd = odd_lanes(red.shape[2])
    for k, one, two, out in ((0, red, black, smoothed), (1, red_left, black_left, residual)):
        for box in range(boxes):
            for tile in range(tiles):
                low, high = one[box, tile], two[box, tile]
                stage[k, box, tile, pl.ds(0, 16, 2), :] = jnp.where(odd == 1, high, low)
                stage[k, box, tile, pl.ds(1, 16, 2), :] = jnp.where(odd == 1, low, high)
                out[0, box, :, tile * LANES : (tile + 1) * LANES] = stage[k, box, tile]


def place_kernel(*refs):
    *got, source, out = refs
    group = lax.axis_index("grp")
    base = (group * 16).astype(jnp.float32)
    marks = [
        [jnp.broadcast_to(one[32 + 4 * box : 33 + 4 * box, :], (16, one.shape[1])) for box in range(2)] for one in got
    ]
    for octant in range(16):
        kept = source[0, octant // 8, octant % 8]
        for sender, labels in zip(got, marks, strict=True):
            for box in range(2):
                mine = labels[box] == base + float(octant)
                kept = jnp.where(mine, sender[16 * box : 16 * box + 16, :], kept)
        out[0, octant // 8, octant % 8] = kept


def per_device(old_fields, old_count, neighbours, parents, coarse_source):
    f32 = jnp.float32
    curve = lax.axis_size("box")
    box_edge, plane_cells = old_fields.shape[3:]
    boxes = neighbours.shape[1]
    params = pltpu.CompilerParams(vmem_limit_bytes=40 << 20)

    def cost(flops, size):
        return pl.CostEstimate(flops=flops, bytes_accessed=size, transcendentals=0)

    def rows(count):
        return jax.ShapeDtypeStruct((count, LANES), f32)

    def swap(message, distance, shift):
        ids = [i for i in range(curve - distance) if (i - shift) % (2 * distance) < distance]
        both = [(i, i + distance) for i in ids] + [(i + distance, i) for i in ids]
        return lax.ppermute(message, "box", both)

    near_a = pl.pallas_call(
        pack_kernel,
        out_shape=rows(NEAR_ROWS),
        in_specs=[HBM] * 3,
        out_specs=VMEM,
        scratch_shapes=[
            pltpu.SMEM(old_count.shape, old_count.dtype),
            pltpu.SMEM(neighbours.shape, neighbours.dtype),
            pltpu.VMEM(old_fields.shape, f32),
            pltpu.SemaphoreType.DMA((2 + 3 * old_fields.shape[2],)),
        ],
        compiler_params=params,
        cost_estimate=cost(10**6, 2 << 20),
        name="pack",
    )(*[pltpu.with_memory_space_constraint(x, pltpu.HBM) for x in (old_count, neighbours, old_fields)])
    near_b, far_a, far_b = pl.pallas_call(
        pack_rest_kernel,
        out_shape=(rows(NEAR_ROWS), rows(FAR_ROWS), rows(FAR_ROWS)),
        in_specs=[SMEM, SMEM, VMEM, pl.BlockSpec(memory_space=pl.ANY)],
        out_specs=(VMEM,) * 3,
        compiler_params=params,
        cost_estimate=cost(10**6, 2 << 20),
        name="pack_rest",
    )(old_count, neighbours, old_fields, near_a)
    moved = [swap(near_a, 1, 0), swap(near_b, 1, 1), swap(far_a, 2, 0), swap(far_b, 2, 2)]
    packed = pltpu.VMEM((2, boxes, TILES, PAIRS, LANES), f32)
    column = pltpu.VMEM((boxes, TILES, PAIRS + 2 * FIRST, LANES), f32)
    raw = pltpu.VMEM((boxes, TILES, ROWS, LANES), f32)
    weight = pltpu.VMEM((2, 6, boxes, TILES, PAIRS, LANES), f32)
    code = pltpu.VMEM((boxes, 4, 8, LANES), f32)
    sums = pltpu.VMEM((32 * boxes, TILES // 2 * LANES), f32)
    fine = jax.ShapeDtypeStruct((1, boxes, box_edge, plane_cells), f32)
    half = jax.ShapeDtypeStruct((boxes, TILES, box_edge // 2, LANES), f32)
    *halves, coarse = pl.pallas_call(
        smooth_kernel,
        out_shape=(half, half, half, half, jax.ShapeDtypeStruct((40, 2 * LANES), f32)),
        in_specs=[SMEM, SMEM, SMEM] + [VMEM] * 5,
        out_specs=(VMEM,) * 5,
        scratch_shapes=[raw] * 3 + [column] * 4 + [weight, packed, packed, code, sums],
        compiler_params=params,
        cost_estimate=cost(10**7, 6 << 20),
        name="smooth",
    )(old_count, neighbours, parents, old_fields, *moved)
    groups = lax.axis_size("grp")
    got = [coarse] + [
        lax.ppermute(coarse, "grp", [(i, (i + k) % groups) for i in range(groups)])
        for k in range(1, groups)
    ]
    smoothed, residual = pl.pallas_call(
        unpack_kernel,
        out_shape=(fine, fine),
        in_specs=[VMEM] * 4,
        out_specs=(VMEM,) * 2,
        scratch_shapes=[pltpu.VMEM((2, boxes, TILES, OWN, LANES), f32)],
        compiler_params=params,
        cost_estimate=pl.CostEstimate(flops=10**6, bytes_accessed=3 << 20, transcendentals=0),
        name="unpack",
    )(*halves)
    coarse_rhs = pl.pallas_call(
        place_kernel,
        out_shape=jax.ShapeDtypeStruct(coarse_source.shape, f32),
        in_specs=[VMEM] * (len(got) + 1),
        out_specs=VMEM,
        compiler_params=params,
        cost_estimate=pl.CostEstimate(flops=10**6, bytes_accessed=1 << 20, transcendentals=0),
        name="place",
    )(*got, coarse_source)
    return smoothed, residual, coarse_rhs


def solution(mesh):
    in_specs = (
        P(None, "grp", "box", None, None),
        P("grp", None),
        P("grp", "box", None),
        P("grp", "box", None),
        P("grp", "box", None, None, None),
    )
    out_specs = (
        P("grp", "box", None, None),
        P("grp", "box", None, None),
        P("grp", "box", None, None, None),
    )
    return jax.shard_map(
        per_device, mesh=mesh, in_specs=in_specs, out_specs=out_specs, check_vma=False
    )
```

```python
import jax
import jax.numpy as jnp
from jax import lax
from jax.experimental import pallas as pl
from jax.experimental.pallas import tpu as pltpu
from jax.sharding import PartitionSpec as P

MASS_TERM = 0.25
LANES = 128
OWN, ROWS, PAIRS, FIRST = 32, 48, 24, 8
LOAD_AHEAD, TURN_AHEAD = 20, 4
TILES = 8
SIDE_END, VALUE_END = 8, 2
SIDE = OWN * TILES
SIDE_ENDS = SIDE + OWN * TILES
LINKS = SIDE_ENDS + 2 * SIDE_END * TILES
VALUE = LINKS + 8
VALUE_ENDS = VALUE + OWN // 2 * TILES
NEAR_ROWS = VALUE_ENDS + 2 * VALUE_END * TILES
FAR_VALUES = SIDE_END * TILES
FAR_ROWS = FAR_VALUES + VALUE_END * TILES

VMEM = pl.BlockSpec(memory_space=pltpu.VMEM)
SMEM = pl.BlockSpec(memory_space=pltpu.SMEM)
HBM = pl.BlockSpec(memory_space=pltpu.HBM)


def lane_ids(rows):
    return lax.broadcasted_iota(jnp.int32, (rows, LANES), 1)


def row_ids(rows):
    return lax.broadcasted_iota(jnp.int32, (rows, LANES), 0)


def odd_lanes(rows):
    lane = lane_ids(rows)
    return ((lane >> 5) + lane) & 1


def offsets(counts, position):
    count = counts.shape[1]
    start = jnp.int32(0)
    for j in range(count):
        start = start + jnp.where(j < position, counts[0, j], 0)
    here = start - 2 * position
    after = here + counts[0, position] - 2
    before = here - counts[0, jnp.maximum(position - 1, 0)] + 2
    beyond = after + counts[0, jnp.minimum(position + 1, count - 1)] - 2
    return before, here, after, beyond


def link_code(links, box, face, first_box):
    target = links[0, box, face]
    return jnp.where(target < 0, 0, jnp.where(target - first_box == box, 1, 2))


def swap_depth(cells):
    odd = lane_ids(cells.shape[0]) & 1
    return jnp.where(odd == 1, pltpu.roll(cells, 1, 1), pltpu.roll(cells, LANES - 1, 1))


def end_tiles(fields, row, tile, upper):
    lanes = slice(tile * LANES, (tile + 1) * LANES)
    rows = slice(OWN - 8, OWN) if upper else slice(0, 8)
    return [fields[field, 0, row, rows, lanes] for field in range(3)]


def side_end(fields, row, tile, upper):
    sol, rhs, coef = end_tiles(fields, row, tile, upper)
    towards = 1 if upper else 7
    next_coef = pltpu.roll(coef, towards, 0)
    folded = rhs + 0.5 * (coef + next_coef) * pltpu.roll(sol, towards, 0)
    mixed = jnp.where(odd_lanes(8) == int(not upper), folded, swap_depth(next_coef))
    side = jnp.where(row_ids(8) == (4 if upper else 3), mixed, rhs)
    rows = slice(4, 8) if upper else slice(0, 4)
    return coef[rows], side[rows]


def value_end(fields, row, tile, upper):
    sol, _, _ = end_tiles(fields, row, tile, upper)
    packed = jnp.where(odd_lanes(8) == 1, sol, pltpu.roll(sol, 7, 0))
    return (packed[4:5], packed[6:7]) if upper else (packed[0:1], packed[2:3])


def store_rows(out, base, pieces):
    for piece in pieces:
        out[base : base + piece.shape[0], :] = piece
        base += piece.shape[0]


def load_rows(ref, base, sizes):
    pieces = []
    for size in sizes:
        pieces.append(ref[base : base + size, :])
        base += size
    return tuple(pieces)


SIDE_SIZES, VALUE_SIZES = (4, 4), (1, 1)


def slots(here):
    return (jnp.maximum(-here, 0), 1 - here), jnp.minimum(2 - here, 3)


def pack_kernel(counts_hbm, links_hbm, fields_hbm, near_a, near_b, counts, links, fields, sems):
    copies = []

    def fetch(source, target):
        copies.append(pltpu.make_async_copy(source, target, sems.at[len(copies)]))

    fetch(counts_hbm, counts)
    fetch(links_hbm, links)
    for row in range(fields.shape[2]):
        for field in range(3):
            fetch(fields_hbm.at[field, 0, row], fields.at[field, 0, row])
    for copy in copies:
        copy.start()
    for copy in copies:
        copy.wait()
    position = lax.axis_index("box")
    here = offsets(counts, position)[1]
    held, move_up = slots(here)
    codes = jnp.zeros((8, LANES), jnp.float32)
    for box in range(2):
        for face in range(2, 6):
            mine = (row_ids(8) == box) & (lane_ids(8) == face - 2)
            codes = jnp.where(mine, link_code(links, box, face, 2 * position).astype(jnp.float32), codes)

    mixed = (row_ids(16) + odd_lanes(16)) & 1

    def message(out, upper):
        row = move_up if upper else 0
        for tile in range(TILES):
            lanes = slice(tile * LANES, (tile + 1) * LANES)
            low = fields[0, 0, row, 0:16, lanes]
            high = pltpu.roll(fields[0, 0, row, 16:32, lanes], 15, 0)
            out[VALUE + 16 * tile : VALUE + 16 * tile + 16, :] = jnp.where(mixed == 1, low, high)
            out[OWN * tile : OWN * (tile + 1), :] = fields[2, 0, row, :, lanes]
            out[SIDE + OWN * tile : SIDE + OWN * (tile + 1), :] = fields[1, 0, row, :, lanes]
            for box in range(2):
                store_rows(
                    out, SIDE_ENDS + SIDE_END * (2 * tile + box), side_end(fields, held[box], tile, upper)
                )
                store_rows(
                    out, VALUE_ENDS + VALUE_END * (2 * tile + box), value_end(fields, held[box], tile, upper)
                )
        out[LINKS : LINKS + 8, :] = codes

    even = position % 2 == 0

    @pl.when(even)
    def _():
        message(near_a, True)
        message(near_b, False)

    @pl.when(jnp.logical_not(even))
    def _():
        message(near_a, False)
        message(near_b, True)


def pack_far_kernel(counts, fields, _, far_a, far_b):
    position = lax.axis_index("box")
    move_up = slots(offsets(counts, position)[1])[1]

    def far_message(out, upper):
        row = move_up if upper else 0
        for tile in range(TILES):
            store_rows(out, SIDE_END * tile, side_end(fields, row, tile, upper))
            store_rows(out, FAR_VALUES + VALUE_END * tile, value_end(fields, row, tile, upper))

    lower = position % 4 < 2

    @pl.when(lower)
    def _():
        far_message(far_a, True)
        far_message(far_b, False)

    @pl.when(jnp.logical_not(lower))
    def _():
        far_message(far_a, False)
        far_message(far_b, True)


def choose(flag, one, other):
    return tuple(jnp.where(flag, a, b) for a, b in zip(one, other, strict=True))


def crossing(links, face, run_first):
    ids = [links[0, box, face] for box in range(2)]
    linked = [one >= 0 for one in ids]
    swap = jnp.where(linked[0], ids[0] - run_first == 1, linked[1] & (ids[1] - run_first == 0))
    return linked, swap


def neighbour_ends(offset, even, lower, swaps, fields, near, far, tile, start, far_start, sizes, local):
    before, here, after, beyond = offset
    near_a, near_b = near
    far_a, far_b = far
    at = [start + sum(sizes) * (2 * tile + i) for i in range(2)]
    far_at = far_start + sum(sizes) * tile
    below = [choose(even, load_rows(near_b, at[i], sizes), load_rows(near_a, at[i], sizes)) for i in range(2)]
    above = [choose(even, load_rows(near_a, at[i], sizes), load_rows(near_b, at[i], sizes)) for i in range(2)]
    far_below = choose(lower, load_rows(far_b, far_at, sizes), load_rows(far_a, far_at, sizes))
    far_above = choose(lower, load_rows(far_a, far_at, sizes), load_rows(far_b, far_at, sizes))
    below = (choose(before == 1, far_below, below[0]), choose(here == -1, local(fields, 0, tile, True), below[1]))
    above = (
        choose(after == 1, local(fields, jnp.minimum(2 - here, 3), tile, False), above[0]),
        choose(beyond == -1, far_above, above[1]),
    )
    return [
        (choose(swaps[0], below[1 - box], below[box]), choose(swaps[1], above[1 - box], above[box]))
        for box in range(2)
    ]


def place_own(here, after, even, place_local, place_moved, near):
    from_below = here == 1
    from_above = after == -1
    held = slots(here)[0]
    for box, moved, first, second in ((0, from_below, near[1], near[0]), (1, from_above, near[0], near[1])):

        @pl.when(jnp.logical_not(moved))
        def _(box=box):
            place_local(box, held[box])

        @pl.when(moved & even)
        def _(box=box, ref=first):
            place_moved(box, ref)

        @pl.when(moved & jnp.logical_not(even))
        def _(box=box, ref=second):
            place_moved(box, ref)


def split_colours(raw, box, tile):
    odd = odd_lanes(PAIRS)
    low = raw[box, tile, pl.ds(0, PAIRS, 2), :]
    high = raw[box, tile, pl.ds(1, PAIRS, 2), :]
    return jnp.where(odd == 1, high, low), jnp.where(odd == 1, low, high)


def store_column(out, box, tile, cells):
    out[box, tile, FIRST : FIRST + PAIRS, :] = cells
    out[box, tile, FIRST - 1 : FIRST, :] = cells[PAIRS - 1 : PAIRS]
    out[box, tile, FIRST + PAIRS : FIRST + PAIRS + 1, :] = cells[0:1]


def block_rows(block, by=0):
    return slice(FIRST + 8 * block + by, FIRST + 8 * block + 8 + by)


def around(ref, colour, blocks, code, use):
    lane = lane_ids(8)
    depth = lane & 31
    low_layer = odd_lanes(8) == colour
    cells, up, down, turned = {}, {}, {}, {}

    def load(block, tile):
        for box in range(2):
            at = block, box, tile
            cells[at] = ref[box, tile, block_rows(block), :]
            up[at] = pltpu.roll(cells[at], 32, 1)
            down[at] = pltpu.roll(cells[at], 96, 1)

    def turn(block, tile):
        for box in range(2):
            at, there = (block, box, tile), (block, 1 - box, tile)
            z_low = jnp.where(code(block, box, 2) == 2, down[there], down[at])
            z_high = jnp.where(code(block, box, 3) == 2, up[there], up[at])
            turned[at] = (
                pltpu.roll(jnp.where(depth == 31, z_low, cells[at]), 1, 1),
                pltpu.roll(jnp.where(depth == 0, z_high, cells[at]), LANES - 1, 1),
            )

    def finish(block, tile):
        for box in range(2):
            at = block, box, tile
            y_low, y_high = up[block, box, (tile - 1) % TILES], down[block, box, (tile + 1) % TILES]
            if tile == 0:
                y_low = jnp.where(code(block, box, 0) == 2, up[block, 1 - box, TILES - 1], y_low)
            if tile == TILES - 1:
                y_high = jnp.where(code(block, box, 1) == 2, down[block, 1 - box, 0], y_high)
            across = jnp.where(
                low_layer, ref[box, tile, block_rows(block, -1), :], ref[box, tile, block_rows(block, 1), :]
            )
            use(
                block,
                box,
                tile,
                (
                    across,
                    cells[at],
                    jnp.where(lane >= 32, up[at], y_low),
                    jnp.where(lane < 96, down[at], y_high),
                    *turned[at],
                ),
            )

    loads = [(block, (tile - 1) % TILES) for block in range(blocks) for tile in range(TILES)]
    steps = [(block, tile) for block in range(blocks) for tile in range(TILES)]
    for k in range(len(steps) + LOAD_AHEAD):
        if k < len(loads):
            load(*loads[k])
        if 0 <= k - LOAD_AHEAD + TURN_AHEAD < len(steps):
            turn(*steps[k - LOAD_AHEAD + TURN_AHEAD])
        if k >= LOAD_AHEAD:
            finish(*steps[k - LOAD_AHEAD])


def smooth_kernel(
    counts,
    links,
    parents,
    fields,
    near_a,
    near_b,
    far_a,
    far_b,
    red_out,
    black_out,
    red_left,
    black_left,
    coarse,
    raw_coef,
    raw_side,
    raw_value,
    red_coef,
    black_coef,
    red,
    black,
    weight,
    source,
    diagonal,
    halo_code,
    sums,
):
    value, coef = (red, black), (red_coef, black_coef)
    position = lax.axis_index("box")
    offset = offsets(counts, position)
    _, here, after, _ = offset
    first_box = 2 * position
    even = position % 2 == 0
    lower = position % 4 < 2
    near, far = (near_a, near_b), (far_a, far_b)

    def place_local(box, row):
        for tile in range(TILES):
            lanes = slice(tile * LANES, (tile + 1) * LANES)
            raw_value[box, tile, 0:OWN, :] = fields[0, 0, row, :, lanes]
            raw_side[box, tile, 0:OWN, :] = fields[1, 0, row, :, lanes]
            raw_coef[box, tile, 0:OWN, :] = fields[2, 0, row, :, lanes]

    def place_moved(box, ref):
        for tile in range(TILES):
            packed = ref[VALUE + 16 * tile : VALUE + 16 * tile + 16, :]
            raw_value[box, tile, 0:16, :] = packed
            raw_value[box, tile, 16:32, :] = pltpu.roll(packed, 1, 0)
            raw_side[box, tile, 0:OWN, :] = ref[SIDE + OWN * tile : SIDE + OWN * (tile + 1), :]
            raw_coef[box, tile, 0:OWN, :] = ref[OWN * tile : OWN * (tile + 1), :]

    place_own(here, after, even, place_local, place_moved, near)
    low_linked, low_swap = crossing(links, 0, first_box - 2)
    high_linked, high_swap = crossing(links, 1, first_box + 2)
    swaps = (low_swap, high_swap)
    ones = jnp.ones((16, LANES), jnp.float32)
    zeros = jnp.zeros((16, LANES), jnp.float32)
    odd = odd_lanes(1)
    for tile in range(TILES):
        sides = neighbour_ends(
            offset, even, lower, swaps, fields, near, far, tile, SIDE_ENDS, 0, SIDE_SIZES, side_end
        )
        values = neighbour_ends(
            offset, even, lower, swaps, fields, near, far, tile, VALUE_ENDS, FAR_VALUES, VALUE_SIZES, value_end
        )
        for box in range(2):
            (below, side_below), (above, side_above) = sides[box]
            raw_coef[box, tile, 32:48, :] = ones
            raw_side[box, tile, 32:48, :] = ones
            raw_value[box, tile, 32:48, :] = zeros
            raw_coef[box, tile, 43:44, :] = jnp.where(odd == 0, swap_depth(side_below[0:1]), below[0:1])
            raw_coef[box, tile, 44:48, :] = below
            raw_side[box, tile, 44:48, :] = side_below
            raw_coef[box, tile, 32:36, :] = above
            raw_coef[box, tile, 36:37, :] = jnp.where(odd == 1, swap_depth(side_above[3:4]), above[3:4])
            raw_side[box, tile, 32:36, :] = side_above
            for base, pieces in zip((44, 32), values[box], strict=True):
                for k in range(4):
                    raw_value[box, tile, base + k : base + k + 1, :] = pieces[k // 2]

    own_code = [[link_code(links, box, face, first_box) for face in range(2, 6)] for box in range(2)]
    tile_a, tile_b = near_a[LINKS : LINKS + 8, :], near_b[LINKS : LINKS + 8, :]
    codes_below, codes_above = jnp.where(even, tile_b, tile_a), jnp.where(even, tile_a, tile_b)
    for face in range(4):
        spread = [
            [jnp.broadcast_to(one[i : i + 1, face : face + 1], (8, LANES)) for i in range(2)]
            for one in (codes_below, codes_above)
        ]
        for box in range(2):
            below = jnp.where(low_swap, spread[0][1 - box], spread[0][box])
            above = jnp.where(high_swap, spread[1][1 - box], spread[1][box])
            halo_code[box, face] = jnp.where(row_ids(8) < 4, above, below)

    def code(block, box, face):
        return own_code[box][face] if block < 2 else halo_code[box, face]

    for box in range(2):
        for tile in range(TILES):
            for raw, out in ((raw_value, value), (raw_coef, coef)):
                for colour, cells in enumerate(split_colours(raw, box, tile)):
                    store_column(out[colour], box, tile, cells)
            source[0, box, tile], source[1, box, tile] = split_colours(raw_side, box, tile)

    lane = lane_ids(8)
    depth = lane & 31
    row = row_ids(8)

    def weigh(colour):
        low_layer = odd_lanes(8) == colour

        def use(block, box, tile, near_coef):
            rows = slice(8 * block, 8 * block + 8)
            cut_low = jnp.logical_not(low_linked[box])
            cut_high = jnp.logical_not(high_linked[box])
            first_row, last_row = (row == 0) & low_layer, (row == 7) & jnp.logical_not(low_layer)
            end = (
                first_row & cut_low,
                last_row & cut_high,
                (first_row & cut_high) | (last_row & cut_low),
            )[block]
            lost = (
                end,
                None,
                (lane < 32) & (code(block, box, 0) == 0) if tile == 0 else None,
                (lane >= 96) & (code(block, box, 1) == 0) if tile == TILES - 1 else None,
                (depth == 0) & (code(block, box, 2) == 0),
                (depth == 31) & (code(block, box, 3) == 0),
            )
            own = coef[colour][box, tile, block_rows(block), :]
            total = jnp.full((8, LANES), MASS_TERM, jnp.float32)
            kept = []
            for one, gone in zip(near_coef, lost, strict=True):
                if gone is None:
                    w = 0.5 * (own + one)
                    kept.append(w)
                else:
                    w = 0.5 * (own + jnp.where(gone, own, one))
                    kept.append(jnp.where(gone, 0.0, w))
                total = total + w
            inverse = 1.0 / total
            diagonal[colour, box, tile, rows, :] = total
            source[colour, box, tile, rows, :] = source[colour, box, tile, rows, :] * inverse
            for d in range(6):
                weight[colour, d, box, tile, rows, :] = kept[d] * inverse

        around(coef[1 - colour], colour, 3, code, use)

    weigh(0)
    weigh(1)

    def update(colour, blocks, take):
        def use(block, box, tile, near_value):
            rows = slice(8 * block, 8 * block + 8)
            terms = [weight[colour, d, box, tile, rows, :] * one for d, one in enumerate(near_value)]
            total = (terms[0] + terms[1]) + (terms[2] + terms[3]) + (terms[4] + terms[5])
            take(block, box, tile, rows, source[colour, box, tile, rows, :] + total)

        around(value[1 - colour], colour, blocks, code, use)

    def sweep(step, carry):
        for colour in range(2):

            def take(block, box, tile, rows, fresh, out=value[colour]):
                out[box, tile, block_rows(block), :] = fresh
                if block == 0:
                    out[box, tile, FIRST + PAIRS : FIRST + PAIRS + 1, :] = fresh[0:1]
                if block == 2:
                    out[box, tile, FIRST - 1 : FIRST, :] = fresh[7:8]

            update(colour, 3, take)
        return carry

    lax.fori_loop(0, 2, sweep, 0)

    halves = TILES // 2
    for colour, out, left in ((0, red_out, red_left), (1, black_out, black_left)):

        def take(block, box, tile, rows, fresh, colour=colour, out=out, left=left):
            kept = value[colour][box, tile, block_rows(block), :]
            rest = diagonal[colour, box, tile, rows, :] * (fresh - kept)
            out[box, tile, rows, :] = kept
            left[box, tile, rows, :] = rest
            if colour == 1:
                at = 32 * (tile // halves) + 16 * box + 8 * block
                lanes = slice(tile % halves * LANES, (tile % halves + 1) * LANES)
                sums[at : at + 8, lanes] = red_left[box, tile, rows, :] + rest

        update(colour, 2, take)
    whole = sums[...]
    first = whole.astype(jnp.bfloat16)
    rest = whole - first.astype(jnp.float32)
    second = rest.astype(jnp.bfloat16)
    third = (rest - second.astype(jnp.float32)).astype(jnp.bfloat16)
    width = halves * LANES
    cell = lax.broadcasted_iota(jnp.int32, (width, LANES), 0)
    block = lax.broadcasted_iota(jnp.int32, (width, LANES), 1)
    merge = jnp.where((cell >> 6) * 16 + ((cell & 31) >> 1) == block, 1.0, 0.0).astype(jnp.bfloat16)
    split = jnp.dot(
        jnp.concatenate([first, second, third], axis=0), merge, preferred_element_type=jnp.float32
    )
    mean = (split[:64] + split[64:128] + split[128:]) * 0.125
    for half in range(2):
        coarse[0:32, half * LANES : (half + 1) * LANES] = mean[32 * half : 32 * half + 32]
    for box in range(2):
        label = parents[0, box, 0] * 16 + parents[0, box, 1] * 8 + parents[0, box, 2]
        coarse[32 + 4 * box : 36 + 4 * box, :] = jnp.full((4, 2 * LANES), label.astype(jnp.float32))


def unpack_kernel(red, black, red_left, black_left, smoothed, residual, stage):
    boxes, tiles = red.shape[:2]
    odd = odd_lanes(red.shape[2])
    for k, one, two, out in ((0, red, black, smoothed), (1, red_left, black_left, residual)):
        for box in range(boxes):
            for tile in range(tiles):
                low, high = one[box, tile], two[box, tile]
                stage[k, box, tile, pl.ds(0, 16, 2), :] = jnp.where(odd == 1, high, low)
                stage[k, box, tile, pl.ds(1, 16, 2), :] = jnp.where(odd == 1, low, high)
                out[0, box, :, tile * LANES : (tile + 1) * LANES] = stage[k, box, tile]


def place_kernel(*refs):
    *got, source, out = refs
    group = lax.axis_index("grp")
    base = (group * 16).astype(jnp.float32)
    marks = [
        [jnp.broadcast_to(one[32 + 4 * box : 33 + 4 * box, :], (16, one.shape[1])) for box in range(2)] for one in got
    ]
    for octant in range(16):
        kept = source[0, octant // 8, octant % 8]
        for sender, labels in zip(got, marks, strict=True):
            for box in range(2):
                mine = labels[box] == base + float(octant)
                kept = jnp.where(mine, sender[16 * box : 16 * box + 16, :], kept)
        out[0, octant // 8, octant % 8] = kept


def per_device(old_fields, old_count, neighbours, parents, coarse_source):
    f32 = jnp.float32
    curve = lax.axis_size("box")
    box_edge, plane_cells = old_fields.shape[3:]
    boxes = neighbours.shape[1]
    params = pltpu.CompilerParams(vmem_limit_bytes=40 << 20)

    def cost(flops, size):
        return pl.CostEstimate(flops=flops, bytes_accessed=size, transcendentals=0)

    def rows(count):
        return jax.ShapeDtypeStruct((count, LANES), f32)

    def swap(message, distance, shift):
        ids = [i for i in range(curve - distance) if (i - shift) % (2 * distance) < distance]
        both = [(i, i + distance) for i in ids] + [(i + distance, i) for i in ids]
        return lax.ppermute(message, "box", both)

    near_a, near_b = pl.pallas_call(
        pack_kernel,
        out_shape=(rows(NEAR_ROWS),) * 2,
        in_specs=[HBM] * 3,
        out_specs=(VMEM,) * 2,
        scratch_shapes=[
            pltpu.SMEM(old_count.shape, old_count.dtype),
            pltpu.SMEM(neighbours.shape, neighbours.dtype),
            pltpu.VMEM(old_fields.shape, f32),
            pltpu.SemaphoreType.DMA((2 + 3 * old_fields.shape[2],)),
        ],
        compiler_params=params,
        cost_estimate=cost(10**6, 2 << 20),
        name="pack",
    )(*[pltpu.with_memory_space_constraint(x, pltpu.HBM) for x in (old_count, neighbours, old_fields)])
    far_a, far_b = pl.pallas_call(
        pack_far_kernel,
        out_shape=(rows(FAR_ROWS),) * 2,
        in_specs=[SMEM, VMEM, pl.BlockSpec(memory_space=pl.ANY)],
        out_specs=(VMEM,) * 2,
        compiler_params=params,
        cost_estimate=cost(10**6, 2 << 20),
        name="pack_far",
    )(old_count, old_fields, near_b)
    moved = [swap(near_a, 1, 0), swap(near_b, 1, 1), swap(far_a, 2, 0), swap(far_b, 2, 2)]
    packed = pltpu.VMEM((2, boxes, TILES, PAIRS, LANES), f32)
    column = pltpu.VMEM((boxes, TILES, PAIRS + 2 * FIRST, LANES), f32)
    raw = pltpu.VMEM((boxes, TILES, ROWS, LANES), f32)
    weight = pltpu.VMEM((2, 6, boxes, TILES, PAIRS, LANES), f32)
    code = pltpu.VMEM((boxes, 4, 8, LANES), f32)
    sums = pltpu.VMEM((32 * boxes, TILES // 2 * LANES), f32)
    fine = jax.ShapeDtypeStruct((1, boxes, box_edge, plane_cells), f32)
    half = jax.ShapeDtypeStruct((boxes, TILES, box_edge // 2, LANES), f32)
    *halves, coarse = pl.pallas_call(
        smooth_kernel,
        out_shape=(half, half, half, half, jax.ShapeDtypeStruct((40, 2 * LANES), f32)),
        in_specs=[SMEM, SMEM, SMEM] + [VMEM] * 5,
        out_specs=(VMEM,) * 5,
        scratch_shapes=[raw] * 3 + [column] * 4 + [weight, packed, packed, code, sums],
        compiler_params=params,
        cost_estimate=cost(10**7, 6 << 20),
        name="smooth",
    )(old_count, neighbours, parents, old_fields, *moved)
    groups = lax.axis_size("grp")
    got = [coarse] + [
        lax.ppermute(coarse, "grp", [(i, (i + k) % groups) for i in range(groups)])
        for k in range(1, groups)
    ]
    smoothed, residual = pl.pallas_call(
        unpack_kernel,
        out_shape=(fine, fine),
        in_specs=[VMEM] * 4,
        out_specs=(VMEM,) * 2,
        scratch_shapes=[pltpu.VMEM((2, boxes, TILES, OWN, LANES), f32)],
        compiler_params=params,
        cost_estimate=pl.CostEstimate(flops=10**6, bytes_accessed=3 << 20, transcendentals=0),
        name="unpack",
    )(*halves)
    coarse_rhs = pl.pallas_call(
        place_kernel,
        out_shape=jax.ShapeDtypeStruct(coarse_source.shape, f32),
        in_specs=[VMEM] * (len(got) + 1),
        out_specs=VMEM,
        compiler_params=params,
        cost_estimate=pl.CostEstimate(flops=10**6, bytes_accessed=1 << 20, transcendentals=0),
        name="place",
    )(*got, coarse_source)
    return smoothed, residual, coarse_rhs


def solution(mesh):
    in_specs = (
        P(None, "grp", "box", None, None),
        P("grp", None),
        P("grp", "box", None),
        P("grp", "box", None),
        P("grp", "box", None, None, None),
    )
    out_specs = (
        P("grp", "box", None, None),
        P("grp", "box", None, None),
        P("grp", "box", None, None, None),
    )
    return jax.shard_map(
        per_device, mesh=mesh, in_specs=in_specs, out_specs=out_specs, check_vma=False
    )
```

```python
import jax
import jax.numpy as jnp
from jax import lax
from jax.experimental import pallas as pl
from jax.experimental.pallas import tpu as pltpu
from jax.sharding import PartitionSpec as P

MASS_TERM = 0.25
LANES = 128
OWN, ROWS, PAIRS, FIRST = 32, 48, 24, 8
LOAD_AHEAD, TURN_AHEAD = 20, 4
TILES = 8
SIDE_END, VALUE_END = 8, 2
SIDE = OWN * TILES
SIDE_ENDS = SIDE + OWN * TILES
LINKS = SIDE_ENDS + 2 * SIDE_END * TILES
VALUE = LINKS + 8
VALUE_ENDS = VALUE + OWN // 2 * TILES
NEAR_ROWS = VALUE_ENDS + 2 * VALUE_END * TILES
FAR_VALUES = SIDE_END * TILES
FAR_ROWS = FAR_VALUES + VALUE_END * TILES

VMEM = pl.BlockSpec(memory_space=pltpu.VMEM)
SMEM = pl.BlockSpec(memory_space=pltpu.SMEM)
HBM = pl.BlockSpec(memory_space=pltpu.HBM)


def lane_ids(rows):
    return lax.broadcasted_iota(jnp.int32, (rows, LANES), 1)


def row_ids(rows):
    return lax.broadcasted_iota(jnp.int32, (rows, LANES), 0)


def odd_lanes(rows):
    lane = lane_ids(rows)
    return ((lane >> 5) + lane) & 1


def offsets(counts, position):
    count = counts.shape[1]
    start = jnp.int32(0)
    for j in range(count):
        start = start + jnp.where(j < position, counts[0, j], 0)
    here = start - 2 * position
    after = here + counts[0, position] - 2
    before = here - counts[0, jnp.maximum(position - 1, 0)] + 2
    beyond = after + counts[0, jnp.minimum(position + 1, count - 1)] - 2
    return before, here, after, beyond


def link_code(links, box, face, first_box):
    target = links[0, box, face]
    return jnp.where(target < 0, 0, jnp.where(target - first_box == box, 1, 2))


def swap_depth(cells):
    odd = lane_ids(cells.shape[0]) & 1
    return jnp.where(odd == 1, pltpu.roll(cells, 1, 1), pltpu.roll(cells, LANES - 1, 1))


def end_tiles(fields, row, tile, upper):
    lanes = slice(tile * LANES, (tile + 1) * LANES)
    rows = slice(OWN - 8, OWN) if upper else slice(0, 8)
    return [fields[field, 0, row, rows, lanes] for field in range(3)]


def side_end(fields, row, tile, upper):
    sol, rhs, coef = end_tiles(fields, row, tile, upper)
    towards = 1 if upper else 7
    next_coef = pltpu.roll(coef, towards, 0)
    folded = rhs + 0.5 * (coef + next_coef) * pltpu.roll(sol, towards, 0)
    mixed = jnp.where(odd_lanes(8) == int(not upper), folded, swap_depth(next_coef))
    side = jnp.where(row_ids(8) == (4 if upper else 3), mixed, rhs)
    rows = slice(4, 8) if upper else slice(0, 4)
    return coef[rows], side[rows]


def value_end(fields, row, tile, upper):
    sol, _, _ = end_tiles(fields, row, tile, upper)
    packed = jnp.where(odd_lanes(8) == 1, sol, pltpu.roll(sol, 7, 0))
    return (packed[4:5], packed[6:7]) if upper else (packed[0:1], packed[2:3])


def store_rows(out, base, pieces):
    for piece in pieces:
        out[base : base + piece.shape[0], :] = piece
        base += piece.shape[0]


def load_rows(ref, base, sizes):
    pieces = []
    for size in sizes:
        pieces.append(ref[base : base + size, :])
        base += size
    return tuple(pieces)


SIDE_SIZES, VALUE_SIZES = (4, 4), (1, 1)


def slots(here):
    return (jnp.maximum(-here, 0), 1 - here), jnp.minimum(2 - here, 3)


def pack_kernel(counts_hbm, links_hbm, fields_hbm, near_a, near_b, counts, links, fields, sems):
    copies = []

    def fetch(source, target):
        copies.append(pltpu.make_async_copy(source, target, sems.at[len(copies)]))

    fetch(counts_hbm, counts)
    fetch(links_hbm, links)
    for row in range(fields.shape[2]):
        for field in range(3):
            fetch(fields_hbm.at[field, 0, row], fields.at[field, 0, row])
    for copy in copies:
        copy.start()
    for copy in copies[:2]:
        copy.wait()
    position = lax.axis_index("box")
    here = offsets(counts, position)[1]
    held, move_up = slots(here)
    codes = jnp.zeros((8, LANES), jnp.float32)
    for box in range(2):
        for face in range(2, 6):
            mine = (row_ids(8) == box) & (lane_ids(8) == face - 2)
            codes = jnp.where(mine, link_code(links, box, face, 2 * position).astype(jnp.float32), codes)

    mixed = (row_ids(16) + odd_lanes(16)) & 1

    for copy in copies[2:]:
        copy.wait()

    def message(out, upper):
        row = move_up if upper else 0
        for tile in range(TILES):
            lanes = slice(tile * LANES, (tile + 1) * LANES)
            low = fields[0, 0, row, 0:16, lanes]
            high = pltpu.roll(fields[0, 0, row, 16:32, lanes], 15, 0)
            out[VALUE + 16 * tile : VALUE + 16 * tile + 16, :] = jnp.where(mixed == 1, low, high)
            out[OWN * tile : OWN * (tile + 1), :] = fields[2, 0, row, :, lanes]
            out[SIDE + OWN * tile : SIDE + OWN * (tile + 1), :] = fields[1, 0, row, :, lanes]
            for box in range(2):
                store_rows(
                    out, SIDE_ENDS + SIDE_END * (2 * tile + box), side_end(fields, held[box], tile, upper)
                )
                store_rows(
                    out, VALUE_ENDS + VALUE_END * (2 * tile + box), value_end(fields, held[box], tile, upper)
                )
        out[LINKS : LINKS + 8, :] = codes

    even = position % 2 == 0

    @pl.when(even)
    def _():
        message(near_a, True)
        message(near_b, False)

    @pl.when(jnp.logical_not(even))
    def _():
        message(near_a, False)
        message(near_b, True)


def pack_far_kernel(counts, fields, _, far_a, far_b):
    position = lax.axis_index("box")
    move_up = slots(offsets(counts, position)[1])[1]

    def far_message(out, upper):
        row = move_up if upper else 0
        for tile in range(TILES):
            store_rows(out, SIDE_END * tile, side_end(fields, row, tile, upper))
            store_rows(out, FAR_VALUES + VALUE_END * tile, value_end(fields, row, tile, upper))

    lower = position % 4 < 2

    @pl.when(lower)
    def _():
        far_message(far_a, True)
        far_message(far_b, False)

    @pl.when(jnp.logical_not(lower))
    def _():
        far_message(far_a, False)
        far_message(far_b, True)


def choose(flag, one, other):
    return tuple(jnp.where(flag, a, b) for a, b in zip(one, other, strict=True))


def crossing(links, face, run_first):
    ids = [links[0, box, face] for box in range(2)]
    linked = [one >= 0 for one in ids]
    swap = jnp.where(linked[0], ids[0] - run_first == 1, linked[1] & (ids[1] - run_first == 0))
    return linked, swap


def neighbour_ends(offset, even, lower, swaps, fields, near, far, tile, start, far_start, sizes, local):
    before, here, after, beyond = offset
    near_a, near_b = near
    far_a, far_b = far
    at = [start + sum(sizes) * (2 * tile + i) for i in range(2)]
    far_at = far_start + sum(sizes) * tile
    below = [choose(even, load_rows(near_b, at[i], sizes), load_rows(near_a, at[i], sizes)) for i in range(2)]
    above = [choose(even, load_rows(near_a, at[i], sizes), load_rows(near_b, at[i], sizes)) for i in range(2)]
    far_below = choose(lower, load_rows(far_b, far_at, sizes), load_rows(far_a, far_at, sizes))
    far_above = choose(lower, load_rows(far_a, far_at, sizes), load_rows(far_b, far_at, sizes))
    below = (choose(before == 1, far_below, below[0]), choose(here == -1, local(fields, 0, tile, True), below[1]))
    above = (
        choose(after == 1, local(fields, jnp.minimum(2 - here, 3), tile, False), above[0]),
        choose(beyond == -1, far_above, above[1]),
    )
    return [
        (choose(swaps[0], below[1 - box], below[box]), choose(swaps[1], above[1 - box], above[box]))
        for box in range(2)
    ]


def place_own(here, after, even, place_local, place_moved, near):
    from_below = here == 1
    from_above = after == -1
    held = slots(here)[0]
    for box, moved, first, second in ((0, from_below, near[1], near[0]), (1, from_above, near[0], near[1])):

        @pl.when(jnp.logical_not(moved))
        def _(box=box):
            place_local(box, held[box])

        @pl.when(moved & even)
        def _(box=box, ref=first):
            place_moved(box, ref)

        @pl.when(moved & jnp.logical_not(even))
        def _(box=box, ref=second):
            place_moved(box, ref)


def split_colours(raw, box, tile):
    odd = odd_lanes(PAIRS)
    low = raw[box, tile, pl.ds(0, PAIRS, 2), :]
    high = raw[box, tile, pl.ds(1, PAIRS, 2), :]
    return jnp.where(odd == 1, high, low), jnp.where(odd == 1, low, high)


def store_column(out, box, tile, cells):
    out[box, tile, FIRST : FIRST + PAIRS, :] = cells
    out[box, tile, FIRST - 1 : FIRST, :] = cells[PAIRS - 1 : PAIRS]
    out[box, tile, FIRST + PAIRS : FIRST + PAIRS + 1, :] = cells[0:1]


def block_rows(block, by=0):
    return slice(FIRST + 8 * block + by, FIRST + 8 * block + 8 + by)


def around(ref, colour, blocks, code, use):
    lane = lane_ids(8)
    depth = lane & 31
    low_layer = odd_lanes(8) == colour
    cells, up, down, turned = {}, {}, {}, {}

    def load(block, tile):
        for box in range(2):
            at = block, box, tile
            cells[at] = ref[box, tile, block_rows(block), :]
            up[at] = pltpu.roll(cells[at], 32, 1)
            down[at] = pltpu.roll(cells[at], 96, 1)

    def turn(block, tile):
        for box in range(2):
            at, there = (block, box, tile), (block, 1 - box, tile)
            z_low = jnp.where(code(block, box, 2) == 2, down[there], down[at])
            z_high = jnp.where(code(block, box, 3) == 2, up[there], up[at])
            turned[at] = (
                pltpu.roll(jnp.where(depth == 31, z_low, cells[at]), 1, 1),
                pltpu.roll(jnp.where(depth == 0, z_high, cells[at]), LANES - 1, 1),
            )

    def finish(block, tile):
        for box in range(2):
            at = block, box, tile
            y_low, y_high = up[block, box, (tile - 1) % TILES], down[block, box, (tile + 1) % TILES]
            if tile == 0:
                y_low = jnp.where(code(block, box, 0) == 2, up[block, 1 - box, TILES - 1], y_low)
            if tile == TILES - 1:
                y_high = jnp.where(code(block, box, 1) == 2, down[block, 1 - box, 0], y_high)
            across = jnp.where(
                low_layer, ref[box, tile, block_rows(block, -1), :], ref[box, tile, block_rows(block, 1), :]
            )
            use(
                block,
                box,
                tile,
                (
                    across,
                    cells[at],
                    jnp.where(lane >= 32, up[at], y_low),
                    jnp.where(lane < 96, down[at], y_high),
                    *turned[at],
                ),
            )

    loads = [(block, (tile - 1) % TILES) for block in range(blocks) for tile in range(TILES)]
    steps = [(block, tile) for block in range(blocks) for tile in range(TILES)]
    for k in range(len(steps) + LOAD_AHEAD):
        if k < len(loads):
            load(*loads[k])
        if 0 <= k - LOAD_AHEAD + TURN_AHEAD < len(steps):
            turn(*steps[k - LOAD_AHEAD + TURN_AHEAD])
        if k >= LOAD_AHEAD:
            finish(*steps[k - LOAD_AHEAD])


def smooth_kernel(
    counts,
    links,
    parents,
    fields,
    near_a,
    near_b,
    far_a,
    far_b,
    red_out,
    black_out,
    red_left,
    black_left,
    coarse,
    raw_coef,
    raw_side,
    raw_value,
    red_coef,
    black_coef,
    red,
    black,
    weight,
    source,
    diagonal,
    halo_code,
    sums,
):
    value, coef = (red, black), (red_coef, black_coef)
    position = lax.axis_index("box")
    offset = offsets(counts, position)
    _, here, after, _ = offset
    first_box = 2 * position
    even = position % 2 == 0
    lower = position % 4 < 2
    near, far = (near_a, near_b), (far_a, far_b)

    def place_local(box, row):
        for tile in range(TILES):
            lanes = slice(tile * LANES, (tile + 1) * LANES)
            raw_value[box, tile, 0:OWN, :] = fields[0, 0, row, :, lanes]
            raw_side[box, tile, 0:OWN, :] = fields[1, 0, row, :, lanes]
            raw_coef[box, tile, 0:OWN, :] = fields[2, 0, row, :, lanes]

    def place_moved(box, ref):
        for tile in range(TILES):
            packed = ref[VALUE + 16 * tile : VALUE + 16 * tile + 16, :]
            raw_value[box, tile, 0:16, :] = packed
            raw_value[box, tile, 16:32, :] = pltpu.roll(packed, 1, 0)
            raw_side[box, tile, 0:OWN, :] = ref[SIDE + OWN * tile : SIDE + OWN * (tile + 1), :]
            raw_coef[box, tile, 0:OWN, :] = ref[OWN * tile : OWN * (tile + 1), :]

    place_own(here, after, even, place_local, place_moved, near)
    low_linked, low_swap = crossing(links, 0, first_box - 2)
    high_linked, high_swap = crossing(links, 1, first_box + 2)
    swaps = (low_swap, high_swap)
    ones = jnp.ones((16, LANES), jnp.float32)
    zeros = jnp.zeros((16, LANES), jnp.float32)
    odd = odd_lanes(1)
    for tile in range(TILES):
        sides = neighbour_ends(
            offset, even, lower, swaps, fields, near, far, tile, SIDE_ENDS, 0, SIDE_SIZES, side_end
        )
        values = neighbour_ends(
            offset, even, lower, swaps, fields, near, far, tile, VALUE_ENDS, FAR_VALUES, VALUE_SIZES, value_end
        )
        for box in range(2):
            (below, side_below), (above, side_above) = sides[box]
            raw_coef[box, tile, 32:48, :] = ones
            raw_side[box, tile, 32:48, :] = ones
            raw_value[box, tile, 32:48, :] = zeros
            raw_coef[box, tile, 43:44, :] = jnp.where(odd == 0, swap_depth(side_below[0:1]), below[0:1])
            raw_coef[box, tile, 44:48, :] = below
            raw_side[box, tile, 44:48, :] = side_below
            raw_coef[box, tile, 32:36, :] = above
            raw_coef[box, tile, 36:37, :] = jnp.where(odd == 1, swap_depth(side_above[3:4]), above[3:4])
            raw_side[box, tile, 32:36, :] = side_above
            for base, pieces in zip((44, 32), values[box], strict=True):
                for k in range(4):
                    raw_value[box, tile, base + k : base + k + 1, :] = pieces[k // 2]

    own_code = [[link_code(links, box, face, first_box) for face in range(2, 6)] for box in range(2)]
    tile_a, tile_b = near_a[LINKS : LINKS + 8, :], near_b[LINKS : LINKS + 8, :]
    codes_below, codes_above = jnp.where(even, tile_b, tile_a), jnp.where(even, tile_a, tile_b)
    for face in range(4):
        spread = [
            [jnp.broadcast_to(one[i : i + 1, face : face + 1], (8, LANES)) for i in range(2)]
            for one in (codes_below, codes_above)
        ]
        for box in range(2):
            below = jnp.where(low_swap, spread[0][1 - box], spread[0][box])
            above = jnp.where(high_swap, spread[1][1 - box], spread[1][box])
            halo_code[box, face] = jnp.where(row_ids(8) < 4, above, below)

    def code(block, box, face):
        return own_code[box][face] if block < 2 else halo_code[box, face]

    for box in range(2):
        for tile in range(TILES):
            for raw, out in ((raw_value, value), (raw_coef, coef)):
                for colour, cells in enumerate(split_colours(raw, box, tile)):
                    store_column(out[colour], box, tile, cells)
            source[0, box, tile], source[1, box, tile] = split_colours(raw_side, box, tile)

    lane = lane_ids(8)
    depth = lane & 31
    row = row_ids(8)

    def weigh(colour):
        low_layer = odd_lanes(8) == colour

        def use(block, box, tile, near_coef):
            rows = slice(8 * block, 8 * block + 8)
            cut_low = jnp.logical_not(low_linked[box])
            cut_high = jnp.logical_not(high_linked[box])
            first_row, last_row = (row == 0) & low_layer, (row == 7) & jnp.logical_not(low_layer)
            end = (
                first_row & cut_low,
                last_row & cut_high,
                (first_row & cut_high) | (last_row & cut_low),
            )[block]
            lost = (
                end,
                None,
                (lane < 32) & (code(block, box, 0) == 0) if tile == 0 else None,
                (lane >= 96) & (code(block, box, 1) == 0) if tile == TILES - 1 else None,
                (depth == 0) & (code(block, box, 2) == 0),
                (depth == 31) & (code(block, box, 3) == 0),
            )
            own = coef[colour][box, tile, block_rows(block), :]
            total = jnp.full((8, LANES), MASS_TERM, jnp.float32)
            kept = []
            for one, gone in zip(near_coef, lost, strict=True):
                if gone is None:
                    w = 0.5 * (own + one)
                    kept.append(w)
                else:
                    w = 0.5 * (own + jnp.where(gone, own, one))
                    kept.append(jnp.where(gone, 0.0, w))
                total = total + w
            inverse = 1.0 / total
            diagonal[colour, box, tile, rows, :] = total
            source[colour, box, tile, rows, :] = source[colour, box, tile, rows, :] * inverse
            for d in range(6):
                weight[colour, d, box, tile, rows, :] = kept[d] * inverse

        around(coef[1 - colour], colour, 3, code, use)

    weigh(0)
    weigh(1)

    def update(colour, blocks, take):
        def use(block, box, tile, near_value):
            rows = slice(8 * block, 8 * block + 8)
            terms = [weight[colour, d, box, tile, rows, :] * one for d, one in enumerate(near_value)]
            total = (terms[0] + terms[1]) + (terms[2] + terms[3]) + (terms[4] + terms[5])
            take(block, box, tile, rows, source[colour, box, tile, rows, :] + total)

        around(value[1 - colour], colour, blocks, code, use)

    def sweep(step, carry):
        for colour in range(2):

            def take(block, box, tile, rows, fresh, out=value[colour]):
                out[box, tile, block_rows(block), :] = fresh
                if block == 0:
                    out[box, tile, FIRST + PAIRS : FIRST + PAIRS + 1, :] = fresh[0:1]
                if block == 2:
                    out[box, tile, FIRST - 1 : FIRST, :] = fresh[7:8]

            update(colour, 3, take)
        return carry

    lax.fori_loop(0, 2, sweep, 0)

    halves = TILES // 2
    for colour, out, left in ((0, red_out, red_left), (1, black_out, black_left)):

        def take(block, box, tile, rows, fresh, colour=colour, out=out, left=left):
            kept = value[colour][box, tile, block_rows(block), :]
            rest = diagonal[colour, box, tile, rows, :] * (fresh - kept)
            out[box, tile, rows, :] = kept
            left[box, tile, rows, :] = rest
            if colour == 1:
                at = 32 * (tile // halves) + 16 * box + 8 * block
                lanes = slice(tile % halves * LANES, (tile % halves + 1) * LANES)
                sums[at : at + 8, lanes] = red_left[box, tile, rows, :] + rest

        update(colour, 2, take)
    whole = sums[...]
    first = whole.astype(jnp.bfloat16)
    rest = whole - first.astype(jnp.float32)
    second = rest.astype(jnp.bfloat16)
    third = (rest - second.astype(jnp.float32)).astype(jnp.bfloat16)
    width = halves * LANES
    cell = lax.broadcasted_iota(jnp.int32, (width, LANES), 0)
    block = lax.broadcasted_iota(jnp.int32, (width, LANES), 1)
    merge = jnp.where((cell >> 6) * 16 + ((cell & 31) >> 1) == block, 1.0, 0.0).astype(jnp.bfloat16)
    split = jnp.dot(
        jnp.concatenate([first, second, third], axis=0), merge, preferred_element_type=jnp.float32
    )
    mean = (split[:64] + split[64:128] + split[128:]) * 0.125
    for half in range(2):
        coarse[0:32, half * LANES : (half + 1) * LANES] = mean[32 * half : 32 * half + 32]
    for box in range(2):
        label = parents[0, box, 0] * 16 + parents[0, box, 1] * 8 + parents[0, box, 2]
        coarse[32 + 4 * box : 36 + 4 * box, :] = jnp.full((4, 2 * LANES), label.astype(jnp.float32))


def unpack_kernel(red, black, red_left, black_left, smoothed, residual, stage):
    boxes, tiles = red.shape[:2]
    odd = odd_lanes(red.shape[2])
    for k, one, two, out in ((0, red, black, smoothed), (1, red_left, black_left, residual)):
        for box in range(boxes):
            for tile in range(tiles):
                low, high = one[box, tile], two[box, tile]
                stage[k, box, tile, pl.ds(0, 16, 2), :] = jnp.where(odd == 1, high, low)
                stage[k, box, tile, pl.ds(1, 16, 2), :] = jnp.where(odd == 1, low, high)
                out[0, box, :, tile * LANES : (tile + 1) * LANES] = stage[k, box, tile]


def place_kernel(*refs):
    *got, source, out = refs
    group = lax.axis_index("grp")
    base = (group * 16).astype(jnp.float32)
    marks = [
        [jnp.broadcast_to(one[32 + 4 * box : 33 + 4 * box, :], (16, one.shape[1])) for box in range(2)] for one in got
    ]
    for octant in range(16):
        kept = source[0, octant // 8, octant % 8]
        for sender, labels in zip(got, marks, strict=True):
            for box in range(2):
                mine = labels[box] == base + float(octant)
                kept = jnp.where(mine, sender[16 * box : 16 * box + 16, :], kept)
        out[0, octant // 8, octant % 8] = kept


def per_device(old_fields, old_count, neighbours, parents, coarse_source):
    f32 = jnp.float32
    curve = lax.axis_size("box")
    box_edge, plane_cells = old_fields.shape[3:]
    boxes = neighbours.shape[1]
    params = pltpu.CompilerParams(vmem_limit_bytes=40 << 20)

    def cost(flops, size):
        return pl.CostEstimate(flops=flops, bytes_accessed=size, transcendentals=0)

    def rows(count):
        return jax.ShapeDtypeStruct((count, LANES), f32)

    def swap(message, distance, shift):
        ids = [i for i in range(curve - distance) if (i - shift) % (2 * distance) < distance]
        both = [(i, i + distance) for i in ids] + [(i + distance, i) for i in ids]
        return lax.ppermute(message, "box", both)

    near_a, near_b = pl.pallas_call(
        pack_kernel,
        out_shape=(rows(NEAR_ROWS),) * 2,
        in_specs=[HBM] * 3,
        out_specs=(VMEM,) * 2,
        scratch_shapes=[
            pltpu.SMEM(old_count.shape, old_count.dtype),
            pltpu.SMEM(neighbours.shape, neighbours.dtype),
            pltpu.VMEM(old_fields.shape, f32),
            pltpu.SemaphoreType.DMA((2 + 3 * old_fields.shape[2],)),
        ],
        compiler_params=params,
        cost_estimate=cost(10**6, 2 << 20),
        name="pack",
    )(*[pltpu.with_memory_space_constraint(x, pltpu.HBM) for x in (old_count, neighbours, old_fields)])
    far_a, far_b = pl.pallas_call(
        pack_far_kernel,
        out_shape=(rows(FAR_ROWS),) * 2,
        in_specs=[SMEM, VMEM, pl.BlockSpec(memory_space=pl.ANY)],
        out_specs=(VMEM,) * 2,
        compiler_params=params,
        cost_estimate=cost(10**6, 2 << 20),
        name="pack_far",
    )(old_count, old_fields, near_b)
    moved = [swap(near_a, 1, 0), swap(near_b, 1, 1), swap(far_a, 2, 0), swap(far_b, 2, 2)]
    packed = pltpu.VMEM((2, boxes, TILES, PAIRS, LANES), f32)
    column = pltpu.VMEM((boxes, TILES, PAIRS + 2 * FIRST, LANES), f32)
    raw = pltpu.VMEM((boxes, TILES, ROWS, LANES), f32)
    weight = pltpu.VMEM((2, 6, boxes, TILES, PAIRS, LANES), f32)
    code = pltpu.VMEM((boxes, 4, 8, LANES), f32)
    sums = pltpu.VMEM((32 * boxes, TILES // 2 * LANES), f32)
    fine = jax.ShapeDtypeStruct((1, boxes, box_edge, plane_cells), f32)
    half = jax.ShapeDtypeStruct((boxes, TILES, box_edge // 2, LANES), f32)
    *halves, coarse = pl.pallas_call(
        smooth_kernel,
        out_shape=(half, half, half, half, jax.ShapeDtypeStruct((40, 2 * LANES), f32)),
        in_specs=[SMEM, SMEM, SMEM] + [VMEM] * 5,
        out_specs=(VMEM,) * 5,
        scratch_shapes=[raw] * 3 + [column] * 4 + [weight, packed, packed, code, sums],
        compiler_params=params,
        cost_estimate=cost(10**7, 6 << 20),
        name="smooth",
    )(old_count, neighbours, parents, old_fields, *moved)
    groups = lax.axis_size("grp")
    got = [coarse] + [
        lax.ppermute(coarse, "grp", [(i, (i + k) % groups) for i in range(groups)])
        for k in range(1, groups)
    ]
    smoothed, residual = pl.pallas_call(
        unpack_kernel,
        out_shape=(fine, fine),
        in_specs=[VMEM] * 4,
        out_specs=(VMEM,) * 2,
        scratch_shapes=[pltpu.VMEM((2, boxes, TILES, OWN, LANES), f32)],
        compiler_params=params,
        cost_estimate=pl.CostEstimate(flops=10**6, bytes_accessed=3 << 20, transcendentals=0),
        name="unpack",
    )(*halves)
    coarse_rhs = pl.pallas_call(
        place_kernel,
        out_shape=jax.ShapeDtypeStruct(coarse_source.shape, f32),
        in_specs=[VMEM] * (len(got) + 1),
        out_specs=VMEM,
        compiler_params=params,
        cost_estimate=pl.CostEstimate(flops=10**6, bytes_accessed=1 << 20, transcendentals=0),
        name="place",
    )(*got, coarse_source)
    return smoothed, residual, coarse_rhs


def solution(mesh):
    in_specs = (
        P(None, "grp", "box", None, None),
        P("grp", None),
        P("grp", "box", None),
        P("grp", "box", None),
        P("grp", "box", None, None, None),
    )
    out_specs = (
        P("grp", "box", None, None),
        P("grp", "box", None, None),
        P("grp", "box", None, None, None),
    )
    return jax.shard_map(
        per_device, mesh=mesh, in_specs=in_specs, out_specs=out_specs, check_vma=False
    )
```

```python
import jax
import jax.numpy as jnp
from jax import lax
from jax.experimental import pallas as pl
from jax.experimental.pallas import tpu as pltpu
from jax.sharding import PartitionSpec as P

MASS_TERM = 0.25
LANES = 128
OWN, ROWS, PAIRS, FIRST = 32, 48, 24, 8
LOAD_AHEAD, TURN_AHEAD = 20, 4
TILES = 8
SIDE_END, VALUE_END = 8, 2
SIDE = OWN * TILES
SIDE_ENDS = SIDE + OWN * TILES
LINKS = SIDE_ENDS + 2 * SIDE_END * TILES
VALUE = LINKS + 8
VALUE_ENDS = VALUE + OWN // 2 * TILES
NEAR_ROWS = VALUE_ENDS + 2 * VALUE_END * TILES
FAR_VALUES = SIDE_END * TILES
FAR_ROWS = FAR_VALUES + VALUE_END * TILES

VMEM = pl.BlockSpec(memory_space=pltpu.VMEM)
SMEM = pl.BlockSpec(memory_space=pltpu.SMEM)
HBM = pl.BlockSpec(memory_space=pltpu.HBM)


def lane_ids(rows):
    return lax.broadcasted_iota(jnp.int32, (rows, LANES), 1)


def row_ids(rows):
    return lax.broadcasted_iota(jnp.int32, (rows, LANES), 0)


def odd_lanes(rows):
    lane = lane_ids(rows)
    return ((lane >> 5) + lane) & 1


def offsets(counts, position):
    count = counts.shape[1]
    start = jnp.int32(0)
    for j in range(count):
        start = start + jnp.where(j < position, counts[0, j], 0)
    here = start - 2 * position
    after = here + counts[0, position] - 2
    before = here - counts[0, jnp.maximum(position - 1, 0)] + 2
    beyond = after + counts[0, jnp.minimum(position + 1, count - 1)] - 2
    return before, here, after, beyond


def link_code(links, box, face, first_box):
    target = links[0, box, face]
    return jnp.where(target < 0, 0, jnp.where(target - first_box == box, 1, 2))


def swap_depth(cells):
    odd = lane_ids(cells.shape[0]) & 1
    return jnp.where(odd == 1, pltpu.roll(cells, 1, 1), pltpu.roll(cells, LANES - 1, 1))


def end_tiles(fields, row, tile, upper):
    lanes = slice(tile * LANES, (tile + 1) * LANES)
    rows = slice(OWN - 8, OWN) if upper else slice(0, 8)
    return [fields[field, 0, row, rows, lanes] for field in range(3)]


def side_end(fields, row, tile, upper):
    sol, rhs, coef = end_tiles(fields, row, tile, upper)
    towards = 1 if upper else 7
    next_coef = pltpu.roll(coef, towards, 0)
    folded = rhs + 0.5 * (coef + next_coef) * pltpu.roll(sol, towards, 0)
    mixed = jnp.where(odd_lanes(8) == int(not upper), folded, swap_depth(next_coef))
    side = jnp.where(row_ids(8) == (4 if upper else 3), mixed, rhs)
    rows = slice(4, 8) if upper else slice(0, 4)
    return coef[rows], side[rows]


def value_end(fields, row, tile, upper):
    sol, _, _ = end_tiles(fields, row, tile, upper)
    packed = jnp.where(odd_lanes(8) == 1, sol, pltpu.roll(sol, 7, 0))
    return (packed[4:5], packed[6:7]) if upper else (packed[0:1], packed[2:3])


def store_rows(out, base, pieces):
    for piece in pieces:
        out[base : base + piece.shape[0], :] = piece
        base += piece.shape[0]


def load_rows(ref, base, sizes):
    pieces = []
    for size in sizes:
        pieces.append(ref[base : base + size, :])
        base += size
    return tuple(pieces)


SIDE_SIZES, VALUE_SIZES = (4, 4), (1, 1)


def slots(here):
    return (jnp.maximum(-here, 0), 1 - here), jnp.minimum(2 - here, 3)


def pack_kernel(counts_hbm, links_hbm, fields_hbm, near_a, near_b, counts, links, fields, sems):
    copies = []

    def fetch(source, target):
        copies.append(pltpu.make_async_copy(source, target, sems.at[len(copies)]))

    fetch(counts_hbm, counts)
    fetch(links_hbm, links)
    for row in range(fields.shape[2]):
        for field in range(3):
            fetch(fields_hbm.at[field, 0, row], fields.at[field, 0, row])
    for copy in copies:
        copy.start()
    for copy in copies[:2]:
        copy.wait()
    position = lax.axis_index("box")
    here = offsets(counts, position)[1]
    held, move_up = slots(here)
    codes = jnp.zeros((8, LANES), jnp.float32)
    for box in range(2):
        for face in range(2, 6):
            mine = (row_ids(8) == box) & (lane_ids(8) == face - 2)
            codes = jnp.where(mine, link_code(links, box, face, 2 * position).astype(jnp.float32), codes)

    mixed = (row_ids(16) + odd_lanes(16)) & 1

    for copy in copies[2:]:
        copy.wait()

    def message(out, upper):
        row = move_up if upper else 0
        for tile in range(TILES):
            lanes = slice(tile * LANES, (tile + 1) * LANES)
            low = fields[0, 0, row, 0:16, lanes]
            high = pltpu.roll(fields[0, 0, row, 16:32, lanes], 15, 0)
            out[VALUE + 16 * tile : VALUE + 16 * tile + 16, :] = jnp.where(mixed == 1, low, high)
            out[OWN * tile : OWN * (tile + 1), :] = fields[2, 0, row, :, lanes]
            out[SIDE + OWN * tile : SIDE + OWN * (tile + 1), :] = fields[1, 0, row, :, lanes]
            for box in range(2):
                store_rows(
                    out, SIDE_ENDS + SIDE_END * (2 * tile + box), side_end(fields, held[box], tile, upper)
                )
                store_rows(
                    out, VALUE_ENDS + VALUE_END * (2 * tile + box), value_end(fields, held[box], tile, upper)
                )
        out[LINKS : LINKS + 8, :] = codes

    even = position % 2 == 0

    @pl.when(even)
    def _():
        message(near_a, True)
        message(near_b, False)

    @pl.when(jnp.logical_not(even))
    def _():
        message(near_a, False)
        message(near_b, True)


def pack_far_kernel(counts, fields, _, far_a, far_b):
    position = lax.axis_index("box")
    move_up = slots(offsets(counts, position)[1])[1]

    def far_message(out, upper):
        row = move_up if upper else 0
        for tile in range(TILES):
            store_rows(out, SIDE_END * tile, side_end(fields, row, tile, upper))
            store_rows(out, FAR_VALUES + VALUE_END * tile, value_end(fields, row, tile, upper))

    lower = position % 4 < 2

    @pl.when(lower)
    def _():
        far_message(far_a, True)
        far_message(far_b, False)

    @pl.when(jnp.logical_not(lower))
    def _():
        far_message(far_a, False)
        far_message(far_b, True)


def choose(flag, one, other):
    return tuple(jnp.where(flag, a, b) for a, b in zip(one, other, strict=True))


def crossing(links, face, run_first):
    ids = [links[0, box, face] for box in range(2)]
    linked = [one >= 0 for one in ids]
    swap = jnp.where(linked[0], ids[0] - run_first == 1, linked[1] & (ids[1] - run_first == 0))
    return linked, swap


def neighbour_ends(offset, even, lower, swaps, fields, near, far, tile, start, far_start, sizes, local):
    before, here, after, beyond = offset
    near_a, near_b = near
    far_a, far_b = far
    at = [start + sum(sizes) * (2 * tile + i) for i in range(2)]
    far_at = far_start + sum(sizes) * tile
    below = [choose(even, load_rows(near_b, at[i], sizes), load_rows(near_a, at[i], sizes)) for i in range(2)]
    above = [choose(even, load_rows(near_a, at[i], sizes), load_rows(near_b, at[i], sizes)) for i in range(2)]
    far_below = choose(lower, load_rows(far_b, far_at, sizes), load_rows(far_a, far_at, sizes))
    far_above = choose(lower, load_rows(far_a, far_at, sizes), load_rows(far_b, far_at, sizes))
    below = (choose(before == 1, far_below, below[0]), choose(here == -1, local(fields, 0, tile, True), below[1]))
    above = (
        choose(after == 1, local(fields, jnp.minimum(2 - here, 3), tile, False), above[0]),
        choose(beyond == -1, far_above, above[1]),
    )
    return [
        (choose(swaps[0], below[1 - box], below[box]), choose(swaps[1], above[1 - box], above[box]))
        for box in range(2)
    ]


def place_own(here, after, even, place_local, place_moved, near):
    from_below = here == 1
    from_above = after == -1
    held = slots(here)[0]
    for box, moved, first, second in ((0, from_below, near[1], near[0]), (1, from_above, near[0], near[1])):

        @pl.when(jnp.logical_not(moved))
        def _(box=box):
            place_local(box, held[box])

        @pl.when(moved & even)
        def _(box=box, ref=first):
            place_moved(box, ref)

        @pl.when(moved & jnp.logical_not(even))
        def _(box=box, ref=second):
            place_moved(box, ref)


def split_colours(raw, box, tile):
    odd = odd_lanes(PAIRS)
    low = raw[box, tile, pl.ds(0, PAIRS, 2), :]
    high = raw[box, tile, pl.ds(1, PAIRS, 2), :]
    return jnp.where(odd == 1, high, low), jnp.where(odd == 1, low, high)


def store_column(out, box, tile, cells):
    out[box, tile, FIRST : FIRST + PAIRS, :] = cells
    out[box, tile, FIRST - 1 : FIRST, :] = cells[PAIRS - 1 : PAIRS]
    out[box, tile, FIRST + PAIRS : FIRST + PAIRS + 1, :] = cells[0:1]


def block_rows(block, by=0):
    return slice(FIRST + 8 * block + by, FIRST + 8 * block + 8 + by)


def around(ref, colour, blocks, code, use):
    lane = lane_ids(8)
    depth = lane & 31
    low_layer = odd_lanes(8) == colour
    cells, up, down, turned = {}, {}, {}, {}

    def load(block, tile):
        for box in range(2):
            at = block, box, tile
            cells[at] = ref[box, tile, block_rows(block), :]
            up[at] = pltpu.roll(cells[at], 32, 1)
            down[at] = pltpu.roll(cells[at], 96, 1)

    def turn(block, tile):
        for box in range(2):
            at, there = (block, box, tile), (block, 1 - box, tile)
            z_low = jnp.where(code(block, box, 2) == 2, down[there], down[at])
            z_high = jnp.where(code(block, box, 3) == 2, up[there], up[at])
            turned[at] = (
                pltpu.roll(jnp.where(depth == 31, z_low, cells[at]), 1, 1),
                pltpu.roll(jnp.where(depth == 0, z_high, cells[at]), LANES - 1, 1),
            )

    def finish(block, tile):
        for box in range(2):
            at = block, box, tile
            y_low, y_high = up[block, box, (tile - 1) % TILES], down[block, box, (tile + 1) % TILES]
            if tile == 0:
                y_low = jnp.where(code(block, box, 0) == 2, up[block, 1 - box, TILES - 1], y_low)
            if tile == TILES - 1:
                y_high = jnp.where(code(block, box, 1) == 2, down[block, 1 - box, 0], y_high)
            across = jnp.where(
                low_layer, ref[box, tile, block_rows(block, -1), :], ref[box, tile, block_rows(block, 1), :]
            )
            use(
                block,
                box,
                tile,
                (
                    across,
                    cells[at],
                    jnp.where(lane >= 32, up[at], y_low),
                    jnp.where(lane < 96, down[at], y_high),
                    *turned[at],
                ),
            )

    loads = [(block, (tile - 1) % TILES) for block in range(blocks) for tile in range(TILES)]
    steps = [(block, tile) for block in range(blocks) for tile in range(TILES)]
    for k in range(len(steps) + LOAD_AHEAD):
        if k < len(loads):
            load(*loads[k])
        if 0 <= k - LOAD_AHEAD + TURN_AHEAD < len(steps):
            turn(*steps[k - LOAD_AHEAD + TURN_AHEAD])
        if k >= LOAD_AHEAD:
            finish(*steps[k - LOAD_AHEAD])


def smooth_kernel(
    counts,
    links,
    parents,
    fields,
    near_a,
    near_b,
    far_a,
    far_b,
    red_out,
    black_out,
    red_left,
    black_left,
    coarse,
    raw_coef,
    raw_side,
    raw_value,
    red_coef,
    black_coef,
    red,
    black,
    weight,
    source,
    diagonal,
    halo_code,
    sums,
):
    value, coef = (red, black), (red_coef, black_coef)
    position = lax.axis_index("box")
    offset = offsets(counts, position)
    _, here, after, _ = offset
    first_box = 2 * position
    even = position % 2 == 0
    lower = position % 4 < 2
    near, far = (near_a, near_b), (far_a, far_b)

    def place_local(box, row):
        for tile in range(TILES):
            lanes = slice(tile * LANES, (tile + 1) * LANES)
            raw_value[box, tile, 0:OWN, :] = fields[0, 0, row, :, lanes]
            raw_side[box, tile, 0:OWN, :] = fields[1, 0, row, :, lanes]
            raw_coef[box, tile, 0:OWN, :] = fields[2, 0, row, :, lanes]

    def place_moved(box, ref):
        for tile in range(TILES):
            packed = ref[VALUE + 16 * tile : VALUE + 16 * tile + 16, :]
            raw_value[box, tile, 0:16, :] = packed
            raw_value[box, tile, 16:32, :] = pltpu.roll(packed, 1, 0)
            raw_side[box, tile, 0:OWN, :] = ref[SIDE + OWN * tile : SIDE + OWN * (tile + 1), :]
            raw_coef[box, tile, 0:OWN, :] = ref[OWN * tile : OWN * (tile + 1), :]

    place_own(here, after, even, place_local, place_moved, near)
    low_linked, low_swap = crossing(links, 0, first_box - 2)
    high_linked, high_swap = crossing(links, 1, first_box + 2)
    swaps = (low_swap, high_swap)
    ones = jnp.ones((16, LANES), jnp.float32)
    zeros = jnp.zeros((16, LANES), jnp.float32)
    odd = odd_lanes(1)
    for tile in range(TILES):
        sides = neighbour_ends(
            offset, even, lower, swaps, fields, near, far, tile, SIDE_ENDS, 0, SIDE_SIZES, side_end
        )
        values = neighbour_ends(
            offset, even, lower, swaps, fields, near, far, tile, VALUE_ENDS, FAR_VALUES, VALUE_SIZES, value_end
        )
        for box in range(2):
            (below, side_below), (above, side_above) = sides[box]
            raw_coef[box, tile, 32:48, :] = ones
            raw_side[box, tile, 32:48, :] = ones
            raw_value[box, tile, 32:48, :] = zeros
            raw_coef[box, tile, 43:44, :] = jnp.where(odd == 0, swap_depth(side_below[0:1]), below[0:1])
            raw_coef[box, tile, 44:48, :] = below
            raw_side[box, tile, 44:48, :] = side_below
            raw_coef[box, tile, 32:36, :] = above
            raw_coef[box, tile, 36:37, :] = jnp.where(odd == 1, swap_depth(side_above[3:4]), above[3:4])
            raw_side[box, tile, 32:36, :] = side_above
            for base, pieces in zip((44, 32), values[box], strict=True):
                for k in range(4):
                    raw_value[box, tile, base + k : base + k + 1, :] = pieces[k // 2]

    own_code = [[link_code(links, box, face, first_box) for face in range(2, 6)] for box in range(2)]
    tile_a, tile_b = near_a[LINKS : LINKS + 8, :], near_b[LINKS : LINKS + 8, :]
    codes_below, codes_above = jnp.where(even, tile_b, tile_a), jnp.where(even, tile_a, tile_b)
    for face in range(4):
        spread = [
            [jnp.broadcast_to(one[i : i + 1, face : face + 1], (8, LANES)) for i in range(2)]
            for one in (codes_below, codes_above)
        ]
        for box in range(2):
            below = jnp.where(low_swap, spread[0][1 - box], spread[0][box])
            above = jnp.where(high_swap, spread[1][1 - box], spread[1][box])
            halo_code[box, face] = jnp.where(row_ids(8) < 4, above, below)

    def code(block, box, face):
        return own_code[box][face] if block < 2 else halo_code[box, face]

    for box in range(2):
        for tile in range(TILES):
            for raw, out in ((raw_value, value), (raw_coef, coef)):
                for colour, cells in enumerate(split_colours(raw, box, tile)):
                    store_column(out[colour], box, tile, cells)
            source[0, box, tile], source[1, box, tile] = split_colours(raw_side, box, tile)

    lane = lane_ids(8)
    depth = lane & 31
    row = row_ids(8)

    def weigh(colour):
        low_layer = odd_lanes(8) == colour

        def use(block, box, tile, near_coef):
            rows = slice(8 * block, 8 * block + 8)
            cut_low = jnp.logical_not(low_linked[box])
            cut_high = jnp.logical_not(high_linked[box])
            first_row, last_row = (row == 0) & low_layer, (row == 7) & jnp.logical_not(low_layer)
            end = (
                first_row & cut_low,
                last_row & cut_high,
                (first_row & cut_high) | (last_row & cut_low),
            )[block]
            lost = (
                end,
                None,
                (lane < 32) & (code(block, box, 0) == 0) if tile == 0 else None,
                (lane >= 96) & (code(block, box, 1) == 0) if tile == TILES - 1 else None,
                (depth == 0) & (code(block, box, 2) == 0),
                (depth == 31) & (code(block, box, 3) == 0),
            )
            own = coef[colour][box, tile, block_rows(block), :]
            total = jnp.full((8, LANES), MASS_TERM, jnp.float32)
            kept = []
            for one, gone in zip(near_coef, lost, strict=True):
                if gone is None:
                    w = 0.5 * (own + one)
                    kept.append(w)
                else:
                    w = 0.5 * (own + jnp.where(gone, own, one))
                    kept.append(jnp.where(gone, 0.0, w))
                total = total + w
            inverse = 1.0 / total
            diagonal[colour, box, tile, rows, :] = total
            source[colour, box, tile, rows, :] = source[colour, box, tile, rows, :] * inverse
            for d in range(6):
                weight[colour, d, box, tile, rows, :] = kept[d] * inverse

        around(coef[1 - colour], colour, 3, code, use)

    weigh(0)
    weigh(1)

    def update(colour, blocks, take):
        def use(block, box, tile, near_value):
            rows = slice(8 * block, 8 * block + 8)
            terms = [weight[colour, d, box, tile, rows, :] * one for d, one in enumerate(near_value)]
            total = (terms[0] + terms[1]) + (terms[2] + terms[3]) + (terms[4] + terms[5])
            take(block, box, tile, rows, source[colour, box, tile, rows, :] + total)

        around(value[1 - colour], colour, blocks, code, use)

    def sweep(step, carry):
        for colour in range(2):

            def take(block, box, tile, rows, fresh, out=value[colour]):
                out[box, tile, block_rows(block), :] = fresh
                if block == 0:
                    out[box, tile, FIRST + PAIRS : FIRST + PAIRS + 1, :] = fresh[0:1]
                if block == 2:
                    out[box, tile, FIRST - 1 : FIRST, :] = fresh[7:8]

            update(colour, 3, take)
        return carry

    for step in range(2):
        sweep(step, 0)

    halves = TILES // 2
    for colour, out, left in ((0, red_out, red_left), (1, black_out, black_left)):

        def take(block, box, tile, rows, fresh, colour=colour, out=out, left=left):
            kept = value[colour][box, tile, block_rows(block), :]
            rest = diagonal[colour, box, tile, rows, :] * (fresh - kept)
            out[box, tile, rows, :] = kept
            left[box, tile, rows, :] = rest
            if colour == 1:
                at = 32 * (tile // halves) + 16 * box + 8 * block
                lanes = slice(tile % halves * LANES, (tile % halves + 1) * LANES)
                sums[at : at + 8, lanes] = red_left[box, tile, rows, :] + rest

        update(colour, 2, take)
    whole = sums[...]
    first = whole.astype(jnp.bfloat16)
    rest = whole - first.astype(jnp.float32)
    second = rest.astype(jnp.bfloat16)
    third = (rest - second.astype(jnp.float32)).astype(jnp.bfloat16)
    width = halves * LANES
    cell = lax.broadcasted_iota(jnp.int32, (width, LANES), 0)
    block = lax.broadcasted_iota(jnp.int32, (width, LANES), 1)
    merge = jnp.where((cell >> 6) * 16 + ((cell & 31) >> 1) == block, 1.0, 0.0).astype(jnp.bfloat16)
    split = jnp.dot(
        jnp.concatenate([first, second, third], axis=0), merge, preferred_element_type=jnp.float32
    )
    mean = (split[:64] + split[64:128] + split[128:]) * 0.125
    for half in range(2):
        coarse[0:32, half * LANES : (half + 1) * LANES] = mean[32 * half : 32 * half + 32]
    for box in range(2):
        label = parents[0, box, 0] * 16 + parents[0, box, 1] * 8 + parents[0, box, 2]
        coarse[32 + 4 * box : 36 + 4 * box, :] = jnp.full((4, 2 * LANES), label.astype(jnp.float32))


def unpack_kernel(red, black, red_left, black_left, smoothed, residual, stage):
    boxes, tiles = red.shape[:2]
    odd = odd_lanes(red.shape[2])
    for k, one, two, out in ((0, red, black, smoothed), (1, red_left, black_left, residual)):
        for box in range(boxes):
            for tile in range(tiles):
                low, high = one[box, tile], two[box, tile]
                stage[k, box, tile, pl.ds(0, 16, 2), :] = jnp.where(odd == 1, high, low)
                stage[k, box, tile, pl.ds(1, 16, 2), :] = jnp.where(odd == 1, low, high)
                out[0, box, :, tile * LANES : (tile + 1) * LANES] = stage[k, box, tile]


def place_kernel(*refs):
    *got, source, out = refs
    group = lax.axis_index("grp")
    base = (group * 16).astype(jnp.float32)
    marks = [
        [jnp.broadcast_to(one[32 + 4 * box : 33 + 4 * box, :], (16, one.shape[1])) for box in range(2)] for one in got
    ]
    for octant in range(16):
        kept = source[0, octant // 8, octant % 8]
        for sender, labels in zip(got, marks, strict=True):
            for box in range(2):
                mine = labels[box] == base + float(octant)
                kept = jnp.where(mine, sender[16 * box : 16 * box + 16, :], kept)
        out[0, octant // 8, octant % 8] = kept


def per_device(old_fields, old_count, neighbours, parents, coarse_source):
    f32 = jnp.float32
    curve = lax.axis_size("box")
    box_edge, plane_cells = old_fields.shape[3:]
    boxes = neighbours.shape[1]
    params = pltpu.CompilerParams(vmem_limit_bytes=40 << 20)

    def cost(flops, size):
        return pl.CostEstimate(flops=flops, bytes_accessed=size, transcendentals=0)

    def rows(count):
        return jax.ShapeDtypeStruct((count, LANES), f32)

    def swap(message, distance, shift):
        ids = [i for i in range(curve - distance) if (i - shift) % (2 * distance) < distance]
        both = [(i, i + distance) for i in ids] + [(i + distance, i) for i in ids]
        return lax.ppermute(message, "box", both)

    near_a, near_b = pl.pallas_call(
        pack_kernel,
        out_shape=(rows(NEAR_ROWS),) * 2,
        in_specs=[HBM] * 3,
        out_specs=(VMEM,) * 2,
        scratch_shapes=[
            pltpu.SMEM(old_count.shape, old_count.dtype),
            pltpu.SMEM(neighbours.shape, neighbours.dtype),
            pltpu.VMEM(old_fields.shape, f32),
            pltpu.SemaphoreType.DMA((2 + 3 * old_fields.shape[2],)),
        ],
        compiler_params=params,
        cost_estimate=cost(10**6, 2 << 20),
        name="pack",
    )(*[pltpu.with_memory_space_constraint(x, pltpu.HBM) for x in (old_count, neighbours, old_fields)])
    far_a, far_b = pl.pallas_call(
        pack_far_kernel,
        out_shape=(rows(FAR_ROWS),) * 2,
        in_specs=[SMEM, VMEM, pl.BlockSpec(memory_space=pl.ANY)],
        out_specs=(VMEM,) * 2,
        compiler_params=params,
        cost_estimate=cost(10**6, 2 << 20),
        name="pack_far",
    )(old_count, old_fields, near_b)
    moved = [swap(near_a, 1, 0), swap(near_b, 1, 1), swap(far_a, 2, 0), swap(far_b, 2, 2)]
    packed = pltpu.VMEM((2, boxes, TILES, PAIRS, LANES), f32)
    column = pltpu.VMEM((boxes, TILES, PAIRS + 2 * FIRST, LANES), f32)
    raw = pltpu.VMEM((boxes, TILES, ROWS, LANES), f32)
    weight = pltpu.VMEM((2, 6, boxes, TILES, PAIRS, LANES), f32)
    code = pltpu.VMEM((boxes, 4, 8, LANES), f32)
    sums = pltpu.VMEM((32 * boxes, TILES // 2 * LANES), f32)
    fine = jax.ShapeDtypeStruct((1, boxes, box_edge, plane_cells), f32)
    half = jax.ShapeDtypeStruct((boxes, TILES, box_edge // 2, LANES), f32)
    *halves, coarse = pl.pallas_call(
        smooth_kernel,
        out_shape=(half, half, half, half, jax.ShapeDtypeStruct((40, 2 * LANES), f32)),
        in_specs=[SMEM, SMEM, SMEM] + [VMEM] * 5,
        out_specs=(VMEM,) * 5,
        scratch_shapes=[raw] * 3 + [column] * 4 + [weight, packed, packed, code, sums],
        compiler_params=params,
        cost_estimate=cost(10**7, 6 << 20),
        name="smooth",
    )(old_count, neighbours, parents, old_fields, *moved)
    groups = lax.axis_size("grp")
    got = [coarse] + [
        lax.ppermute(coarse, "grp", [(i, (i + k) % groups) for i in range(groups)])
        for k in range(1, groups)
    ]
    smoothed, residual = pl.pallas_call(
        unpack_kernel,
        out_shape=(fine, fine),
        in_specs=[VMEM] * 4,
        out_specs=(VMEM,) * 2,
        scratch_shapes=[pltpu.VMEM((2, boxes, TILES, OWN, LANES), f32)],
        compiler_params=params,
        cost_estimate=pl.CostEstimate(flops=10**6, bytes_accessed=3 << 20, transcendentals=0),
        name="unpack",
    )(*halves)
    coarse_rhs = pl.pallas_call(
        place_kernel,
        out_shape=jax.ShapeDtypeStruct(coarse_source.shape, f32),
        in_specs=[VMEM] * (len(got) + 1),
        out_specs=VMEM,
        compiler_params=params,
        cost_estimate=pl.CostEstimate(flops=10**6, bytes_accessed=1 << 20, transcendentals=0),
        name="place",
    )(*got, coarse_source)
    return smoothed, residual, coarse_rhs


def solution(mesh):
    in_specs = (
        P(None, "grp", "box", None, None),
        P("grp", None),
        P("grp", "box", None),
        P("grp", "box", None),
        P("grp", "box", None, None, None),
    )
    out_specs = (
        P("grp", "box", None, None),
        P("grp", "box", None, None),
        P("grp", "box", None, None, None),
    )
    return jax.shard_map(
        per_device, mesh=mesh, in_specs=in_specs, out_specs=out_specs, check_vma=False
    )
```
